512 devices in a mesh: seq: 64 (over z, y_lo, core), chan: 8 (over x, y_hi).
Axes of the slice: x: 4, y: 8 (y_hi: 2, y_lo: 4; y = y_hi * 4 + y_lo), z: 8, core: 2. Of those that a mesh axis runs over, the one named last changes fastest.
Arguments:
- tokens: bfloat16 [16384, 512], P('seq', 'chan'), may hold values from -6 to 6
- out_grad: bfloat16 [16384, 512], P('seq', 'chan'), may hold values from -6 to 6
- in_weight: bfloat16 [512, 1024], P('seq', 'chan'), may hold values from -0.25 to 0.25
- dt_weight: bfloat16 [512, 16], P('seq', 'chan'), may hold values from -0.25 to 0.25
- bc_weight: bfloat16 [512, 128], P('seq'), may hold values from -0.0625 to 0.0625
- out_weight: bfloat16 [1024, 512], P('chan', 'seq'), may hold values from -0.1875 to 0.1875
- decay_rate: float32 [2, 16], P(None, 'chan'), may hold values from 0.00036621094 to 8
- dt_bias: float32 [2, 16], P(None, 'chan'), may hold values from -5 to -4
- skip_gain: float32 [16], P('chan'), may hold values from 0.5 to 1.5
Outputs:
- tokens_grad: bfloat16 [16384, 512], P('seq', 'chan')
- in_weight_grad: float32 [512, 1024], P('seq', 'chan')
- dt_weight_grad: float32 [512, 16], P('seq', 'chan')
- bc_weight_grad: float32 [512, 128], P('seq')
- out_weight_grad: float32 [1024, 512], P('chan', 'seq')
- rate_grad: float32 [2, 16], P(None, 'chan')
- bias_grad: float32 [2, 16], P(None, 'chan')
- skip_grad: float32 [16], P('chan')
The draws below stay inside these ranges and needn't reach their ends.
All inputs are finite; a program needn't handle non-finite values.
Results may differ from the reference program's by a relative error of at most 0.0034.
Values may be sent and summed in bfloat16 or wider, within the bound.
No kernel may reach another device: no remote copies, remote signals or barrier semaphores. Data moves between devices by JAX's collectives and lax.ppermute only.
A program may use at most 64 MiB of HBM per device.

```python
import math
import jax
import jax.numpy as jnp
from jax import lax

D = 512
E = 1024
STATE = 64
HEAD = 64
HEADS = 16
GROUP = 256
TOKENS = 16384


def draw_decay_rate(key, part):
    base_key = jax.random.fold_in(key, 11)
    mask_key, slow_key, fast_key = jax.random.split(base_key, 3)
    slow_share = 0.5
    slow_mask = jax.random.uniform(mask_key, (2, HEADS)) < slow_share
    slow_value = jnp.exp(jax.random.uniform(slow_key, (2, HEADS), minval=math.log(6.0), maxval=math.log(40.0))) / TOKENS
    fast_value = jnp.exp(jax.random.uniform(fast_key, (2, HEADS), minval=math.log(2.0), maxval=math.log(8.0)))
    return jnp.where(slow_mask, slow_value, fast_value).astype(jnp.float32)


def shard_levels(own_key, shape, cuts, smallest, high):
    def one(position, shards_of):
        draws = jax.random.uniform(jax.random.fold_in(jax.random.fold_in(own_key, 6), position), (shards_of,), jnp.float32, smallest / len(cuts), high / len(cuts))
        return jnp.repeat(jnp.exp(draws), shape[position] // shards_of).reshape((-1,) + (1,) * (len(shape) - position - 1))

    gain = one(*cuts[0])
    for cut in cuts[1:]:
        gain = gain * one(*cut)
    return gain


def scatter_about(rng, extent, scale, reach, cuts=(), held_as=jnp.bfloat16):
    values = jax.random.normal(rng, extent, jnp.float32) * scale
    if len(cuts) > 0:
        values = shard_levels(rng, extent, cuts, -0.22, 0.18) * values
    return jnp.clip(values, min=-reach, max=reach).astype(held_as)


def setup_inputs(seed: int = 0) -> dict:
    key_list = jax.random.split(jax.random.key(seed), 10)
    tokens = scatter_about(key_list[0], (TOKENS, D), 1.0, 6.0, ((0, 64), (1, 8)))
    out_grad = scatter_about(key_list[1], (TOKENS, D), 1.0, 6.0, ((0, 64), (1, 8)))
    in_weight = scatter_about(key_list[2], (D, E), D ** -0.5, 0.25, ((0, 64), (1, 8)))
    dt_weight = scatter_about(key_list[3], (D, HEADS), D ** -0.5, 0.25, ((0, 64), (1, 8)))
    bc_weight = scatter_about(key_list[4], (D, 2 * STATE), (D * 16) ** -0.5, 0.0625, ((0, 64),))
    out_weight = scatter_about(key_list[5], (E, D), E ** -0.5, 0.1875, ((0, 8), (1, 64)))
    decay_rate = draw_decay_rate(jax.random.fold_in(key_list[9], 71), 0)
    dt_bias = jnp.clip(-5.0 + 1.0 * jax.random.uniform(key_list[7], (2, HEADS), jnp.float32) ** shard_levels(key_list[7], (2, HEADS), ((1, 8),), -0.2, 0.2), -5.0, -4.0)
    skip_gain = jnp.clip(0.5 + 1.0 * jax.random.uniform(key_list[8], (HEADS,), jnp.float32) ** shard_levels(key_list[8], (HEADS,), ((0, 8),), -0.2, 0.2), 0.5, 1.5)
    return {"tokens": tokens, "out_grad": out_grad, "in_weight": in_weight, "dt_weight": dt_weight, "bc_weight": bc_weight, "out_weight": out_weight, "decay_rate": decay_rate, "dt_bias": dt_bias, "skip_gain": skip_gain}


def ssd_core(gated, step_size, b_proj, c_proj, rate, skip_gain, start_state):
    length, width = gated.shape
    heads = step_size.shape[1]
    head_dim = width // heads
    blocks = length // GROUP
    log_decay = -rate[None, :] * step_size
    driven = gated.reshape(length, heads, head_dim) * step_size[:, :, None]
    causal = lax.broadcasted_iota(jnp.int32, (GROUP, GROUP), 0) >= lax.broadcasted_iota(jnp.int32, (GROUP, GROUP), 1)

    def advance(memory, block):
        plain, pushed, decays, b_block, c_block = block
        running = jnp.cumsum(decays, axis=0)
        across = running.T
        spread = across[:, :, None] - across[:, None, :]
        kept = jnp.where(causal[None], jnp.exp(jnp.where(causal[None], spread, 0.0)), 0.0)
        scores = jnp.dot(c_block, b_block.T, precision=lax.Precision.HIGHEST)
        weighted = kept * scores[None]
        within = jnp.einsum('hts,shp->thp', weighted, pushed, precision=lax.Precision.HIGHEST)
        carried = jnp.einsum('tn,hpn->thp', c_block, memory, precision=lax.Precision.HIGHEST) * jnp.exp(running)[:, :, None]
        output = within + carried + skip_gain[None, :, None] * plain
        tail_decay = jnp.exp(running[-1][None, :] - running)
        memory = jnp.exp(running[-1])[:, None, None] * memory + jnp.einsum('sh,shp,sn->hpn', tail_decay, pushed, b_block, precision=lax.Precision.HIGHEST)
        return (memory, output.reshape(GROUP, width))
    final_state, outputs = lax.scan(jax.checkpoint(advance), start_state, (gated.reshape(blocks, GROUP, heads, head_dim), driven.reshape(blocks, GROUP, heads, head_dim), log_decay.reshape(blocks, GROUP, heads), b_proj.reshape(blocks, GROUP, b_proj.shape[1]), c_proj.reshape(blocks, GROUP, c_proj.shape[1])))
    return (outputs.reshape(length, width), final_state)

def one_direction(inputs, cotangent, in_weight, dt_weight, bc_weight, out_weight, rate, bias, skip_gain):
    packed = jnp.concatenate([in_weight, dt_weight, bc_weight], 1)
    projected = jnp.dot(inputs, packed, preferred_element_type=jnp.float32)
    preact = projected[:, :E]
    dt_pre = projected[:, E:E + HEADS] + bias[None, :]
    bc_proj = projected[:, E + HEADS:]
    gated = jax.nn.silu(preact)
    step_size = jax.nn.softplus(dt_pre)
    output_adjoint = jnp.dot(cotangent, out_weight.T, preferred_element_type=jnp.float32)
    start_state = jnp.zeros((HEADS, HEAD, STATE), jnp.float32)

    def core_only(gated_in, step_in, bc_in, rate_in, gain_in):
        return ssd_core(gated_in, step_in, bc_in[:, :STATE], bc_in[:, STATE:], rate_in, gain_in, start_state)[0]
    mixed, pullback = jax.vjp(core_only, gated, step_size, bc_proj, rate, skip_gain)
    d_gated, d_step, d_bc, d_rate, d_skip = pullback(output_adjoint)
    sig_pre = jax.nn.sigmoid(preact)
    d_pre = d_gated * sig_pre * (1.0 + preact * (1.0 - sig_pre))
    d_z = d_step * jax.nn.sigmoid(dt_pre)
    leading_gradient = jnp.concatenate([d_pre, d_z], 1).astype(jnp.bfloat16)
    primary_weight = jnp.concatenate([in_weight, dt_weight], 1)
    input_grad = jnp.dot(leading_gradient, primary_weight.T, preferred_element_type=jnp.float32) + jnp.dot(d_bc, bc_weight.astype(jnp.float32).T, precision=lax.Precision.HIGHEST)
    front_grad = jnp.dot(inputs.T, leading_gradient, preferred_element_type=jnp.float32)
    bc_grad = jnp.dot(inputs.astype(jnp.float32).T, d_bc, precision=lax.Precision.HIGHEST)
    out_grad_w = jnp.dot(mixed.astype(jnp.bfloat16).T, cotangent, preferred_element_type=jnp.float32)
    return (input_grad, front_grad, bc_grad, out_grad_w, d_rate * rate, lax.optimization_barrier(jnp.sum(d_z, axis=0)), d_skip)

def reference(tokens, out_grad, in_weight, dt_weight, bc_weight, out_weight, decay_rate, dt_bias, skip_gain):
    grad_scale = TOKENS ** (-0.5)
    forward = one_direction(tokens, out_grad, in_weight, dt_weight, bc_weight, out_weight, decay_rate[0], dt_bias[0], skip_gain)
    backward = one_direction(tokens[::-1], out_grad[::-1], in_weight, dt_weight, bc_weight, out_weight, decay_rate[1], dt_bias[1], skip_gain)
    tokens_grad = (forward[0] + backward[0][::-1]).astype(jnp.bfloat16)
    front_total = grad_scale * (forward[1] + backward[1])
    in_weight_grad = front_total[:, :E]
    dt_weight_grad = front_total[:, E:]
    bc_weight_grad = grad_scale * (forward[2] + backward[2])
    out_weight_grad = grad_scale * (forward[3] + backward[3])
    rate_grad = grad_scale * jnp.stack([forward[4], backward[4]])
    bias_grad = grad_scale * jnp.stack([forward[5], backward[5]])
    skip_grad = grad_scale * (forward[6] + backward[6])
    return (tokens_grad, in_weight_grad, dt_weight_grad, bc_weight_grad, out_weight_grad, rate_grad, bias_grad, skip_grad)
```

```python
import jax
import jax.numpy as jnp
from jax import lax
from jax.experimental import pallas as pl
from jax.experimental.pallas import tpu as pltpu
from jax.sharding import Mesh
from jax.sharding import PartitionSpec as P

STATE = 64
HEAD = 64
SEQ = ("seq_0", "seq_1", "seq_2")
NN = (((1,), (0,)), ((), ()))
NT = (((1,), (1,)), ((), ()))
TN = (((0,), (0,)), ((), ()))
F32 = jnp.float32
BF16 = jnp.bfloat16
INTERPRET = False


def low(x, y, dims):
    return lax.dot_general(x.astype(BF16), y.astype(BF16), dims, preferred_element_type=F32)


def halves(x):
    top = x.astype(BF16)
    return top, (x - top.astype(F32)).astype(BF16)


def mid(x, y, dims):
    xt, xl = halves(x)
    yt, yl = halves(y)
    return low(xt, yt, dims) + (low(xt, yl, dims) + low(xl, yt, dims))


def exact(x, y, dims):
    return lax.dot_general(
        x, y, dims, precision=lax.Precision.HIGHEST, preferred_element_type=F32
    )


def before(n, flip=False):
    i = lax.broadcasted_iota(jnp.int32, (n, n), 0)
    j = lax.broadcasted_iota(jnp.int32, (n, n), 1)
    return (i >= j if flip else i <= j).astype(F32)


def by_head(x, r, width):
    n = x.shape[1]
    return jnp.concatenate(
        [
            jnp.broadcast_to(x[2 * r : 2 * r + 1], (width // 2, n)),
            jnp.broadcast_to(x[2 * r + 1 : 2 * r + 2], (width // 2, n)),
        ],
        0,
    )


def forward_rows(n):
    return lax.broadcasted_iota(jnp.int32, (8, n), 0) < 2


def sigmoid(x):
    return 1.0 / (1.0 + jnp.exp(-x))


def features(both):
    n = both.shape[0] // 128
    up = [both[128 * k : 128 * k + 64] for k in range(n)]
    down = [both[128 * k + 64 : 128 * k + 128] for k in range(n)]
    return jnp.concatenate(up, 0), jnp.concatenate(down, 0)


def stage_project(both, weights, params):
    width = 128
    n = both.shape[1]
    u, q = features(both)
    pre = lax.dot_general(weights[:, :width], u, TN, preferred_element_type=F32)
    bc = lax.dot_general(weights[:, 128:256], u, TN, preferred_element_type=F32)
    cot = lax.dot_general(weights[:, 256:384], q, TN, preferred_element_type=F32)
    z = lax.dot_general(weights[:, 384:512], u, TN, preferred_element_type=F32)[:8]
    rate, bias = params[:, 0:1], params[:, 1:2]
    v = z + bias
    step = jnp.maximum(v, 0.0) + jnp.log1p(jnp.exp(-jnp.abs(v)))
    slope = sigmoid(v)
    decay = -rate * step
    run = jnp.where(
        forward_rows(n), exact(decay, before(n), NN), exact(decay, before(n, True), NN)
    )
    total = jnp.sum(decay, axis=1, keepdims=True)
    grown = jnp.exp(run)
    tail = jnp.exp(total - run)
    gated = pre * sigmoid(pre)
    b, c = bc[:STATE], bc[STATE:]
    push = step * tail
    pushed = jnp.concatenate([gated * by_head(push, r, width) for r in (0, 1)], 0)
    pulled = jnp.concatenate([cot * by_head(grown, r, width) for r in (0, 1)], 0)
    ps = mid(b, pushed, NT)
    pl_ = mid(c, pulled, NT)
    kept = jnp.broadcast_to(jnp.exp(total), (8, width))
    lane = lax.broadcasted_iota(jnp.int32, (1, width), 1)
    kept = [
        jnp.broadcast_to(
            jnp.where(lane < HEAD, kept[2 * r : 2 * r + 1], kept[2 * r + 1 : 2 * r + 2]),
            (STATE, width),
        )
        for r in (0, 1)
    ]
    sends = [
        ps[:, :width],
        pl_[:, width:],
        pl_[:, :width],
        ps[:, width:],
        kept[0],
        kept[1],
        kept[0],
        kept[1],
    ]
    vec = jnp.concatenate(
        [step, run, grown, tail, slope, jnp.broadcast_to(jnp.exp(total), (8, n))], 0
    )
    return sends, pre, bc, cot, vec


def stage_within(pre, bc, cot, vec, params):
    n = pre.shape[1]
    gated = pre * sigmoid(pre)
    b, c = bc[:STATE], bc[STATE:]
    step, run = vec[0:8], vec[8:16]
    columns = jnp.concatenate([run, jnp.zeros((120, n), F32)], 0).T
    t = lax.broadcasted_iota(jnp.int32, (n, n), 0)
    s = lax.broadcasted_iota(jnp.int32, (n, n), 1)
    later, same = t >= s, t == s
    earlier = t <= s
    scores = mid(c.T, b, NN)
    dscores = jnp.zeros((n, n), F32)
    mixed, dgated = ([], []), ([], [])
    lanes = lax.broadcasted_iota(jnp.int32, (n, 128), 1)
    rows = jnp.zeros((n, 128), F32)
    direct = [None] * 4
    for h in (0, 1):
        x = gated[HEAD * h : HEAD * (h + 1)]
        dy = cot[HEAD * h : HEAD * (h + 1)]
        step0, step1 = step[h : h + 1], step[2 + h : 3 + h]
        up = columns[:, h : h + 1] - run[h : h + 1]
        down = columns[:, 2 + h : 3 + h] - run[2 + h : 3 + h]
        fade = jnp.exp(jnp.where(later, up, down))
        pair = mid(dy.T, x, NN)
        faded = scores * fade
        moved = faded * pair
        scaled = fade * jnp.where(later, step0, step1) + jnp.where(same, step1, 0.0)
        dscores = dscores + scaled * pair
        for r, (mask, st) in enumerate(((later, step0), (earlier, step1))):
            part = jnp.where(mask, moved, 0.0)
            mix = jnp.where(mask, faded, 0.0) * st
            mixed[r].append(mid(x, mix, NT))
            dgated[r].append(mid(dy, mix, NN))
            direct[2 * r + h] = jnp.sum(part, axis=0, keepdims=True)
            rows = jnp.where(
                lanes == 2 * r + h, jnp.sum(part * st, axis=1, keepdims=True), rows
            )
    direct = jnp.concatenate(direct + [jnp.zeros((4, n), F32)], 0)
    drun = rows.T[:8] - step * direct
    gains = jnp.concatenate(
        [jnp.broadcast_to(params[h : h + 1, 2:3], (HEAD, n)) for h in (0, 1)], 0
    )
    mixed = jnp.concatenate([jnp.concatenate(m, 0) + gains * gated for m in mixed], 0)
    dgated = jnp.concatenate([jnp.concatenate(d, 0) + gains * cot for d in dgated], 0)
    both = gated * cot
    dskip = [
        2.0 * jnp.sum(both[HEAD * h : HEAD * (h + 1)], axis=0, keepdims=True) for h in (0, 1)
    ]
    dbc = jnp.concatenate([mid(c, dscores, NN), mid(b, dscores, NT)], 0)
    extra = jnp.concatenate([direct, drun] + dskip + [jnp.zeros((6, n), F32)], 0)
    return mixed, dgated, dbc, extra


def stage_finish(both, weights, params, pre, bc, cot, vec, mixed, dgated, dbc, extra, carried):
    width = 128
    n = pre.shape[1]
    u, q = features(both)
    sig = sigmoid(pre)
    gated = pre * sig
    b, c = bc[:STATE], bc[STATE:]
    step, grown, tail, slope = vec[0:8], vec[16:24], vec[24:32], vec[32:40]
    kept = vec[40:48, 0:1]
    rate = params[:, 0:1]
    h0, g1, g0, h1 = carried
    start = jnp.concatenate([h0, h1], 1)
    end = jnp.concatenate([g0, g1], 1)
    reach = mid(start.T, c, NN)
    pull = mid(end.T, b, NN)
    gains, falls, pushed, pulled = [], [], [], []
    dpre, lower = [], []
    bend = sig * (1.0 + pre * (1.0 - sig))
    for r in (0, 1):
        grow, tails, steps = (by_head(v, r, width) for v in (grown, tail, step))
        here = slice(width * r, width * (r + 1))
        got = reach[here] * grow
        lower.append((mixed[here] + got).astype(BF16))
        back = pull[here] * tails
        dpre.append(((dgated[here] + steps * back) * bend).astype(BF16))
        gain, fall = cot * got, gated * back
        for h in (0, 1):
            gains.append(jnp.sum(gain[HEAD * h : HEAD * (h + 1)], axis=0, keepdims=True))
            falls.append(jnp.sum(fall[HEAD * h : HEAD * (h + 1)], axis=0, keepdims=True))
        pulled.append(cot * grow)
        pushed.append(gated * steps * tails)
    none = [jnp.zeros((4, n), F32)]
    gains = jnp.concatenate(gains + none, 0)
    falls = jnp.concatenate(falls + none, 0)
    pulled = jnp.concatenate(pulled, 0)
    pushed = jnp.concatenate(pushed, 0)
    dbc = dbc + jnp.concatenate([mid(end, pushed, NN), mid(start, pulled, NN)], 0)
    lost = step * falls
    drun = extra[8:16] + gains - lost
    overlap = jnp.sum(start * end, axis=0, keepdims=True)
    lane = lax.broadcasted_iota(jnp.int32, (1, 2 * width), 1)
    ends = [
        jnp.sum(jnp.where(lane // HEAD == k, overlap, 0.0), axis=1, keepdims=True)
        for k in range(4)
    ]
    ends = jnp.concatenate(ends + [jnp.zeros((4, 1), F32)], 0)
    ends = kept * ends + jnp.sum(lost, axis=1, keepdims=True)
    ddecay = ends + jnp.where(
        forward_rows(n), exact(drun, before(n, True), NN), exact(drun, before(n), NN)
    )
    dstep = extra[0:8] + falls - rate * ddecay
    valid = lax.broadcasted_iota(jnp.int32, (8, n), 0) < 4
    dz = jnp.where(valid, dstep * slope, 0.0)
    drate = -jnp.sum(ddecay * step, axis=1, keepdims=True)
    dbias = jnp.sum(dz, axis=1, keepdims=True)
    dskip = jnp.sum(extra[16:24], axis=1, keepdims=True)
    dzs = jnp.concatenate([dz, jnp.zeros((120, n), F32)], 0).astype(BF16)
    dbcs = halves(dbc) if FINE else (dbc.astype(BF16),)
    front, inside = weights[:, :width], weights[:, 128:256]
    dinput = low(jnp.concatenate([front, front], 1), jnp.concatenate(dpre, 0), NN)
    dinput = dinput + low(
        jnp.concatenate([weights[:, 384:512]] + [inside] * len(dbcs), 1),
        jnp.concatenate([dzs, *dbcs], 0),
        NN,
    )
    dfront = low(u, dpre[0], NT) + low(u, dpre[1], NT)
    rest = low(u, jnp.concatenate([dbcs[0], dzs], 0), NT)
    dinside = rest[:, :width] + (low(u, dbcs[1], NT) if FINE else 0.0)
    dout = low(q, lower[0], NT) + low(q, lower[1], NT)
    lane = lax.broadcasted_iota(jnp.int32, (1, width), 1)
    numbers = jnp.zeros((1, width), F32)
    for k in range(4):
        numbers = jnp.where(lane == 8 + k, drate[k : k + 1], numbers)
        numbers = jnp.where(lane == 12 + k, dbias[k : k + 1], numbers)
    for k in range(2):
        numbers = jnp.where(lane == 16 + k, dskip[k : k + 1], numbers)
    rough = numbers.astype(BF16).astype(F32)
    fine = pltpu_roll(numbers - rough, 32)
    last = rest[:, width:] + jnp.broadcast_to(rough + fine, (u.shape[0], width))
    grads = jnp.concatenate([dfront, dinside, dout, last], 1)
    return dinput.astype(BF16), grads.astype(BF16)


def pltpu_roll(x, by):
    wide = jnp.broadcast_to(x, (8, x.shape[1]))
    return (jnp.roll(wide, by, 1) if PLAIN else pltpu.roll(wide, by, 1))[:1]


PLAIN = False
FINE = True


def call(fn, outs, args, flops):
    def kernel(*refs):
        ins, results = refs[: len(args)], refs[len(args) :]
        fn(ins, results)

    size = sum(a.size * a.dtype.itemsize for a in args)
    return pl.pallas_call(
        kernel,
        out_shape=[jax.ShapeDtypeStruct(s, d) for s, d in outs],
        cost_estimate=pl.CostEstimate(flops=flops, bytes_accessed=size, transcendentals=0),
        interpret=INTERPRET,
    )(*args)


def project(both, weights, params):
    if PLAIN:
        sends, *rest = stage_project(both, weights, params)
        return (jnp.stack(sends, 1).reshape(512, 128), *rest)

    def fn(ins, outs):
        sends, *rest = stage_project(*(r[...] for r in ins))
        for j, part in enumerate(sends):
            outs[0][pl.ds(j, STATE, stride=8), :] = part
        for ref, value in zip(outs[1:], rest):
            ref[...] = value

    n = both.shape[1]
    outs = [((512, 128), F32), ((128, n), F32), ((128, n), F32), ((128, n), F32), ((48, n), F32)]
    return call(fn, outs, (both, weights, params), 300_000_000)


def within(pre, bc, cot, vec, params):
    if PLAIN:
        return stage_within(pre, bc, cot, vec, params)

    def fn(ins, outs):
        for ref, value in zip(outs, stage_within(*(r[...] for r in ins))):
            ref[...] = value

    n = pre.shape[1]
    outs = [((256, n), F32), ((256, n), F32), ((128, n), F32), ((24, n), F32)]
    return call(fn, outs, (pre, bc, cot, vec, params), 300_000_000)


def finish(both, weights, params, pre, bc, cot, vec, mixed, dgated, dbc, extra, back):
    args = (both, weights, params, pre, bc, cot, vec, mixed, dgated, dbc, extra)
    if PLAIN:
        rows = back.reshape(64, 8, 128)
        return stage_finish(*args, [rows[:, j] for j in range(4)])

    def fn(ins, outs):
        carried = [ins[-1][pl.ds(j, STATE, stride=8), :] for j in range(4)]
        values = stage_finish(*(r[...] for r in ins[:-1]), carried)
        for ref, value in zip(outs, values):
            ref[...] = value

    n = pre.shape[1]
    outs = [((512, n), BF16), ((512, 512), BF16)]
    return call(fn, outs, (*args, back), 600_000_000)


def carry(blocks):
    count = blocks.shape[0] // 8
    if PLAIN:
        parts = blocks.reshape(count, 8, 128)
        kept, added = parts[:, 4:], parts[:, :4]
        up, down = [], []
        run = jnp.zeros((4, 128), F32)
        for k in range(count):
            up.append(run)
            run = kept[k] * run + added[k]
        run = jnp.zeros((4, 128), F32)
        for k in reversed(range(count)):
            down.append(run)
            run = kept[k] * run + added[k]
        up, down = jnp.stack(up), jnp.stack(down[::-1])
        out = jnp.concatenate([up[:, :2], down[:, 2:], jnp.zeros((count, 4, 128), F32)], 1)
        return out.reshape(-1, 128)

    def fn(ins, outs):
        src, dst = ins[0], outs[0]
        dst[...] = jnp.zeros(dst.shape, F32)
        up = jnp.zeros((2, 128), F32)
        down = jnp.zeros((2, 128), F32)
        for k in range(count):
            m = count - 1 - k
            dst[8 * k : 8 * k + 2, :] = up
            dst[8 * m + 2 : 8 * m + 4, :] = down
            up = src[8 * k + 4 : 8 * k + 6, :] * up + src[8 * k : 8 * k + 2, :]
            down = src[8 * m + 6 : 8 * m + 8, :] * down + src[8 * m + 2 : 8 * m + 4, :]

    return call(fn, [((8 * count, 128), F32)], (blocks,), 1_000_000)[0]


def exchange(array, axis):
    return lax.all_to_all(array, axis, 0, 0, tiled=True)


def to_all(array, axis):
    return exchange(jnp.broadcast_to(array[None], (lax.axis_size(axis), *array.shape)), axis)


def body(
    tokens, out_grad, in_weight, dt_weight, bc_weight, out_weight, decay_rate, dt_bias, skip_gain
):
    seq_count = lax.axis_size(SEQ)
    tok_rows = tokens.shape[0]
    width = in_weight.shape[1]
    heads = dt_weight.shape[1]
    scale = (tok_rows * seq_count) ** (-0.5)
    own = jnp.concatenate([tokens.T, out_grad.T], 0)
    both = to_all(own, "chan").reshape(-1, tok_rows)
    packed = jnp.concatenate(
        [
            in_weight,
            bc_weight,
            out_weight.T,
            dt_weight,
            dt_weight,
            jnp.zeros((in_weight.shape[0], 128 - 2 * heads), BF16),
        ],
        1,
    )
    weights = to_all(packed, SEQ).reshape(-1, 512)
    params = jnp.stack(
        [decay_rate.reshape(-1), dt_bias.reshape(-1), jnp.tile(skip_gain, 2)], 1
    )
    params = jnp.pad(params, ((0, 4), (0, 125)))
    sums, pre, bc, cot, vec = project(both, weights, params)
    sums = exchange(sums.reshape(64, 8, 128), SEQ).reshape(512, 128)
    mixed, dgated, dbc, extra = within(pre, bc, cot, vec, params)
    back = exchange(carry(sums).reshape(64, 8, 128), SEQ).reshape(512, 128)
    dinput, grads = finish(
        both, weights, params, pre, bc, cot, vec, mixed, dgated, dbc, extra, back
    )
    grads = exchange(grads.reshape(64, 8, 512), SEQ)
    summed = jnp.sum(grads.astype(F32), axis=0)
    parts = exchange(dinput.reshape(8, 64, tok_rows), "chan")
    tokens_grad = jnp.sum(parts.astype(F32), axis=0).astype(BF16).T
    in_weight_grad = scale * summed[:, :width]
    bc_weight_grad = scale * jnp.sum(to_all(summed[:, 128:256], "chan"), axis=0)
    out_weight_grad = scale * summed[:, 256:384].T
    dt_weight_grad = scale * (summed[:, 384:386] + summed[:, 386:388])
    numbers = summed[0, 392:402] + summed[0, 424:434]
    rate_grad = scale * decay_rate * numbers[:4].reshape(2, 2)
    bias_grad = scale * numbers[4:8].reshape(2, 2)
    skip_grad = scale * numbers[8:10]
    return (
        tokens_grad,
        in_weight_grad,
        dt_weight_grad,
        bc_weight_grad,
        out_weight_grad,
        rate_grad,
        bias_grad,
        skip_grad,
    )


def solution(mesh):
    split = Mesh(
        mesh.devices.reshape(8, 4, 2, mesh.shape["chan"]), ("seq_0", "seq_1", "seq_2", "chan")
    )
    return jax.shard_map(
        body,
        mesh=split,
        in_specs=(
            P(SEQ, "chan"),
            P(SEQ, "chan"),
            P(SEQ, "chan"),
            P(SEQ, "chan"),
            P(SEQ, None),
            P("chan", SEQ),
            P(None, "chan"),
            P(None, "chan"),
            P("chan"),
        ),
        out_specs=(
            P(SEQ, "chan"),
            P(SEQ, "chan"),
            P(SEQ, "chan"),
            P(SEQ, None),
            P("chan", SEQ),
            P(None, "chan"),
            P(None, "chan"),
            P("chan"),
        ),
        check_vma=False,
    )
```

```python
import jax
import jax.numpy as jnp
from jax import lax
from jax.experimental import pallas as pl
from jax.experimental.pallas import tpu as pltpu
from jax.sharding import Mesh
from jax.sharding import PartitionSpec as P

STATE = 64
HEAD = 64
SEQ = ("seq_0", "seq_1", "seq_2")
CHAN = ("chan_0", "chan_1")
NN = (((1,), (0,)), ((), ()))
NT = (((1,), (1,)), ((), ()))
TN = (((0,), (0,)), ((), ()))
F32 = jnp.float32
BF16 = jnp.bfloat16
INTERPRET = False


def low(x, y, dims):
    return lax.dot_general(x.astype(BF16), y.astype(BF16), dims, preferred_element_type=F32)


def halves(x):
    top = x.astype(BF16)
    return top, (x - top.astype(F32)).astype(BF16)


def mid(x, y, dims):
    xt, xl = halves(x)
    yt, yl = halves(y)
    return low(xt, yt, dims) + (low(xt, yl, dims) + low(xl, yt, dims))


def exact(x, y, dims):
    return lax.dot_general(
        x, y, dims, precision=lax.Precision.HIGHEST, preferred_element_type=F32
    )


def before(n, flip=False):
    i = lax.broadcasted_iota(jnp.int32, (n, n), 0)
    j = lax.broadcasted_iota(jnp.int32, (n, n), 1)
    return (i >= j if flip else i <= j).astype(F32)


def by_head(x, r, width):
    n = x.shape[1]
    return jnp.concatenate(
        [
            jnp.broadcast_to(x[2 * r : 2 * r + 1], (width // 2, n)),
            jnp.broadcast_to(x[2 * r + 1 : 2 * r + 2], (width // 2, n)),
        ],
        0,
    )


def forward_rows(n):
    return lax.broadcasted_iota(jnp.int32, (8, n), 0) < 2


def sigmoid(x):
    return 1.0 / (1.0 + jnp.exp(-x))


def features(parts):
    up, down = [], []
    for part in parts:
        for k in range(part.shape[0] // 128):
            up.append(part[128 * k : 128 * k + 64])
            down.append(part[128 * k + 64 : 128 * k + 128])
    return jnp.concatenate(up, 0), jnp.concatenate(down, 0)


def stage_project(u, q, weights, params):
    width = 128
    n = u.shape[1]
    pre = lax.dot_general(weights[:, :width], u, TN, preferred_element_type=F32)
    bc = lax.dot_general(weights[:, 128:256], u, TN, preferred_element_type=F32)
    cot = lax.dot_general(weights[:, 256:384], q, TN, preferred_element_type=F32)
    z = lax.dot_general(weights[:, 384:512], u, TN, preferred_element_type=F32)[:8]
    rate, bias = params[:, 0:1], params[:, 1:2]
    v = z + bias
    step = jnp.maximum(v, 0.0) + jnp.log1p(jnp.exp(-jnp.abs(v)))
    slope = sigmoid(v)
    decay = -rate * step
    run = jnp.where(
        forward_rows(n), exact(decay, before(n), NN), exact(decay, before(n, True), NN)
    )
    total = jnp.sum(decay, axis=1, keepdims=True)
    grown = jnp.exp(run)
    tail = jnp.exp(total - run)
    gated = pre * sigmoid(pre)
    b, c = bc[:STATE], bc[STATE:]
    push = step * tail
    pushed = jnp.concatenate([gated * by_head(push, r, width) for r in (0, 1)], 0)
    pulled = jnp.concatenate([cot * by_head(grown, r, width) for r in (0, 1)], 0)
    ps = mid(b, pushed, NT)
    pl_ = mid(c, pulled, NT)
    kept = jnp.broadcast_to(jnp.exp(total), (8, width))
    lane = lax.broadcasted_iota(jnp.int32, (1, width), 1)
    sends = [ps[:, :width], pl_[:, width:], pl_[:, :width], ps[:, width:]]
    for r in (0, 1, 0, 1):
        row = jnp.where(lane < HEAD, kept[2 * r : 2 * r + 1], kept[2 * r + 1 : 2 * r + 2])
        sends.append(jnp.broadcast_to(row, (STATE, width)))
    vec = jnp.concatenate(
        [step, run, grown, tail, slope, jnp.broadcast_to(jnp.exp(total), (8, n))], 0
    )
    return sends, pre, bc, cot, vec


def stage_within(pre, bc, cot, vec, params):
    n = pre.shape[1]
    gated = pre * sigmoid(pre)
    b, c = bc[:STATE], bc[STATE:]
    step, run = vec[0:8], vec[8:16]
    columns = jnp.concatenate([run, jnp.zeros((120, n), F32)], 0).T
    t = lax.broadcasted_iota(jnp.int32, (n, n), 0)
    s = lax.broadcasted_iota(jnp.int32, (n, n), 1)
    later, same = t >= s, t == s
    earlier = t <= s
    scores = mid(c.T, b, NN)
    dscores = jnp.zeros((n, n), F32)
    mixed, dgated = ([], []), ([], [])
    lanes = lax.broadcasted_iota(jnp.int32, (n, 128), 1)
    rows = jnp.zeros((n, 128), F32)
    direct = [None] * 4
    for h in (0, 1):
        x = gated[HEAD * h : HEAD * (h + 1)]
        dy = cot[HEAD * h : HEAD * (h + 1)]
        step0, step1 = step[h : h + 1], step[2 + h : 3 + h]
        up = columns[:, h : h + 1] - run[h : h + 1]
        down = columns[:, 2 + h : 3 + h] - run[2 + h : 3 + h]
        fade = jnp.exp(jnp.where(later, up, down))
        pair = mid(dy.T, x, NN)
        faded = scores * fade
        moved = faded * pair
        scaled = fade * jnp.where(later, step0, step1) + jnp.where(same, step1, 0.0)
        dscores = dscores + scaled * pair
        for r, (mask, st) in enumerate(((later, step0), (earlier, step1))):
            part = jnp.where(mask, moved, 0.0)
            mix = jnp.where(mask, faded, 0.0) * st
            mixed[r].append(mid(x, mix, NT))
            dgated[r].append(mid(dy, mix, NN))
            direct[2 * r + h] = jnp.sum(part, axis=0, keepdims=True)
            rows = jnp.where(
                lanes == 2 * r + h, jnp.sum(part * st, axis=1, keepdims=True), rows
            )
    direct = jnp.concatenate(direct + [jnp.zeros((4, n), F32)], 0)
    drun = rows.T[:8] - step * direct
    gains = jnp.concatenate(
        [jnp.broadcast_to(params[h : h + 1, 2:3], (HEAD, n)) for h in (0, 1)], 0
    )
    mixed = jnp.concatenate([jnp.concatenate(m, 0) + gains * gated for m in mixed], 0)
    dgated = jnp.concatenate([jnp.concatenate(d, 0) + gains * cot for d in dgated], 0)
    both = gated * cot
    dskip = [
        2.0 * jnp.sum(both[HEAD * h : HEAD * (h + 1)], axis=0, keepdims=True) for h in (0, 1)
    ]
    dbc = jnp.concatenate([mid(c, dscores, NN), mid(b, dscores, NT)], 0)
    extra = jnp.concatenate([direct, drun] + dskip + [jnp.zeros((6, n), F32)], 0)
    return mixed, dgated, dbc, extra


def stage_finish(u, q, weights, params, pre, bc, cot, vec, mixed, dgated, dbc, extra, carried):
    width = 128
    n = pre.shape[1]
    sig = sigmoid(pre)
    gated = pre * sig
    b, c = bc[:STATE], bc[STATE:]
    step, grown, tail, slope = vec[0:8], vec[16:24], vec[24:32], vec[32:40]
    kept = vec[40:48, 0:1]
    rate = params[:, 0:1]
    h0, g1, g0, h1 = carried
    start = jnp.concatenate([h0, h1], 1)
    end = jnp.concatenate([g0, g1], 1)
    reach = mid(start.T, c, NN)
    pull = mid(end.T, b, NN)
    gains, falls, pushed, pulled = [], [], [], []
    dpre, lower = [], []
    bend = sig * (1.0 + pre * (1.0 - sig))
    for r in (0, 1):
        grow, tails, steps = (by_head(v, r, width) for v in (grown, tail, step))
        here = slice(width * r, width * (r + 1))
        got = reach[here] * grow
        lower.append((mixed[here] + got).astype(BF16))
        back = pull[here] * tails
        dpre.append(((dgated[here] + steps * back) * bend).astype(BF16))
        gain, fall = cot * got, gated * back
        for h in (0, 1):
            gains.append(jnp.sum(gain[HEAD * h : HEAD * (h + 1)], axis=0, keepdims=True))
            falls.append(jnp.sum(fall[HEAD * h : HEAD * (h + 1)], axis=0, keepdims=True))
        pulled.append(cot * grow)
        pushed.append(gated * steps * tails)
    none = [jnp.zeros((4, n), F32)]
    gains = jnp.concatenate(gains + none, 0)
    falls = jnp.concatenate(falls + none, 0)
    pulled = jnp.concatenate(pulled, 0)
    pushed = jnp.concatenate(pushed, 0)
    dbc = dbc + jnp.concatenate([mid(end, pushed, NN), mid(start, pulled, NN)], 0)
    lost = step * falls
    drun = extra[8:16] + gains - lost
    overlap = jnp.sum(start * end, axis=0, keepdims=True)
    lane = lax.broadcasted_iota(jnp.int32, (1, 2 * width), 1)
    ends = [
        jnp.sum(jnp.where(lane // HEAD == k, overlap, 0.0), axis=1, keepdims=True)
        for k in range(4)
    ]
    ends = jnp.concatenate(ends + [jnp.zeros((4, 1), F32)], 0)
    ends = kept * ends + jnp.sum(lost, axis=1, keepdims=True)
    ddecay = ends + jnp.where(
        forward_rows(n), exact(drun, before(n, True), NN), exact(drun, before(n), NN)
    )
    dstep = extra[0:8] + falls - rate * ddecay
    valid = lax.broadcasted_iota(jnp.int32, (8, n), 0) < 4
    dz = jnp.where(valid, dstep * slope, 0.0)
    drate = -jnp.sum(ddecay * step, axis=1, keepdims=True)
    dbias = jnp.sum(dz, axis=1, keepdims=True)
    dskip = jnp.sum(extra[16:24], axis=1, keepdims=True)
    dzs = jnp.concatenate([dz, jnp.zeros((120, n), F32)], 0).astype(BF16)
    dbcs = halves(dbc) if FINE else (dbc.astype(BF16),)
    front, inside = weights[:, :width], weights[:, 128:256]
    dinput = low(jnp.concatenate([front, front], 1), jnp.concatenate(dpre, 0), NN)
    dinput = dinput + low(
        jnp.concatenate([weights[:, 384:512]] + [inside] * len(dbcs), 1),
        jnp.concatenate([dzs, *dbcs], 0),
        NN,
    )
    dfront = low(u, dpre[0], NT) + low(u, dpre[1], NT)
    rest = low(u, jnp.concatenate([dbcs[0], dzs], 0), NT)
    dinside = rest[:, :width] + (low(u, dbcs[1], NT) if FINE else 0.0)
    dout = low(q, lower[0], NT) + low(q, lower[1], NT)
    lane = lax.broadcasted_iota(jnp.int32, (1, width), 1)
    numbers = jnp.zeros((1, width), F32)
    for k in range(4):
        numbers = jnp.where(lane == 8 + k, drate[k : k + 1], numbers)
        numbers = jnp.where(lane == 12 + k, dbias[k : k + 1], numbers)
    for k in range(2):
        numbers = jnp.where(lane == 16 + k, dskip[k : k + 1], numbers)
    rough = numbers.astype(BF16).astype(F32)
    fine = pltpu_roll(numbers - rough, 32)
    last = rest[:, width:] + jnp.broadcast_to(rough + fine, (u.shape[0], width))
    grads = jnp.concatenate([dfront, dinside, dout, last], 1)
    return dinput.astype(BF16), grads.astype(BF16)


def pltpu_roll(x, by):
    wide = jnp.broadcast_to(x, (8, x.shape[1]))
    return (jnp.roll(wide, by, 1) if PLAIN else pltpu.roll(wide, by, 1))[:1]


PLAIN = False
FINE = True


def call(fn, outs, args, flops, scratch=(), scalars=0):
    def kernel(*refs):
        k = len(args)
        fn(refs[:k], refs[k : k + len(outs)], *refs[k + len(outs) :])

    size = sum(a.size * a.dtype.itemsize for a in args)
    spaces = [pltpu.SMEM] * scalars + [pltpu.VMEM] * (len(args) - scalars)
    return pl.pallas_call(
        kernel,
        out_shape=[jax.ShapeDtypeStruct(s, d) for s, d in outs],
        in_specs=[pl.BlockSpec(memory_space=m) for m in spaces],
        scratch_shapes=list(scratch),
        cost_estimate=pl.CostEstimate(flops=flops, bytes_accessed=size, transcendentals=0),
        compiler_params=pltpu.CompilerParams(vmem_limit_bytes=24 << 20),
        interpret=INTERPRET,
    )(*args)


def in_order(order, weights):
    if PLAIN:
        return weights.reshape(8, 64, -1)[order].reshape(weights.shape)
    rows = [weights[pl.ds(pl.multiple_of(order[k] * 64, 64), 64), :] for k in range(8)]
    return jnp.concatenate(rows, 0)


def project(order, parts, weights, params):
    if PLAIN:
        sends, *rest = stage_project(*features(parts), in_order(order, weights), params)
        return (jnp.stack(sends, 1).reshape(512, 128), *rest)

    count = len(parts)

    def fn(ins, outs):
        u, q = features([r[...] for r in ins[1 : 1 + count]])
        rows = in_order(ins[0], ins[1 + count])
        sends, *rest = stage_project(u, q, rows, ins[2 + count][...])
        for j, part in enumerate(sends):
            outs[0][pl.ds(j, STATE, stride=8), :] = part
        for ref, value in zip(outs[1:], rest):
            ref[...] = value

    n = parts[0].shape[1]
    outs = [((512, 128), F32), ((128, n), F32), ((128, n), F32), ((128, n), F32), ((48, n), F32)]
    return call(fn, outs, (order, *parts, weights, params), 300_000_000, (), 1)


def within(pre, bc, cot, vec, params):
    if PLAIN:
        return stage_within(pre, bc, cot, vec, params)

    def fn(ins, outs):
        for ref, value in zip(outs, stage_within(*(r[...] for r in ins))):
            ref[...] = value

    n = pre.shape[1]
    outs = [((256, n), F32), ((256, n), F32), ((128, n), F32), ((24, n), F32)]
    return call(fn, outs, (pre, bc, cot, vec, params), 300_000_000)


def finish(order, parts, weights, params, pre, bc, cot, vec, mixed, dgated, dbc, extra, back):
    more = (params, pre, bc, cot, vec, mixed, dgated, dbc, extra)
    n = pre.shape[1]
    count = len(parts)
    if PLAIN:
        rows = back.astype(F32).reshape(64, 8, 128)
        carried = [rows[:, j] + rows[:, 4 + j] for j in range(4)]
        dinput, grads = stage_finish(
            *features(parts), in_order(order, weights), *more, carried
        )
        wide = jnp.zeros((8, 64, n), BF16).at[order].set(dinput.reshape(8, 64, n))
        grads = jnp.zeros((8, 64, 512), BF16).at[order].set(grads.reshape(8, 64, 512))
        return wide.reshape(-1, n), grads.reshape(512, 512)

    def fn(ins, outs, lines):
        u, q = features([r[...] for r in ins[1 : 1 + count]])
        rows = in_order(ins[0], ins[1 + count])
        lines[...] = ins[-1][...].astype(F32)
        carried = [
            lines[pl.ds(j, STATE, stride=8), :] + lines[pl.ds(4 + j, STATE, stride=8), :]
            for j in range(4)
        ]
        dinput, grads = stage_finish(
            u, q, rows, *(r[...] for r in ins[2 + count : -1]), carried
        )
        for k in range(8):
            at = ins[0][k]
            block = slice(64 * k, 64 * k + 64)
            outs[0][pl.ds(pl.multiple_of(at * 64, 64), 64), :] = dinput[block]
            outs[1][pl.ds(pl.multiple_of(at * 64, 64), 64), :] = grads[block]

    outs = [((512, n), BF16), ((512, 512), BF16)]
    lines = pltpu.VMEM((512, 128), F32)
    args = (order, *parts, weights, *more, back)
    return call(fn, outs, args, 600_000_000, (lines,), 1)


def carry(blocks):
    count = blocks.shape[0] // 8

    def scan(src, keep):
        up = jnp.zeros((2, 128), F32)
        down = jnp.zeros((2, 128), F32)
        for k in range(count):
            m = count - 1 - k
            keep(k, up, m, down)
            up = src[8 * k + 4 : 8 * k + 6, :] * up + src[8 * k : 8 * k + 2, :]
            down = src[8 * m + 6 : 8 * m + 8, :] * down + src[8 * m + 2 : 8 * m + 4, :]

    if PLAIN:
        ups, downs = [None] * count, [None] * count

        def keep(k, up, m, down):
            ups[k], downs[m] = up, down

        scan(blocks, keep)
        full = jnp.concatenate([jnp.stack(ups), jnp.stack(downs)], 1)
        top = full.astype(BF16)
        rest = (full - top.astype(F32)).astype(BF16)
        return jnp.concatenate([top, rest], 1).reshape(-1, 128)

    def fn(ins, outs, sums):
        def keep(k, up, m, down):
            sums[8 * k : 8 * k + 2, :] = up
            sums[8 * m + 2 : 8 * m + 4, :] = down

        scan(ins[0], keep)
        full = sums[...]
        top = full.astype(BF16).astype(F32)
        rest = pltpu.roll(full - top, 4, 0)
        line = lax.broadcasted_iota(jnp.int32, full.shape, 0)
        outs[0][...] = jnp.where(line % 8 < 4, top, rest).astype(BF16)

    lines = pltpu.VMEM((8 * count, 128), F32)
    return call(fn, [((8 * count, 128), BF16)], (blocks,), 1_000_000, (lines,))[0]


def exchange(array, axis):
    return lax.all_to_all(array, axis, 0, 0, tiled=True)


def to_all(array, axis):
    return exchange(jnp.broadcast_to(array[None], (lax.axis_size(axis), *array.shape)), axis)


def body(
    tokens, out_grad, in_weight, dt_weight, bc_weight, out_weight, decay_rate, dt_bias, skip_gain
):
    seq_count = lax.axis_size(SEQ)
    tok_rows = tokens.shape[0]
    width = in_weight.shape[1]
    heads = dt_weight.shape[1]
    scale = (tok_rows * seq_count) ** (-0.5)
    own = jnp.concatenate([tokens.T, out_grad.T], 0)
    across, around = lax.axis_index("chan_0"), lax.axis_index("chan_1")
    order = jnp.stack(
        [((across - d) % 4) * 2 + (around ^ e) for d in range(4) for e in range(2)]
    ).astype(jnp.int32)
    other = lax.ppermute(own, "chan_1", [(0, 1), (1, 0)])
    pair = jnp.concatenate([own, other], 0)
    parts = [pair] + [
        lax.ppermute(pair, "chan_0", [(k, (k + d) % 4) for k in range(4)]) for d in (1, 2, 3)
    ]
    packed = jnp.concatenate(
        [
            in_weight,
            bc_weight,
            out_weight.T,
            dt_weight,
            dt_weight,
            jnp.zeros((in_weight.shape[0], 128 - 2 * heads), BF16),
        ],
        1,
    )
    weights = to_all(packed, SEQ).reshape(-1, 512)
    params = jnp.stack(
        [decay_rate.reshape(-1), dt_bias.reshape(-1), jnp.tile(skip_gain, 2)], 1
    )
    params = jnp.pad(params, ((0, 4), (0, 125)))
    sums, pre, bc, cot, vec = project(order, parts, weights, params)
    sums = exchange(sums.reshape(64, 8, 128), SEQ).reshape(512, 128)
    mixed, dgated, dbc, extra = within(pre, bc, cot, vec, params)
    back = exchange(carry(sums).reshape(64, 8, 128), SEQ).reshape(512, 128)
    wide, grads = finish(
        order, parts, weights, params, pre, bc, cot, vec, mixed, dgated, dbc, extra, back
    )
    grads = exchange(grads.reshape(64, 8, 512), SEQ)
    summed = jnp.sum(grads.astype(F32), axis=0)
    inside = jnp.concatenate(halves(summed[:, 128:256]), 1)
    wide = jnp.concatenate(
        [wide.reshape(8, -1, tok_rows), jnp.broadcast_to(inside[None], (8, *inside.shape))], 1
    )
    parts = jnp.sum(exchange(wide, CHAN).astype(F32), axis=0)
    tokens_grad = parts[:64].astype(BF16).T
    bc_weight_grad = scale * (parts[64:, :width] + parts[64:, width:])
    in_weight_grad = scale * summed[:, :width]
    out_weight_grad = scale * summed[:, 256:384].T
    dt_weight_grad = scale * (summed[:, 384:386] + summed[:, 386:388])
    numbers = summed[0, 392:402] + summed[0, 424:434]
    rate_grad = scale * decay_rate * numbers[:4].reshape(2, 2)
    bias_grad = scale * numbers[4:8].reshape(2, 2)
    skip_grad = scale * numbers[8:10]
    return (
        tokens_grad,
        in_weight_grad,
        dt_weight_grad,
        bc_weight_grad,
        out_weight_grad,
        rate_grad,
        bias_grad,
        skip_grad,
    )


def solution(mesh):
    split = Mesh(
        mesh.devices.reshape(8, 4, 2, 4, 2), (*SEQ, *CHAN)
    )
    return jax.shard_map(
        body,
        mesh=split,
        in_specs=(
            P(SEQ, CHAN),
            P(SEQ, CHAN),
            P(SEQ, CHAN),
            P(SEQ, CHAN),
            P(SEQ, None),
            P(CHAN, SEQ),
            P(None, CHAN),
            P(None, CHAN),
            P(CHAN),
        ),
        out_specs=(
            P(SEQ, CHAN),
            P(SEQ, CHAN),
            P(SEQ, CHAN),
            P(SEQ, None),
            P(CHAN, SEQ),
            P(None, CHAN),
            P(None, CHAN),
            P(CHAN),
        ),
        check_vma=False,
    )
```

```python
import jax
import jax.numpy as jnp
from jax import lax
from jax.experimental import pallas as pl
from jax.experimental.pallas import tpu as pltpu
from jax.sharding import Mesh
from jax.sharding import PartitionSpec as P


STATE = 64
HEAD = 64
SEQ = ("seq_0", "seq_1", "seq_2")
CHAN = ("chan_0", "chan_1")
NN = (((1,), (0,)), ((), ()))
NT = (((1,), (1,)), ((), ()))
TN = (((0,), (0,)), ((), ()))
F32 = jnp.float32
BF16 = jnp.bfloat16
INTERPRET = False


def low(x, y, dims):
    return lax.dot_general(x.astype(BF16), y.astype(BF16), dims, preferred_element_type=F32)


def halves(x):
    top = x.astype(BF16)
    return top, (x - top.astype(F32)).astype(BF16)


def mid(x, y, dims):
    xt, xl = halves(x)
    yt, yl = halves(y)
    return low(xt, yt, dims) + (low(xt, yl, dims) + low(xl, yt, dims))


def exact(x, y, dims):
    return lax.dot_general(
        x, y, dims, precision=lax.Precision.HIGHEST, preferred_element_type=F32
    )


def before(n, flip=False):
    i = lax.broadcasted_iota(jnp.int32, (n, n), 0)
    j = lax.broadcasted_iota(jnp.int32, (n, n), 1)
    return (i >= j if flip else i <= j).astype(F32)


def by_head(x, r, width):
    n = x.shape[1]
    return jnp.concatenate(
        [
            jnp.broadcast_to(x[2 * r : 2 * r + 1], (width // 2, n)),
            jnp.broadcast_to(x[2 * r + 1 : 2 * r + 2], (width // 2, n)),
        ],
        0,
    )


def forward_rows(n):
    return lax.broadcasted_iota(jnp.int32, (8, n), 0) < 2


def sigmoid(x):
    return 1.0 / (1.0 + jnp.exp(-x))


def features(parts):
    up, down = [], []
    for part in parts:
        for k in range(part.shape[0] // 128):
            up.append(part[128 * k : 128 * k + 64])
            down.append(part[128 * k + 64 : 128 * k + 128])
    return jnp.concatenate(up, 0), jnp.concatenate(down, 0)


def stage_project(u, q, weights, params):
    width = 128
    n = u.shape[1]
    pre = lax.dot_general(weights[:, :width], u, TN, preferred_element_type=F32)
    bc = lax.dot_general(weights[:, 128:256], u, TN, preferred_element_type=F32)
    cot = lax.dot_general(weights[:, 256:384], q, TN, preferred_element_type=F32)
    z = lax.dot_general(weights[:, 384:512], u, TN, preferred_element_type=F32)[:8]
    rate, bias = params[:, 0:1], params[:, 1:2]
    v = z + bias
    step = jnp.maximum(v, 0.0) + jnp.log1p(jnp.exp(-jnp.abs(v)))
    slope = sigmoid(v)
    decay = -rate * step
    run = jnp.where(
        forward_rows(n), exact(decay, before(n), NN), exact(decay, before(n, True), NN)
    )
    total = jnp.sum(decay, axis=1, keepdims=True)
    grown = jnp.exp(run)
    tail = jnp.exp(total - run)
    gated = pre * sigmoid(pre)
    b, c = bc[:STATE], bc[STATE:]
    push = step * tail
    pushed = jnp.concatenate([gated * by_head(push, r, width) for r in (0, 1)], 0)
    pulled = jnp.concatenate([cot * by_head(grown, r, width) for r in (0, 1)], 0)
    ps = mid(b, pushed, NT)
    pl_ = mid(c, pulled, NT)
    kept = jnp.broadcast_to(jnp.exp(total), (8, width))
    lane = lax.broadcasted_iota(jnp.int32, (1, width), 1)
    sends = [ps[:, :width], pl_[:, width:], pl_[:, :width], ps[:, width:]]
    for r in (0, 1, 0, 1):
        row = jnp.where(lane < HEAD, kept[2 * r : 2 * r + 1], kept[2 * r + 1 : 2 * r + 2])
        sends.append(jnp.broadcast_to(row, (STATE, width)))
    vec = jnp.concatenate(
        [step, run, grown, tail, slope, jnp.broadcast_to(jnp.exp(total), (8, n))], 0
    )
    return sends, pre, bc, cot, vec


def stage_within(pre, bc, cot, vec, params):
    n = pre.shape[1]
    gated = pre * sigmoid(pre)
    b, c = bc[:STATE], bc[STATE:]
    step, run = vec[0:8], vec[8:16]
    columns = jnp.concatenate([run, jnp.zeros((120, n), F32)], 0).T
    t = lax.broadcasted_iota(jnp.int32, (n, n), 0)
    s = lax.broadcasted_iota(jnp.int32, (n, n), 1)
    later, same = t >= s, t == s
    earlier = t <= s
    scores = mid(c.T, b, NN)
    dscores = jnp.zeros((n, n), F32)
    mixed, dgated = ([], []), ([], [])
    lanes = lax.broadcasted_iota(jnp.int32, (n, 128), 1)
    rows = jnp.zeros((n, 128), F32)
    direct = [None] * 4
    for h in (0, 1):
        x = gated[HEAD * h : HEAD * (h + 1)]
        dy = cot[HEAD * h : HEAD * (h + 1)]
        step0, step1 = step[h : h + 1], step[2 + h : 3 + h]
        up = columns[:, h : h + 1] - run[h : h + 1]
        down = columns[:, 2 + h : 3 + h] - run[2 + h : 3 + h]
        fade = jnp.exp(jnp.where(later, up, down))
        pair = mid(dy.T, x, NN)
        faded = scores * fade
        moved = faded * pair
        scaled = fade * jnp.where(later, step0, step1) + jnp.where(same, step1, 0.0)
        dscores = dscores + scaled * pair
        for r, (mask, st) in enumerate(((later, step0), (earlier, step1))):
            part = jnp.where(mask, moved, 0.0)
            mix = jnp.where(mask, faded, 0.0) * st
            mixed[r].append(mid(x, mix, NT))
            dgated[r].append(mid(dy, mix, NN))
            direct[2 * r + h] = jnp.sum(part, axis=0, keepdims=True)
            rows = jnp.where(
                lanes == 2 * r + h, jnp.sum(part * st, axis=1, keepdims=True), rows
            )
    direct = jnp.concatenate(direct + [jnp.zeros((4, n), F32)], 0)
    drun = rows.T[:8] - step * direct
    gains = jnp.concatenate(
        [jnp.broadcast_to(params[h : h + 1, 2:3], (HEAD, n)) for h in (0, 1)], 0
    )
    mixed = jnp.concatenate([jnp.concatenate(m, 0) + gains * gated for m in mixed], 0)
    dgated = jnp.concatenate([jnp.concatenate(d, 0) + gains * cot for d in dgated], 0)
    both = gated * cot
    dskip = [
        2.0 * jnp.sum(both[HEAD * h : HEAD * (h + 1)], axis=0, keepdims=True) for h in (0, 1)
    ]
    dbc = jnp.concatenate([mid(c, dscores, NN), mid(b, dscores, NT)], 0)
    extra = jnp.concatenate([direct, drun] + dskip + [jnp.zeros((6, n), F32)], 0)
    return mixed, dgated, dbc, extra


def stage_finish(u, q, weights, params, pre, bc, cot, vec, mixed, dgated, dbc, extra, carried):
    width = 128
    n = pre.shape[1]
    sig = sigmoid(pre)
    gated = pre * sig
    b, c = bc[:STATE], bc[STATE:]
    step, grown, tail, slope = vec[0:8], vec[16:24], vec[24:32], vec[32:40]
    kept = vec[40:48, 0:1]
    rate = params[:, 0:1]
    h0, g1, g0, h1 = carried
    start = jnp.concatenate([h0, h1], 1)
    end = jnp.concatenate([g0, g1], 1)
    reach = mid(start.T, c, NN)
    pull = mid(end.T, b, NN)
    gains, falls, pushed, pulled = [], [], [], []
    dpre, lower = [], []
    bend = sig * (1.0 + pre * (1.0 - sig))
    for r in (0, 1):
        grow, tails, steps = (by_head(v, r, width) for v in (grown, tail, step))
        here = slice(width * r, width * (r + 1))
        got = reach[here] * grow
        lower.append((mixed[here] + got).astype(BF16))
        back = pull[here] * tails
        dpre.append(((dgated[here] + steps * back) * bend).astype(BF16))
        gain, fall = cot * got, gated * back
        for h in (0, 1):
            gains.append(jnp.sum(gain[HEAD * h : HEAD * (h + 1)], axis=0, keepdims=True))
            falls.append(jnp.sum(fall[HEAD * h : HEAD * (h + 1)], axis=0, keepdims=True))
        pulled.append(cot * grow)
        pushed.append(gated * steps * tails)
    none = [jnp.zeros((4, n), F32)]
    gains = jnp.concatenate(gains + none, 0)
    falls = jnp.concatenate(falls + none, 0)
    pulled = jnp.concatenate(pulled, 0)
    pushed = jnp.concatenate(pushed, 0)
    dbc = dbc + jnp.concatenate([mid(end, pushed, NN), mid(start, pulled, NN)], 0)
    lost = step * falls
    drun = extra[8:16] + gains - lost
    overlap = jnp.sum(start * end, axis=0, keepdims=True)
    lane = lax.broadcasted_iota(jnp.int32, (1, 2 * width), 1)
    ends = [
        jnp.sum(jnp.where(lane // HEAD == k, overlap, 0.0), axis=1, keepdims=True)
        for k in range(4)
    ]
    ends = jnp.concatenate(ends + [jnp.zeros((4, 1), F32)], 0)
    ends = kept * ends + jnp.sum(lost, axis=1, keepdims=True)
    ddecay = ends + jnp.where(
        forward_rows(n), exact(drun, before(n, True), NN), exact(drun, before(n), NN)
    )
    dstep = extra[0:8] + falls - rate * ddecay
    valid = lax.broadcasted_iota(jnp.int32, (8, n), 0) < 4
    dz = jnp.where(valid, dstep * slope, 0.0)
    drate = -jnp.sum(ddecay * step, axis=1, keepdims=True)
    dbias = jnp.sum(dz, axis=1, keepdims=True)
    dskip = jnp.sum(extra[16:24], axis=1, keepdims=True)
    dzs = jnp.concatenate([dz, jnp.zeros((120, n), F32)], 0).astype(BF16)
    dbcs = halves(dbc) if FINE else (dbc.astype(BF16),)
    front, inside = weights[:, :width], weights[:, 128:256]
    dinput = low(jnp.concatenate([front, front], 1), jnp.concatenate(dpre, 0), NN)
    dinput = dinput + low(
        jnp.concatenate([weights[:, 384:512]] + [inside] * len(dbcs), 1),
        jnp.concatenate([dzs, *dbcs], 0),
        NN,
    )
    dfront = low(u, dpre[0], NT) + low(u, dpre[1], NT)
    rest = low(u, jnp.concatenate([dbcs[0], dzs], 0), NT)
    dinside = rest[:, :width] + (low(u, dbcs[1], NT) if FINE else 0.0)
    dout = low(q, lower[0], NT) + low(q, lower[1], NT)
    lane = lax.broadcasted_iota(jnp.int32, (1, width), 1)
    numbers = jnp.zeros((1, width), F32)
    for k in range(4):
        numbers = jnp.where(lane == 8 + k, drate[k : k + 1], numbers)
        numbers = jnp.where(lane == 12 + k, dbias[k : k + 1], numbers)
    for k in range(2):
        numbers = jnp.where(lane == 16 + k, dskip[k : k + 1], numbers)
    rough = numbers.astype(BF16).astype(F32)
    fine = rolled(jnp.broadcast_to(numbers - rough, (8, width)), 32)[:1]
    last = rest[:, width:] + jnp.broadcast_to(rough + fine, (u.shape[0], width))
    grads = jnp.concatenate([dfront, dinside, dout, last], 1)
    return dinput.astype(BF16), grads.astype(BF16)


def rolled(x, by):
    return jnp.roll(x, by, 1) if PLAIN else pltpu.roll(x, by, 1)


PLAIN = False
FINE = True


def call(fn, outs, args, flops, scratch=(), scalars=0, aliases=None):
    def kernel(*refs):
        k = len(args)
        fn(refs[:k], refs[k : k + len(outs)], *refs[k + len(outs) :])

    size = sum(a.size * a.dtype.itemsize for a in args)
    spaces = [pltpu.SMEM] * scalars + [pltpu.VMEM] * (len(args) - scalars)
    return pl.pallas_call(
        kernel,
        out_shape=[jax.ShapeDtypeStruct(s, d) for s, d in outs],
        in_specs=[pl.BlockSpec(memory_space=m) for m in spaces],
        scratch_shapes=list(scratch),
        input_output_aliases=aliases or {},
        cost_estimate=pl.CostEstimate(flops=flops, bytes_accessed=size, transcendentals=0),
        compiler_params=pltpu.CompilerParams(vmem_limit_bytes=24 << 20),
        interpret=INTERPRET,
    )(*args)


def in_order(order, weights):
    if PLAIN:
        return weights.reshape(8, 64, -1)[order].reshape(weights.shape)
    rows = [weights[pl.ds(pl.multiple_of(order[k] * 64, 64), 64), :] for k in range(8)]
    return jnp.concatenate(rows, 0)


def project(order, parts, weights, params):
    if PLAIN:
        sends, *rest = stage_project(*features(parts), in_order(order, weights), params)
        return (jnp.stack(sends, 1).reshape(512, 128), *rest)

    count = len(parts)

    def fn(ins, outs):
        u, q = features([r[...] for r in ins[1 : 1 + count]])
        rows = in_order(ins[0], ins[1 + count])
        sends, *rest = stage_project(u, q, rows, ins[2 + count][...])
        for j, part in enumerate(sends):
            outs[0][pl.ds(j, STATE, stride=8), :] = part
        for ref, value in zip(outs[1:], rest):
            ref[...] = value

    n = parts[0].shape[1]
    outs = [((512, 128), F32), ((128, n), F32), ((128, n), F32), ((128, n), F32), ((48, n), F32)]
    return call(fn, outs, (order, *parts, weights, params), 300_000_000, (), 1)


def within(pre, bc, cot, vec, params):
    if PLAIN:
        return stage_within(pre, bc, cot, vec, params)

    def fn(ins, outs):
        for ref, value in zip(outs, stage_within(*(r[...] for r in ins))):
            ref[...] = value

    n = pre.shape[1]
    outs = [((256, n), F32), ((256, n), F32), ((128, n), F32), ((24, n), F32)]
    return call(fn, outs, (pre, bc, cot, vec, params), 300_000_000)


def finish(order, parts, weights, params, pre, bc, cot, vec, mixed, dgated, dbc, extra, back):
    more = (params, pre, bc, cot, vec, mixed, dgated, dbc, extra)
    n = pre.shape[1]
    count = len(parts)
    if PLAIN:
        rows = back.astype(F32).reshape(64, 8, 128)
        carried = [rows[:, j] + rows[:, 4 + j] for j in range(4)]
        dinput, grads = stage_finish(
            *features(parts), in_order(order, weights), *more, carried
        )
        wide = jnp.zeros((8, 72, n), BF16).at[order, :64].set(dinput.reshape(8, 64, n))
        grads = jnp.zeros((8, 64, 512), BF16).at[order].set(grads.reshape(8, 64, 512))
        return wide, grads.reshape(512, 512)

    def fn(ins, outs, lines):
        u, q = features([r[...] for r in ins[1 : 1 + count]])
        rows = in_order(ins[0], ins[1 + count])
        lines[...] = ins[-1][...].astype(F32)
        carried = [
            lines[pl.ds(j, STATE, stride=8), :] + lines[pl.ds(4 + j, STATE, stride=8), :]
            for j in range(4)
        ]
        dinput, grads = stage_finish(
            u, q, rows, *(r[...] for r in ins[2 + count : -1]), carried
        )
        for k in range(8):
            at = ins[0][k]
            block = slice(64 * k, 64 * k + 64)
            outs[0][at, :64, :] = dinput[block]
            outs[0][at, 64:, :] = jnp.zeros((8, n), BF16)
            outs[1][pl.ds(pl.multiple_of(at * 64, 64), 64), :] = grads[block]

    outs = [((8, 72, n), BF16), ((512, 512), BF16)]
    lines = pltpu.VMEM((512, 128), F32)
    args = (order, *parts, weights, *more, back)
    return call(fn, outs, args, 600_000_000, (lines,), 1)


def carry(blocks):
    count = blocks.shape[0] // 8

    def scan(src, keep):
        up = jnp.zeros((2, 128), F32)
        down = jnp.zeros((2, 128), F32)
        for k in range(count):
            m = count - 1 - k
            keep(k, up, m, down)
            up = src[8 * k + 4 : 8 * k + 6, :] * up + src[8 * k : 8 * k + 2, :]
            down = src[8 * m + 6 : 8 * m + 8, :] * down + src[8 * m + 2 : 8 * m + 4, :]

    if PLAIN:
        ups, downs = [None] * count, [None] * count

        def keep(k, up, m, down):
            ups[k], downs[m] = up, down

        scan(blocks, keep)
        full = jnp.concatenate([jnp.stack(ups), jnp.stack(downs)], 1)
        top = full.astype(BF16)
        rest = (full - top.astype(F32)).astype(BF16)
        return jnp.concatenate([top, rest], 1).reshape(-1, 128)

    def fn(ins, outs, sums):
        def keep(k, up, m, down):
            sums[8 * k : 8 * k + 2, :] = up
            sums[8 * m + 2 : 8 * m + 4, :] = down

        scan(ins[0], keep)
        full = sums[...]
        top = full.astype(BF16).astype(F32)
        rest = pltpu.roll(full - top, 4, 0)
        line = lax.broadcasted_iota(jnp.int32, full.shape, 0)
        outs[0][...] = jnp.where(line % 8 < 4, top, rest).astype(BF16)

    lines = pltpu.VMEM((8 * count, 128), F32)
    return call(fn, [((8 * count, 128), BF16)], (blocks,), 1_000_000, (lines,))[0]


def send_rows(in_weight, bc_weight, out_rows, dt_rows):
    def fill(inw, bcw, outw, dtw):
        lane = lax.broadcasted_iota(jnp.int32, (8, 128), 1)
        square = lax.broadcasted_iota(jnp.int32, (8, 8), 0) == lax.broadcasted_iota(
            jnp.int32, (8, 8), 1
        )
        last = jnp.zeros((8, 128), F32)
        for k in range(4):
            row = jnp.broadcast_to(dtw[k % 2 : k % 2 + 1].astype(F32), (8, 8))
            column = jnp.sum(jnp.where(square, row, 0.0), axis=1, keepdims=True)
            last = jnp.where(lane == k, column, last)
        return jnp.concatenate([inw, bcw, outw, last.astype(BF16)], 1)

    args = (in_weight, bc_weight, out_rows, dt_rows)
    if PLAIN:
        return jnp.broadcast_to(fill(*args)[None], (64, 8, 512))

    def fn(ins, outs):
        rows = fill(*(r[...] for r in ins))
        outs[0][...] = jnp.broadcast_to(rows[None], (64, 8, 512))

    return call(fn, [((64, 8, 512), BF16)], args, 1_000_000)[0]


def add_rows(grads, wide, decay_rate, scale):
    def add(pieces, rates):
        total = jnp.sum(pieces.astype(F32), axis=0)
        inside = jnp.concatenate(halves(total[:, 128:256]), 1)
        last = total[:, 384:512]
        numbers = scale * (last + rolled(last, 96))[:1]
        lane = lax.broadcasted_iota(jnp.int32, (1, 128), 1)

        def pick(k):
            return jnp.sum(jnp.where(lane == k, numbers, 0.0), axis=1, keepdims=True)

        def table(shape, at):
            i = lax.broadcasted_iota(jnp.int32, shape, 0)
            j = lax.broadcasted_iota(jnp.int32, shape, 1)
            out = jnp.zeros(shape, F32)
            for k in range(shape[0] * shape[1]):
                out = jnp.where(i * shape[1] + j == k, pick(at + k), out)
            return out

        square = lax.broadcasted_iota(jnp.int32, (8, 8), 0) == lax.broadcasted_iota(
            jnp.int32, (8, 8), 1
        )
        steps = [
            jnp.sum(
                jnp.where(square, last[:, k : k + 1] + last[:, k + 2 : k + 3], 0.0),
                axis=0,
                keepdims=True,
            )
            for k in (0, 1)
        ]
        return (
            jnp.broadcast_to(inside[None], (8, *inside.shape)),
            scale * total[:, :128],
            scale * total[:, 256:384],
            scale * jnp.concatenate(steps, 0),
            table((2, 2), 8) * rates,
            table((2, 2), 12),
            table((1, 2), 16),
        )

    if PLAIN:
        inside, *rest = add(grads, decay_rate)
    else:

        def fn(ins, outs):
            for ref, value in zip(outs, add(ins[0][...], ins[1][...])):
                ref[...] = value

        shapes = [(8, 128), (8, 128), (2, 8), (2, 2), (2, 2), (1, 2)]
        outs = [((8, 8, 256), BF16)] + [(shape, F32) for shape in shapes]
        inside, *rest = call(fn, outs, (grads, decay_rate), 1_000_000)
    return wide.at[:, 64:].set(inside), *rest


def add_parts(parts, scale):
    def add(pieces):
        total = jnp.sum(pieces.astype(F32), axis=0)
        return total[:64].astype(BF16), scale * (total[64:, :128] + total[64:, 128:])

    if PLAIN:
        return add(parts)

    def fn(ins, outs):
        outs[0][...], outs[1][...] = add(ins[0][...])

    n = parts.shape[2]
    return call(fn, [((64, n), BF16), ((8, 128), F32)], (parts,), 1_000_000)


def exchange(array, axis):
    return lax.all_to_all(array, axis, 0, 0, tiled=True)


def body(
    tokens, out_grad, in_weight, dt_weight, bc_weight, out_weight, decay_rate, dt_bias, skip_gain
):
    seq_count = lax.axis_size(SEQ)
    tok_rows = tokens.shape[0]
    scale = (tok_rows * seq_count) ** (-0.5)
    own = jnp.concatenate([tokens.T, out_grad.T], 0)
    across, around = lax.axis_index("chan_0"), lax.axis_index("chan_1")
    order = jnp.stack(
        [((across - d) % 4) * 2 + (around ^ e) for d in range(4) for e in range(2)]
    ).astype(jnp.int32)
    other = lax.ppermute(own, "chan_1", [(0, 1), (1, 0)])
    pair = jnp.concatenate([own, other], 0)
    parts = [pair] + [
        lax.ppermute(pair, "chan_0", [(k, (k + d) % 4) for k in range(4)]) for d in (1, 2, 3)
    ]
    rows = send_rows(in_weight, bc_weight, out_weight.T, dt_weight.T)
    weights = exchange(rows, SEQ).reshape(-1, 512)
    params = jnp.stack(
        [decay_rate.reshape(-1), dt_bias.reshape(-1), jnp.tile(skip_gain, 2)], 1
    )
    params = jnp.pad(params, ((0, 4), (0, 125)))
    sums, pre, bc, cot, vec = project(order, parts, weights, params)
    sums = exchange(sums.reshape(64, 8, 128), SEQ).reshape(512, 128)
    mixed, dgated, dbc, extra = within(pre, bc, cot, vec, params)
    back = exchange(carry(sums).reshape(64, 8, 128), SEQ).reshape(512, 128)
    wide, grads = finish(
        order, parts, weights, params, pre, bc, cot, vec, mixed, dgated, dbc, extra, back
    )
    grads = exchange(grads.reshape(64, 8, 512), SEQ)
    wide, in_weight_grad, out_rows, dt_rows, rate_grad, bias_grad, skip_grad = add_rows(
        grads, wide, decay_rate, scale
    )
    tokens_grad, bc_weight_grad = add_parts(exchange(wide, CHAN), scale)
    tokens_grad = tokens_grad.T
    out_weight_grad = out_rows.T
    dt_weight_grad = dt_rows.T
    skip_grad = skip_grad.reshape(-1)
    return (
        tokens_grad,
        in_weight_grad,
        dt_weight_grad,
        bc_weight_grad,
        out_weight_grad,
        rate_grad,
        bias_grad,
        skip_grad,
    )


def solution(mesh):
    split = Mesh(
        mesh.devices.reshape(8, 4, 2, 4, 2), (*SEQ, *CHAN)
    )
    return jax.shard_map(
        body,
        mesh=split,
        in_specs=(
            P(SEQ, CHAN),
            P(SEQ, CHAN),
            P(SEQ, CHAN),
            P(SEQ, CHAN),
            P(SEQ, None),
            P(CHAN, SEQ),
            P(None, CHAN),
            P(None, CHAN),
            P(CHAN),
        ),
        out_specs=(
            P(SEQ, CHAN),
            P(SEQ, CHAN),
            P(SEQ, CHAN),
            P(SEQ, None),
            P(CHAN, SEQ),
            P(None, CHAN),
            P(None, CHAN),
            P(CHAN),
        ),
        check_vma=False,
    )
```

```python
import jax
import jax.numpy as jnp
from jax import lax
from jax.experimental import pallas as pl
from jax.experimental.pallas import tpu as pltpu
from jax.sharding import Mesh
from jax.sharding import PartitionSpec as P


STATE = 64
HEAD = 64
SEQ = ("seq_0", "seq_1", "seq_2")
ZY = ("seq_0", "seq_1")
CORE = "seq_2"
CHAN = ("chan_0", "chan_1")
NN = (((1,), (0,)), ((), ()))
NT = (((1,), (1,)), ((), ()))
TN = (((0,), (0,)), ((), ()))
F32 = jnp.float32
BF16 = jnp.bfloat16
INTERPRET = False


def low(x, y, dims):
    return lax.dot_general(x.astype(BF16), y.astype(BF16), dims, preferred_element_type=F32)


def halves(x):
    top = x.astype(BF16)
    return top, (x - top.astype(F32)).astype(BF16)


def mid(x, y, dims):
    xt, xl = halves(x)
    yt, yl = halves(y)
    return low(xt, yt, dims) + (low(xt, yl, dims) + low(xl, yt, dims))


def exact(x, y, dims):
    return lax.dot_general(
        x, y, dims, precision=lax.Precision.HIGHEST, preferred_element_type=F32
    )


def before(n, flip=False):
    i = lax.broadcasted_iota(jnp.int32, (n, n), 0)
    j = lax.broadcasted_iota(jnp.int32, (n, n), 1)
    return (i >= j if flip else i <= j).astype(F32)


def by_head(x, r, width):
    n = x.shape[1]
    return jnp.concatenate(
        [
            jnp.broadcast_to(x[2 * r : 2 * r + 1], (width // 2, n)),
            jnp.broadcast_to(x[2 * r + 1 : 2 * r + 2], (width // 2, n)),
        ],
        0,
    )


def forward_rows(n):
    return lax.broadcasted_iota(jnp.int32, (8, n), 0) < 2


def sigmoid(x):
    return 1.0 / (1.0 + jnp.exp(-x))


def stage_project(u, q, weights, params):
    width = 128
    n = u.shape[1]
    pre = lax.dot_general(weights[:, :width], u, TN, preferred_element_type=F32)
    bc = lax.dot_general(weights[:, 128:256], u, TN, preferred_element_type=F32)
    cot = lax.dot_general(weights[:, 256:384], q, TN, preferred_element_type=F32)
    z = lax.dot_general(weights[:, 384:512], u, TN, preferred_element_type=F32)[:8]
    rate, bias = params[:, 0:1], params[:, 1:2]
    v = z + bias
    step = jnp.maximum(v, 0.0) + jnp.log1p(jnp.exp(-jnp.abs(v)))
    slope = sigmoid(v)
    decay = -rate * step
    run = jnp.where(
        forward_rows(n), exact(decay, before(n), NN), exact(decay, before(n, True), NN)
    )
    total = jnp.sum(decay, axis=1, keepdims=True)
    grown = jnp.exp(run)
    tail = jnp.exp(total - run)
    gated = pre * sigmoid(pre)
    b, c = bc[:STATE], bc[STATE:]
    push = step * tail
    pushed = jnp.concatenate([gated * by_head(push, r, width) for r in (0, 1)], 0)
    pulled = jnp.concatenate([cot * by_head(grown, r, width) for r in (0, 1)], 0)
    ps = mid(b, pushed, NT)
    pl_ = mid(c, pulled, NT)
    kept = jnp.broadcast_to(jnp.exp(total), (8, width))
    lane = lax.broadcasted_iota(jnp.int32, (1, width), 1)
    sends = [ps[:, :width], pl_[:, width:], pl_[:, :width], ps[:, width:]]
    tops = [part.astype(BF16).astype(F32) for part in sends]
    rests = [part - top for part, top in zip(sends, tops)]
    for k in range(4):
        top = kept[k : k + 1].astype(BF16).astype(F32)
        rests[3] = jnp.where(lane == 120 + 2 * k, top, rests[3])
        rests[3] = jnp.where(lane == 121 + 2 * k, kept[k : k + 1] - top, rests[3])
    sends = tops + rests
    vec = jnp.concatenate(
        [step, run, grown, tail, slope, jnp.broadcast_to(jnp.exp(total), (8, n))], 0
    )
    return sends, pre, bc, cot, vec


def stage_within(pre, bc, cot, vec, params):
    n = pre.shape[1]
    gated = pre * sigmoid(pre)
    b, c = bc[:STATE], bc[STATE:]
    step, run = vec[0:8], vec[8:16]
    columns = jnp.concatenate([run, jnp.zeros((120, n), F32)], 0).T
    t = lax.broadcasted_iota(jnp.int32, (n, n), 0)
    s = lax.broadcasted_iota(jnp.int32, (n, n), 1)
    later, same = t >= s, t == s
    earlier = t <= s
    scores = mid(c.T, b, NN)
    dscores = jnp.zeros((n, n), F32)
    mixed, dgated = ([], []), ([], [])
    lanes = lax.broadcasted_iota(jnp.int32, (n, 128), 1)
    rows = jnp.zeros((n, 128), F32)
    direct = [None] * 4
    for h in (0, 1):
        x = gated[HEAD * h : HEAD * (h + 1)]
        dy = cot[HEAD * h : HEAD * (h + 1)]
        step0, step1 = step[h : h + 1], step[2 + h : 3 + h]
        up = columns[:, h : h + 1] - run[h : h + 1]
        down = columns[:, 2 + h : 3 + h] - run[2 + h : 3 + h]
        fade = jnp.exp(jnp.where(later, up, down))
        pair = mid(dy.T, x, NN)
        faded = scores * fade
        moved = faded * pair
        scaled = fade * jnp.where(later, step0, step1) + jnp.where(same, step1, 0.0)
        dscores = dscores + scaled * pair
        for r, (mask, st) in enumerate(((later, step0), (earlier, step1))):
            part = jnp.where(mask, moved, 0.0)
            mix = jnp.where(mask, faded, 0.0) * st
            mixed[r].append(mid(x, mix, NT))
            dgated[r].append(mid(dy, mix, NN))
            direct[2 * r + h] = jnp.sum(part, axis=0, keepdims=True)
            rows = jnp.where(
                lanes == 2 * r + h, jnp.sum(part * st, axis=1, keepdims=True), rows
            )
    direct = jnp.concatenate(direct + [jnp.zeros((4, n), F32)], 0)
    drun = rows.T[:8] - step * direct
    gains = jnp.concatenate(
        [jnp.broadcast_to(params[h : h + 1, 2:3], (HEAD, n)) for h in (0, 1)], 0
    )
    mixed = jnp.concatenate([jnp.concatenate(m, 0) + gains * gated for m in mixed], 0)
    dgated = jnp.concatenate([jnp.concatenate(d, 0) + gains * cot for d in dgated], 0)
    both = gated * cot
    dskip = [
        2.0 * jnp.sum(both[HEAD * h : HEAD * (h + 1)], axis=0, keepdims=True) for h in (0, 1)
    ]
    dbc = jnp.concatenate([mid(c, dscores, NN), mid(b, dscores, NT)], 0)
    extra = jnp.concatenate([direct, drun] + dskip + [jnp.zeros((6, n), F32)], 0)
    return mixed, dgated, dbc, extra


def stage_finish(u, q, weights, params, pre, bc, cot, vec, mixed, dgated, dbc, extra, carried):
    width = 128
    n = pre.shape[1]
    sig = sigmoid(pre)
    gated = pre * sig
    b, c = bc[:STATE], bc[STATE:]
    step, grown, tail, slope = vec[0:8], vec[16:24], vec[24:32], vec[32:40]
    kept = vec[40:48, 0:1]
    rate = params[:, 0:1]
    h0, g1, g0, h1 = carried
    start = jnp.concatenate([h0, h1], 1)
    end = jnp.concatenate([g0, g1], 1)
    reach = mid(start.T, c, NN)
    pull = mid(end.T, b, NN)
    gains, falls, pushed, pulled = [], [], [], []
    dpre, lower = [], []
    bend = sig * (1.0 + pre * (1.0 - sig))
    for r in (0, 1):
        grow, tails, steps = (by_head(v, r, width) for v in (grown, tail, step))
        here = slice(width * r, width * (r + 1))
        got = reach[here] * grow
        lower.append((mixed[here] + got).astype(BF16))
        back = pull[here] * tails
        dpre.append(((dgated[here] + steps * back) * bend).astype(BF16))
        gain, fall = cot * got, gated * back
        for h in (0, 1):
            gains.append(jnp.sum(gain[HEAD * h : HEAD * (h + 1)], axis=0, keepdims=True))
            falls.append(jnp.sum(fall[HEAD * h : HEAD * (h + 1)], axis=0, keepdims=True))
        pulled.append(cot * grow)
        pushed.append(gated * steps * tails)
    none = [jnp.zeros((4, n), F32)]
    gains = jnp.concatenate(gains + none, 0)
    falls = jnp.concatenate(falls + none, 0)
    pulled = jnp.concatenate(pulled, 0)
    pushed = jnp.concatenate(pushed, 0)
    dbc = dbc + jnp.concatenate([mid(end, pushed, NN), mid(start, pulled, NN)], 0)
    lost = step * falls
    drun = extra[8:16] + gains - lost
    overlap = jnp.sum(start * end, axis=0, keepdims=True)
    lane = lax.broadcasted_iota(jnp.int32, (1, 2 * width), 1)
    ends = [
        jnp.sum(jnp.where(lane // HEAD == k, overlap, 0.0), axis=1, keepdims=True)
        for k in range(4)
    ]
    ends = jnp.concatenate(ends + [jnp.zeros((4, 1), F32)], 0)
    ends = kept * ends + jnp.sum(lost, axis=1, keepdims=True)
    ddecay = ends + jnp.where(
        forward_rows(n), exact(drun, before(n, True), NN), exact(drun, before(n), NN)
    )
    dstep = extra[0:8] + falls - rate * ddecay
    valid = lax.broadcasted_iota(jnp.int32, (8, n), 0) < 4
    dz = jnp.where(valid, dstep * slope, 0.0)
    drate = -jnp.sum(ddecay * step, axis=1, keepdims=True)
    dbias = jnp.sum(dz, axis=1, keepdims=True)
    dskip = jnp.sum(extra[16:24], axis=1, keepdims=True)
    dzs = jnp.concatenate([dz, jnp.zeros((120, n), F32)], 0).astype(BF16)
    dbcs = halves(dbc) if FINE else (dbc.astype(BF16),)
    front, inside = weights[:, :width], weights[:, 128:256]
    dinput = low(jnp.concatenate([front, front], 1), jnp.concatenate(dpre, 0), NN)
    dinput = dinput + low(
        jnp.concatenate([weights[:, 384:512]] + [inside] * len(dbcs), 1),
        jnp.concatenate([dzs, *dbcs], 0),
        NN,
    )
    dfront = low(u, dpre[0], NT) + low(u, dpre[1], NT)
    rest = low(u, jnp.concatenate([dbcs[0], dzs], 0), NT)
    dinside = rest[:, :width] + (low(u, dbcs[1], NT) if FINE else 0.0)
    dout = low(q, lower[0], NT) + low(q, lower[1], NT)
    lane = lax.broadcasted_iota(jnp.int32, (1, width), 1)
    numbers = jnp.zeros((1, width), F32)
    for k in range(4):
        numbers = jnp.where(lane == 8 + k, drate[k : k + 1], numbers)
        numbers = jnp.where(lane == 12 + k, dbias[k : k + 1], numbers)
    for k in range(2):
        numbers = jnp.where(lane == 16 + k, dskip[k : k + 1], numbers)
    rough = numbers.astype(BF16).astype(F32)
    fine = rolled(jnp.broadcast_to(numbers - rough, (8, width)), 32)[:1]
    last = rest[:, width:] + jnp.broadcast_to(rough + fine, (u.shape[0], width))
    grads = jnp.concatenate([dfront, dinside, dout, last], 1)
    return dinput, grads


def rolled(x, by):
    return jnp.roll(x, by, 1) if PLAIN else pltpu.roll(x, by, 1)


PLAIN = False
SWAP = [(0, 1), (1, 0)]
FINE = True


def call(fn, outs, args, flops, scratch=(), scalars=0, grant=24 << 20):
    def kernel(*refs):
        k = len(args)
        fn(refs[:k], refs[k : k + len(outs)], *refs[k + len(outs) :])

    size = sum(a.size * a.dtype.itemsize for a in args)
    spaces = [pltpu.SMEM] * scalars + [pltpu.VMEM] * (len(args) - scalars)
    return pl.pallas_call(
        kernel,
        out_shape=[jax.ShapeDtypeStruct(s, d) for s, d in outs],
        in_specs=[pl.BlockSpec(memory_space=m) for m in spaces],
        scratch_shapes=list(scratch),
        cost_estimate=pl.CostEstimate(flops=flops, bytes_accessed=size, transcendentals=0),
        compiler_params=pltpu.CompilerParams(vmem_limit_bytes=grant),
        interpret=INTERPRET,
    )(*args)


def gathered(order, parts, own, other):
    if PLAIN:
        n = parts[0].shape[1]
        blocks = jnp.concatenate(parts, 0).reshape(8, 2, 2, 32, n)
        mine = order[8]
        u, q = (
            jnp.concatenate([blocks[:, k, mine], blocks[:, k, 1 - mine]], 0).reshape(512, n)
            for k in (0, 1)
        )
        halves_ = [w.reshape(8, 32, -1)[order[:8]] for w in (own, other)]
        return u, q, jnp.concatenate(halves_, 0).reshape(512, -1)
    mine = order[8] * 32
    up, down, rows = [], [], []
    for at, weights in ((mine, own), (32 - mine, other)):
        for k in range(8):
            part, base = parts[k // 2], 128 * (k % 2)
            up.append(part[pl.ds(pl.multiple_of(base + at, 32), 32), :])
            down.append(part[pl.ds(pl.multiple_of(base + 64 + at, 32), 32), :])
            rows.append(weights[pl.ds(pl.multiple_of(order[k] * 32, 32), 32), :])
    return jnp.concatenate(up, 0), jnp.concatenate(down, 0), jnp.concatenate(rows, 0)


def project(order, parts, own, other, params):
    if PLAIN:
        sends, *rest = stage_project(*gathered(order, parts, own, other), params)
        return (jnp.stack(sends, 1).reshape(512, 128).astype(BF16), *rest)

    def fn(ins, outs, lines):
        sends, *rest = stage_project(*gathered(ins[0], ins[1:5], ins[5], ins[6]), ins[7][...])
        for j, part in enumerate(sends):
            lines[pl.ds(j, STATE, stride=8), :] = part
        outs[0][...] = lines[...].astype(BF16)
        for ref, value in zip(outs[1:], rest):
            ref[...] = value

    n = parts[0].shape[1]
    outs = [((512, 128), BF16), ((128, n), F32), ((128, n), F32), ((128, n), F32), ((48, n), F32)]
    lines = pltpu.VMEM((512, 128), F32)
    return call(fn, outs, (order, *parts, own, other, params), 300_000_000, (lines,), 1)


def within(pre, bc, cot, vec, params):
    if PLAIN:
        return stage_within(pre, bc, cot, vec, params)

    def fn(ins, outs):
        for ref, value in zip(outs, stage_within(*(r[...] for r in ins))):
            ref[...] = value

    n = pre.shape[1]
    outs = [((256, n), F32), ((256, n), F32), ((128, n), F32), ((24, n), F32)]
    return call(fn, outs, (pre, bc, cot, vec, params), 300_000_000)


def finish(order, parts, own, other, params, pre, bc, cot, vec, mixed, dgated, dbc, extra, back):
    more = (params, pre, bc, cot, vec, mixed, dgated, dbc, extra)
    n = pre.shape[1]
    if PLAIN:
        rows = back.astype(F32).reshape(64, 8, 128)
        carried = [rows[:, j] + rows[:, 4 + j] for j in range(4)]
        dinput, grads = stage_finish(*gathered(order, parts, own, other), *more, carried)
        at, mine = order[:8], order[8]
        dinput = dinput.astype(BF16).reshape(2, 8, 32, n)
        dinput = jnp.where(mine == 0, dinput, dinput[::-1]).transpose(1, 0, 2, 3)
        wide = jnp.zeros((8, 72, n), BF16).at[at, :64].set(dinput.reshape(8, 64, n))
        grads = grads.reshape(2, 8, 32, 512)
        keep = jnp.zeros((8, 32, 512), F32).at[at].set(grads[0]).reshape(256, 512)
        give = jnp.zeros((8, 32, 512), F32).at[at].set(grads[1]).reshape(256, 512)
        return wide, keep, give.astype(BF16)

    def fn(ins, outs, lines):
        order = ins[0]
        lines[...] = ins[-1][...].astype(F32)
        carried = [
            lines[pl.ds(j, STATE, stride=8), :] + lines[pl.ds(4 + j, STATE, stride=8), :]
            for j in range(4)
        ]
        dinput, grads = stage_finish(
            *gathered(order, ins[1:5], ins[5], ins[6]), *(r[...] for r in ins[7:-1]), carried
        )
        dinput = dinput.astype(BF16)
        give = grads[256:].astype(BF16)
        mine = order[8] * 32
        for k in range(8):
            at = order[k]
            block = slice(32 * k, 32 * k + 32)
            rows = pl.ds(pl.multiple_of(at * 32, 32), 32)
            outs[0][at, pl.ds(pl.multiple_of(mine, 32), 32), :] = dinput[block]
            outs[0][at, pl.ds(pl.multiple_of(32 - mine, 32), 32), :] = dinput[256:][block]
            outs[0][at, 64:, :] = jnp.zeros((8, n), BF16)
            outs[1][rows, :] = grads[block]
            outs[2][rows, :] = give[block]

    outs = [((8, 72, n), BF16), ((256, 512), F32), ((256, 512), BF16)]
    lines = pltpu.VMEM((512, 128), F32)
    args = (order, *parts, own, other, *more, back)
    return call(fn, outs, args, 600_000_000, (lines,), 1)


def join(keep, got):
    def add(mine, theirs):
        total = mine + theirs.astype(F32)
        last = total[:, 384:]
        lane = lax.broadcasted_iota(jnp.int32, last.shape, 1)
        numbers = last + rolled(last, 96)
        rough = numbers.astype(BF16).astype(F32)
        fine = rolled(numbers - rough, 32)
        last = jnp.where(lane < 8, last, jnp.where(lane < 32, rough, fine))
        return jnp.concatenate([total[:, :384], last], 1).astype(BF16)

    if PLAIN:
        return add(keep, got)

    def fn(ins, outs):
        outs[0][...] = add(ins[0][...], ins[1][...])

    return call(fn, [(keep.shape, BF16)], (keep, got), 1_000_000)[0]


def carry(blocks):
    count = blocks.shape[0] // 8

    def unpack(take):
        lane = lax.broadcasted_iota(jnp.int32, (1, 128), 1)
        last = take(7)
        rests = [take(4), take(5), take(6), jnp.where(lane < 120, last, 0.0)]
        sums = [take(j) + rests[j] for j in range(4)]
        kept = [last[:, k : k + 1] + last[:, k + 1 : k + 2] for k in range(120, 128, 2)]
        return sums, [jnp.where(lane < HEAD, kept[2 * r], kept[2 * r + 1]) for r in (0, 1)]

    def scan(added, kept, keep):
        up = jnp.zeros((2, 128), F32)
        down = jnp.zeros((2, 128), F32)
        for k in range(count):
            m = count - 1 - k
            keep(k, up, m, down)
            up = kept[2 * k : 2 * k + 2, :] * up + added[4 * k : 4 * k + 2, :]
            down = kept[2 * m : 2 * m + 2, :] * down + added[4 * m + 2 : 4 * m + 4, :]

    if PLAIN:
        lines = blocks.astype(F32).reshape(count, 8, 128)
        sums, kept = unpack(lambda j: lines[:, j])
        ups, downs = [None] * count, [None] * count

        def keep(k, up, m, down):
            ups[k], downs[m] = up, down

        scan(jnp.stack(sums, 1).reshape(-1, 128), jnp.stack(kept, 1).reshape(-1, 128), keep)
        full = jnp.concatenate([jnp.stack(ups), jnp.stack(downs)], 1)
        top = full.astype(BF16)
        rest = (full - top.astype(F32)).astype(BF16)
        return jnp.concatenate([top, rest], 1).reshape(-1, 128)

    def fn(ins, outs, lines, added, factors, done):
        lines[...] = ins[0][...].astype(F32)
        sums, kept = unpack(lambda j: lines[pl.ds(j, count, stride=8), :])
        for j in range(4):
            added[pl.ds(j, count, stride=4), :] = sums[j]
        for r in (0, 1):
            factors[pl.ds(r, count, stride=2), :] = kept[r]

        def keep(k, up, m, down):
            done[8 * k : 8 * k + 2, :] = up
            done[8 * m + 2 : 8 * m + 4, :] = down

        scan(added, factors, keep)
        full = done[...]
        top = full.astype(BF16).astype(F32)
        rest = pltpu.roll(full - top, 4, 0)
        line = lax.broadcasted_iota(jnp.int32, full.shape, 0)
        outs[0][...] = jnp.where(line % 8 < 4, top, rest).astype(BF16)

    scratch = [pltpu.VMEM((rows * count, 128), F32) for rows in (8, 4, 2, 8)]
    return call(fn, [((8 * count, 128), BF16)], (blocks,), 1_000_000, scratch)[0]


def pack(tokens, cotangents, in_weight, bc_weight, out_rows, dt_rows):
    def fill(tok, cot, inw, bcw, outw, dtw):
        blocks = []
        for x in (tok.astype(F32), cot.astype(F32)):
            for odd in (0, 8):
                blocks += [x[k + odd : k + odd + 8] for k in range(0, 64, 16)]
        lane = lax.broadcasted_iota(jnp.int32, (8, 128), 1)
        square = lax.broadcasted_iota(jnp.int32, (8, 8), 0) == lax.broadcasted_iota(
            jnp.int32, (8, 8), 1
        )
        last = jnp.zeros((8, 128), F32)
        for k in range(4):
            row = jnp.broadcast_to(dtw[k % 2 : k % 2 + 1].astype(F32), (8, 8))
            column = jnp.sum(jnp.where(square, row, 0.0), axis=1, keepdims=True)
            last = jnp.where(lane == k, column, last)
        rows = jnp.concatenate([inw, bcw, outw, last.astype(BF16)], 1)
        return jnp.concatenate(blocks, 0).astype(BF16), jnp.broadcast_to(rows[None], (32, 8, 512))

    args = (tokens, cotangents, in_weight, bc_weight, out_rows, dt_rows)
    if PLAIN:
        return fill(*args)

    def fn(ins, outs):
        outs[0][...], outs[1][...] = fill(*(r[...] for r in ins))

    n = tokens.shape[1]
    return call(fn, [((128, n), BF16), ((32, 8, 512), BF16)], args, 1_000_000, grant=None)


def add_rows(grads, wide, decay_rate, scale):
    def add(pieces, rates):
        total = jnp.sum(pieces.astype(F32), axis=0)
        inside = jnp.concatenate(halves(total[:, 128:256]), 1)
        last = total[:, 384:512]
        numbers = scale * (last + rolled(last, 96))[:1]
        lane = lax.broadcasted_iota(jnp.int32, (1, 128), 1)

        def pick(k):
            return jnp.sum(jnp.where(lane == k, numbers, 0.0), axis=1, keepdims=True)

        def table(shape, at):
            i = lax.broadcasted_iota(jnp.int32, shape, 0)
            j = lax.broadcasted_iota(jnp.int32, shape, 1)
            out = jnp.zeros(shape, F32)
            for k in range(shape[0] * shape[1]):
                out = jnp.where(i * shape[1] + j == k, pick(at + k), out)
            return out

        square = lax.broadcasted_iota(jnp.int32, (8, 8), 0) == lax.broadcasted_iota(
            jnp.int32, (8, 8), 1
        )
        steps = [
            jnp.sum(
                jnp.where(square, last[:, k : k + 1] + last[:, k + 2 : k + 3], 0.0),
                axis=0,
                keepdims=True,
            )
            for k in (0, 1)
        ]
        return (
            jnp.broadcast_to(inside[None], (8, *inside.shape)),
            scale * total[:, :128],
            scale * total[:, 256:384],
            scale * jnp.concatenate(steps, 0),
            table((2, 2), 8) * rates,
            table((2, 2), 12),
            table((1, 2), 16),
        )

    if PLAIN:
        inside, *rest = add(grads, decay_rate)
    else:

        def fn(ins, outs):
            for ref, value in zip(outs, add(ins[0][...], ins[1][...])):
                ref[...] = value

        shapes = [(8, 128), (8, 128), (2, 8), (2, 2), (2, 2), (1, 2)]
        outs = [((8, 8, 256), BF16)] + [(shape, F32) for shape in shapes]
        inside, *rest = call(fn, outs, (grads, decay_rate), 1_000_000)
    return wide.at[:, 64:].set(inside), *rest


def add_parts(parts, scale):
    def add(pieces):
        total = jnp.sum(pieces.astype(F32), axis=0)
        blocks = [total[8 * (k // 2) + 32 * (k % 2) :][:8] for k in range(8)]
        return jnp.concatenate(blocks, 0).astype(BF16), scale * (total[64:, :128] + total[64:, 128:])

    if PLAIN:
        return add(parts)

    def fn(ins, outs):
        outs[0][...], outs[1][...] = add(ins[0][...])

    n = parts.shape[2]
    return call(fn, [((64, n), BF16), ((8, 128), F32)], (parts,), 1_000_000)


def exchange(array, axis):
    return lax.all_to_all(array, axis, 0, 0, tiled=True)


def body(
    tokens, out_grad, in_weight, dt_weight, bc_weight, out_weight, decay_rate, dt_bias, skip_gain
):
    seq_count = lax.axis_size(SEQ)
    tok_rows = tokens.shape[0]
    scale = (tok_rows * seq_count) ** (-0.5)
    own, rows = pack(
        tokens.T, out_grad.T, in_weight, bc_weight, out_weight.T, dt_weight.T
    )
    across, around = lax.axis_index("chan_0"), lax.axis_index("chan_1")
    order = jnp.stack(
        [((across - d) % 4) * 2 + (around ^ e) for d in range(4) for e in range(2)]
        + [lax.axis_index(CORE)]
    ).astype(jnp.int32)
    other = lax.ppermute(own, "chan_1", SWAP)
    pair = jnp.concatenate([own, other], 0)
    parts = [pair] + [
        lax.ppermute(pair, "chan_0", [(k, (k + d) % 4) for k in range(4)])
        for d in (1, 2, 3)
    ]
    here = exchange(rows, ZY).reshape(-1, 512)
    there = lax.ppermute(here, CORE, SWAP)
    params = jnp.stack([decay_rate.reshape(-1), dt_bias.reshape(-1), jnp.tile(skip_gain, 2)], 1)
    params = jnp.pad(params, ((0, 4), (0, 125)))
    sums, pre, bc, cot, vec = project(order, parts, here, there, params)
    sums = exchange(sums.reshape(64, 8, 128), SEQ).reshape(512, 128)
    mixed, dgated, dbc, extra = within(pre, bc, cot, vec, params)
    back = exchange(carry(sums).reshape(64, 8, 128), SEQ).reshape(512, 128)
    wide, keep, give = finish(
        order, parts, here, there, params, pre, bc, cot, vec, mixed, dgated, dbc, extra, back
    )
    grads = join(keep, lax.ppermute(give, CORE, SWAP))
    grads = exchange(grads.reshape(32, 8, 512), ZY)
    wide, in_weight_grad, out_rows, dt_rows, rate_grad, bias_grad, skip_grad = add_rows(
        grads, wide, decay_rate, scale
    )
    tokens_grad, bc_weight_grad = add_parts(exchange(wide, CHAN), scale)
    tokens_grad = tokens_grad.T
    out_weight_grad = out_rows.T
    dt_weight_grad = dt_rows.T
    skip_grad = skip_grad.reshape(-1)
    return (
        tokens_grad,
        in_weight_grad,
        dt_weight_grad,
        bc_weight_grad,
        out_weight_grad,
        rate_grad,
        bias_grad,
        skip_grad,
    )


def solution(mesh):
    split = Mesh(
        mesh.devices.reshape(8, 4, 2, 4, 2), (*SEQ, *CHAN)
    )
    return jax.shard_map(
        body,
        mesh=split,
        in_specs=(
            P(SEQ, CHAN),
            P(SEQ, CHAN),
            P(SEQ, CHAN),
            P(SEQ, CHAN),
            P(SEQ, None),
            P(CHAN, SEQ),
            P(None, CHAN),
            P(None, CHAN),
            P(CHAN),
        ),
        out_specs=(
            P(SEQ, CHAN),
            P(SEQ, CHAN),
            P(SEQ, CHAN),
            P(SEQ, None),
            P(CHAN, SEQ),
            P(None, CHAN),
            P(None, CHAN),
            P(CHAN),
        ),
        check_vma=False,
    )
```

```python
import jax
import jax.numpy as jnp
from jax import lax
from jax.experimental import pallas as pl
from jax.experimental.pallas import tpu as pltpu
from jax.sharding import Mesh
from jax.sharding import PartitionSpec as P


STATE = 64
HEAD = 64
SEQ = ("seq_0", "seq_1", "seq_2")
ZY = ("seq_0", "seq_1")
CORE = "seq_2"
CHAN = ("chan_0", "chan_1")
NN = (((1,), (0,)), ((), ()))
NT = (((1,), (1,)), ((), ()))
TN = (((0,), (0,)), ((), ()))
F32 = jnp.float32
BF16 = jnp.bfloat16
INTERPRET = False


def low(x, y, dims):
    return lax.dot_general(x.astype(BF16), y.astype(BF16), dims, preferred_element_type=F32)


def halves(x):
    top = x.astype(BF16)
    return top, (x - top.astype(F32)).astype(BF16)


def mid(x, y, dims):
    xt, xl = halves(x)
    yt, yl = halves(y)
    return low(xt, yt, dims) + (low(xt, yl, dims) + low(xl, yt, dims))


def running(x):
    n = x.shape[1]
    top, rest = halves(x)
    low_ = (x - top.astype(F32) - rest.astype(F32)).astype(BF16)
    parts = jnp.concatenate([top.astype(F32), rest.astype(F32), low_.astype(F32)], 0)
    both = jnp.concatenate([before(n), before(n, True)], 1)
    sums = low(parts, both, NN)
    sums = sums[:8] + (sums[8:16] + sums[16:24])
    return sums[:, :n], sums[:, n:]


def before(n, flip=False):
    i = lax.broadcasted_iota(jnp.int32, (n, n), 0)
    j = lax.broadcasted_iota(jnp.int32, (n, n), 1)
    return (i >= j if flip else i <= j).astype(F32)


def by_head(x, r, width):
    n = x.shape[1]
    return jnp.concatenate(
        [
            jnp.broadcast_to(x[2 * r : 2 * r + 1], (width // 2, n)),
            jnp.broadcast_to(x[2 * r + 1 : 2 * r + 2], (width // 2, n)),
        ],
        0,
    )


def forward_rows(n):
    return lax.broadcasted_iota(jnp.int32, (8, n), 0) < 2


def sigmoid(x):
    return 1.0 / (1.0 + jnp.exp(-x))


def stage_project(u, q, weights, params):
    width = 128
    n = u.shape[1]
    pre = lax.dot_general(weights[:, :width], u, TN, preferred_element_type=F32)
    bc = lax.dot_general(weights[:, 128:256], u, TN, preferred_element_type=F32)
    cot = lax.dot_general(weights[:, 256:384], q, TN, preferred_element_type=F32)
    z = lax.dot_general(weights[:, 384:512], u, TN, preferred_element_type=F32)[:8]
    rate, bias = params[:, 0:1], params[:, 1:2]
    v = z + bias
    step = jnp.maximum(v, 0.0) + jnp.log1p(jnp.exp(-jnp.abs(v)))
    slope = sigmoid(v)
    decay = -rate * step
    from_start, from_end = running(decay)
    run = jnp.where(forward_rows(n), from_start, from_end)
    total = jnp.sum(decay, axis=1, keepdims=True)
    grown = jnp.exp(run)
    tail = jnp.exp(total - run)
    gated = pre * sigmoid(pre)
    b, c = bc[:STATE], bc[STATE:]
    push = step * tail
    pushed = jnp.concatenate([gated * by_head(push, r, width) for r in (0, 1)], 0)
    pulled = jnp.concatenate([cot * by_head(grown, r, width) for r in (0, 1)], 0)
    ps = mid(b, pushed, NT)
    pl_ = mid(c, pulled, NT)
    kept = jnp.broadcast_to(jnp.exp(total), (8, width))
    lane = lax.broadcasted_iota(jnp.int32, (1, width), 1)
    sends = [ps[:, :width], pl_[:, width:], pl_[:, :width], ps[:, width:]]
    tops = [part.astype(BF16).astype(F32) for part in sends]
    rests = [part - top for part, top in zip(sends, tops)]
    for k in range(4):
        top = kept[k : k + 1].astype(BF16).astype(F32)
        rests[3] = jnp.where(lane == 120 + 2 * k, top, rests[3])
        rests[3] = jnp.where(lane == 121 + 2 * k, kept[k : k + 1] - top, rests[3])
    sends = tops + rests
    vec = jnp.concatenate(
        [step, run, grown, tail, slope, jnp.broadcast_to(jnp.exp(total), (8, n))], 0
    )
    return sends, pre, bc, cot, vec


def stage_within(pre, bc, cot, vec, params):
    n = pre.shape[1]
    gated = pre * sigmoid(pre)
    b, c = bc[:STATE], bc[STATE:]
    step, run = vec[0:8], vec[8:16]
    columns = jnp.concatenate([run, jnp.zeros((120, n), F32)], 0).T
    t = lax.broadcasted_iota(jnp.int32, (n, n), 0)
    s = lax.broadcasted_iota(jnp.int32, (n, n), 1)
    later, same = t >= s, t == s
    earlier = t <= s
    scores = mid(c.T, b, NN)
    dscores = jnp.zeros((n, n), F32)
    mixed, dgated = ([], []), ([], [])
    lanes = lax.broadcasted_iota(jnp.int32, (n, 128), 1)
    rows = jnp.zeros((n, 128), F32)
    direct = [None] * 4
    for h in (0, 1):
        x = gated[HEAD * h : HEAD * (h + 1)]
        dy = cot[HEAD * h : HEAD * (h + 1)]
        step0, step1 = step[h : h + 1], step[2 + h : 3 + h]
        up = columns[:, h : h + 1] - run[h : h + 1]
        down = columns[:, 2 + h : 3 + h] - run[2 + h : 3 + h]
        fade = jnp.exp(jnp.where(later, up, down))
        pair = mid(dy.T, x, NN)
        faded = scores * fade
        moved = faded * pair
        scaled = fade * jnp.where(later, step0, step1) + jnp.where(same, step1, 0.0)
        dscores = dscores + scaled * pair
        for r, (mask, st) in enumerate(((later, step0), (earlier, step1))):
            part = jnp.where(mask, moved, 0.0)
            mix = jnp.where(mask, faded, 0.0) * st
            mixed[r].append(mid(x, mix, NT))
            dgated[r].append(mid(dy, mix, NN))
            direct[2 * r + h] = jnp.sum(part, axis=0, keepdims=True)
            rows = jnp.where(
                lanes == 2 * r + h, jnp.sum(part * st, axis=1, keepdims=True), rows
            )
    direct = jnp.concatenate(direct + [jnp.zeros((4, n), F32)], 0)
    drun = rows.T[:8] - step * direct
    gains = jnp.concatenate(
        [jnp.broadcast_to(params[h : h + 1, 2:3], (HEAD, n)) for h in (0, 1)], 0
    )
    mixed = jnp.concatenate([jnp.concatenate(m, 0) + gains * gated for m in mixed], 0)
    dgated = jnp.concatenate([jnp.concatenate(d, 0) + gains * cot for d in dgated], 0)
    both = gated * cot
    dskip = [
        2.0 * jnp.sum(both[HEAD * h : HEAD * (h + 1)], axis=0, keepdims=True) for h in (0, 1)
    ]
    dbc = jnp.concatenate([mid(c, dscores, NN), mid(b, dscores, NT)], 0)
    extra = jnp.concatenate([direct, drun] + dskip + [jnp.zeros((6, n), F32)], 0)
    return mixed, dgated, dbc, extra


def stage_finish(u, q, weights, params, pre, bc, cot, vec, mixed, dgated, dbc, extra, carried):
    width = 128
    n = pre.shape[1]
    sig = sigmoid(pre)
    gated = pre * sig
    b, c = bc[:STATE], bc[STATE:]
    step, grown, tail, slope = vec[0:8], vec[16:24], vec[24:32], vec[32:40]
    kept = vec[40:48, 0:1]
    rate = params[:, 0:1]
    h0, g1, g0, h1 = carried
    start = jnp.concatenate([h0, h1], 1)
    end = jnp.concatenate([g0, g1], 1)
    reach = mid(start.T, c, NN)
    pull = mid(end.T, b, NN)
    gains, falls, pushed, pulled = [], [], [], []
    dpre, lower = [], []
    bend = sig * (1.0 + pre * (1.0 - sig))
    for r in (0, 1):
        grow, tails, steps = (by_head(v, r, width) for v in (grown, tail, step))
        here = slice(width * r, width * (r + 1))
        got = reach[here] * grow
        lower.append((mixed[here] + got).astype(BF16))
        back = pull[here] * tails
        dpre.append(((dgated[here] + steps * back) * bend).astype(BF16))
        gain, fall = cot * got, gated * back
        for h in (0, 1):
            gains.append(jnp.sum(gain[HEAD * h : HEAD * (h + 1)], axis=0, keepdims=True))
            falls.append(jnp.sum(fall[HEAD * h : HEAD * (h + 1)], axis=0, keepdims=True))
        pulled.append(cot * grow)
        pushed.append(gated * steps * tails)
    none = [jnp.zeros((4, n), F32)]
    gains = jnp.concatenate(gains + none, 0)
    falls = jnp.concatenate(falls + none, 0)
    pulled = jnp.concatenate(pulled, 0)
    pushed = jnp.concatenate(pushed, 0)
    dbc = dbc + jnp.concatenate([mid(end, pushed, NN), mid(start, pulled, NN)], 0)
    lost = step * falls
    drun = extra[8:16] + gains - lost
    overlap = jnp.sum(start * end, axis=0, keepdims=True)
    lane = lax.broadcasted_iota(jnp.int32, (1, 2 * width), 1)
    ends = [
        jnp.sum(jnp.where(lane // HEAD == k, overlap, 0.0), axis=1, keepdims=True)
        for k in range(4)
    ]
    ends = jnp.concatenate(ends + [jnp.zeros((4, 1), F32)], 0)
    ends = kept * ends + jnp.sum(lost, axis=1, keepdims=True)
    from_start, from_end = running(drun)
    ddecay = ends + jnp.where(forward_rows(n), from_end, from_start)
    dstep = extra[0:8] + falls - rate * ddecay
    valid = lax.broadcasted_iota(jnp.int32, (8, n), 0) < 4
    dz = jnp.where(valid, dstep * slope, 0.0)
    drate = -jnp.sum(ddecay * step, axis=1, keepdims=True)
    dbias = jnp.sum(dz, axis=1, keepdims=True)
    dskip = jnp.sum(extra[16:24], axis=1, keepdims=True)
    dzs = jnp.concatenate([dz, jnp.zeros((120, n), F32)], 0).astype(BF16)
    dbcs = halves(dbc) if FINE else (dbc.astype(BF16),)
    front, inside = weights[:, :width], weights[:, 128:256]
    dinput = low(jnp.concatenate([front, front], 1), jnp.concatenate(dpre, 0), NN)
    dinput = dinput + low(
        jnp.concatenate([weights[:, 384:512]] + [inside] * len(dbcs), 1),
        jnp.concatenate([dzs, *dbcs], 0),
        NN,
    )
    dfront = low(u, dpre[0], NT) + low(u, dpre[1], NT)
    rest = low(u, jnp.concatenate([dbcs[0], dzs], 0), NT)
    dinside = rest[:, :width] + (low(u, dbcs[1], NT) if FINE else 0.0)
    dout = low(q, lower[0], NT) + low(q, lower[1], NT)
    lane = lax.broadcasted_iota(jnp.int32, (1, width), 1)
    numbers = jnp.zeros((1, width), F32)
    for k in range(4):
        numbers = jnp.where(lane == 8 + k, drate[k : k + 1], numbers)
        numbers = jnp.where(lane == 12 + k, dbias[k : k + 1], numbers)
    for k in range(2):
        numbers = jnp.where(lane == 16 + k, dskip[k : k + 1], numbers)
    rough = numbers.astype(BF16).astype(F32)
    fine = rolled(jnp.broadcast_to(numbers - rough, (8, width)), 32)[:1]
    last = rest[:, width:] + jnp.broadcast_to(rough + fine, (u.shape[0], width))
    grads = jnp.concatenate([dfront, dinside, dout, last], 1)
    return dinput, grads


def rolled(x, by):
    return jnp.roll(x, by, 1) if PLAIN else pltpu.roll(x, by, 1)


PLAIN = False
SWAP = [(0, 1), (1, 0)]
FINE = True


def call(fn, outs, args, flops, scratch=(), scalars=0, grant=24 << 20):
    def kernel(*refs):
        k = len(args)
        fn(refs[:k], refs[k : k + len(outs)], *refs[k + len(outs) :])

    size = sum(a.size * a.dtype.itemsize for a in args)
    spaces = [pltpu.SMEM] * scalars + [pltpu.VMEM] * (len(args) - scalars)
    return pl.pallas_call(
        kernel,
        out_shape=[jax.ShapeDtypeStruct(s, d) for s, d in outs],
        in_specs=[pl.BlockSpec(memory_space=m) for m in spaces],
        scratch_shapes=list(scratch),
        cost_estimate=pl.CostEstimate(flops=flops, bytes_accessed=size, transcendentals=0),
        compiler_params=pltpu.CompilerParams(vmem_limit_bytes=grant),
        interpret=INTERPRET,
    )(*args)


def gathered(order, parts, own, other):
    if PLAIN:
        n = parts.shape[1]
        blocks = parts.reshape(8, 2, 2, 32, n)
        mine = order[8]
        u, q = (
            jnp.concatenate([blocks[:, k, mine], blocks[:, k, 1 - mine]], 0).reshape(512, n)
            for k in (0, 1)
        )
        halves_ = [w.reshape(8, 32, -1)[order[:8]] for w in (own, other)]
        return u, q, jnp.concatenate(halves_, 0).reshape(512, -1)
    mine = order[8] * 32
    up, down, rows = [], [], []
    for at, weights in ((mine, own), (32 - mine, other)):
        for k in range(8):
            base = 128 * k
            up.append(parts[pl.ds(pl.multiple_of(base + at, 32), 32), :])
            down.append(parts[pl.ds(pl.multiple_of(base + 64 + at, 32), 32), :])
            rows.append(weights[pl.ds(pl.multiple_of(order[k] * 32, 32), 32), :])
    return jnp.concatenate(up, 0), jnp.concatenate(down, 0), jnp.concatenate(rows, 0)


def project(order, parts, own, other, params):
    if PLAIN:
        sends, *rest = stage_project(*gathered(order, parts, own, other), params)
        return (jnp.stack(sends, 1).reshape(512, 128).astype(BF16), *rest)

    def fn(ins, outs, lines):
        sends, *rest = stage_project(*gathered(*ins[:4]), ins[4][...])
        for j, part in enumerate(sends):
            lines[pl.ds(j, STATE, stride=8), :] = part
        outs[0][...] = lines[...].astype(BF16)
        for ref, value in zip(outs[1:], rest):
            ref[...] = value

    n = parts.shape[1]
    outs = [((512, 128), BF16), ((128, n), F32), ((128, n), F32), ((128, n), F32), ((48, n), F32)]
    lines = pltpu.VMEM((512, 128), F32)
    return call(fn, outs, (order, parts, own, other, params), 300_000_000, (lines,), 1)


def within(pre, bc, cot, vec, params):
    if PLAIN:
        return stage_within(pre, bc, cot, vec, params)

    def fn(ins, outs):
        for ref, value in zip(outs, stage_within(*(r[...] for r in ins))):
            ref[...] = value

    n = pre.shape[1]
    outs = [((256, n), F32), ((256, n), F32), ((128, n), F32), ((24, n), F32)]
    return call(fn, outs, (pre, bc, cot, vec, params), 300_000_000)


def finish(order, parts, own, other, params, pre, bc, cot, vec, mixed, dgated, dbc, extra, back):
    more = (params, pre, bc, cot, vec, mixed, dgated, dbc, extra)
    n = pre.shape[1]
    if PLAIN:
        rows = back.astype(F32).reshape(64, 8, 128)
        carried = [rows[:, j] + rows[:, 4 + j] for j in range(4)]
        dinput, grads = stage_finish(*gathered(order, parts, own, other), *more, carried)
        at, mine = order[:8], order[8]
        dinput = dinput.astype(BF16).reshape(2, 8, 32, n)
        dinput = jnp.where(mine == 0, dinput, dinput[::-1]).transpose(1, 0, 2, 3)
        wide = jnp.zeros((8, 72, n), BF16).at[at, :64].set(dinput.reshape(8, 64, n))
        grads = grads.reshape(2, 8, 32, 512)
        keep = jnp.zeros((8, 32, 512), F32).at[at].set(grads[0]).reshape(256, 512)
        give = jnp.zeros((8, 32, 512), F32).at[at].set(grads[1]).reshape(256, 512)
        return wide, keep, give.astype(BF16)

    def fn(ins, outs, lines):
        order = ins[0]
        lines[...] = ins[-1][...].astype(F32)
        carried = [
            lines[pl.ds(j, STATE, stride=8), :] + lines[pl.ds(4 + j, STATE, stride=8), :]
            for j in range(4)
        ]
        dinput, grads = stage_finish(
            *gathered(*ins[:4]), *(r[...] for r in ins[4:-1]), carried
        )
        dinput = dinput.astype(BF16)
        give = grads[256:].astype(BF16)
        mine = order[8] * 32
        for k in range(8):
            at = order[k]
            block = slice(32 * k, 32 * k + 32)
            rows = pl.ds(pl.multiple_of(at * 32, 32), 32)
            outs[0][at, pl.ds(pl.multiple_of(mine, 32), 32), :] = dinput[block]
            outs[0][at, pl.ds(pl.multiple_of(32 - mine, 32), 32), :] = dinput[256:][block]
            outs[0][at, 64:, :] = jnp.zeros((8, n), BF16)
            outs[1][rows, :] = grads[block]
            outs[2][rows, :] = give[block]

    outs = [((8, 72, n), BF16), ((256, 512), F32), ((256, 512), BF16)]
    lines = pltpu.VMEM((512, 128), F32)
    args = (order, parts, own, other, *more, back)
    return call(fn, outs, args, 600_000_000, (lines,), 1)


def join(keep, got):
    def add(mine, theirs):
        total = mine + theirs.astype(F32)
        last = total[:, 384:]
        lane = lax.broadcasted_iota(jnp.int32, last.shape, 1)
        numbers = last + rolled(last, 96)
        rough = numbers.astype(BF16).astype(F32)
        fine = rolled(numbers - rough, 32)
        last = jnp.where(lane < 8, last, jnp.where(lane < 32, rough, fine))
        return jnp.concatenate([total[:, :384], last], 1).astype(BF16)

    if PLAIN:
        return add(keep, got)

    def fn(ins, outs):
        outs[0][...] = add(ins[0][...], ins[1][...])

    return call(fn, [(keep.shape, BF16)], (keep, got), 1_000_000)[0]


def carry(blocks):
    count = blocks.shape[0] // 8

    def unpack(take):
        lane = lax.broadcasted_iota(jnp.int32, (1, 128), 1)
        last = take(7)
        rests = [take(4), take(5), take(6), jnp.where(lane < 120, last, 0.0)]
        sums = [take(j) + rests[j] for j in range(4)]
        kept = [last[:, k : k + 1] + last[:, k + 1 : k + 2] for k in range(120, 128, 2)]
        return sums, [jnp.where(lane < HEAD, kept[2 * r], kept[2 * r + 1]) for r in (0, 1)]

    def scan(added, kept, keep):
        up = jnp.zeros((2, 128), F32)
        down = jnp.zeros((2, 128), F32)
        for k in range(count):
            m = count - 1 - k
            keep(k, up, m, down)
            up = kept[2 * k : 2 * k + 2, :] * up + added[4 * k : 4 * k + 2, :]
            down = kept[2 * m : 2 * m + 2, :] * down + added[4 * m + 2 : 4 * m + 4, :]

    if PLAIN:
        lines = blocks.astype(F32).reshape(count, 8, 128)
        sums, kept = unpack(lambda j: lines[:, j])
        ups, downs = [None] * count, [None] * count

        def keep(k, up, m, down):
            ups[k], downs[m] = up, down

        scan(jnp.stack(sums, 1).reshape(-1, 128), jnp.stack(kept, 1).reshape(-1, 128), keep)
        full = jnp.concatenate([jnp.stack(ups), jnp.stack(downs)], 1)
        top = full.astype(BF16)
        rest = (full - top.astype(F32)).astype(BF16)
        return jnp.concatenate([top, rest], 1).reshape(-1, 128)

    def fn(ins, outs, lines, added, factors, done):
        lines[...] = ins[0][...].astype(F32)
        sums, kept = unpack(lambda j: lines[pl.ds(j, count, stride=8), :])
        for j in range(4):
            added[pl.ds(j, count, stride=4), :] = sums[j]
        for r in (0, 1):
            factors[pl.ds(r, count, stride=2), :] = kept[r]

        def keep(k, up, m, down):
            done[8 * k : 8 * k + 2, :] = up
            done[8 * m + 2 : 8 * m + 4, :] = down

        scan(added, factors, keep)
        full = done[...]
        top = full.astype(BF16).astype(F32)
        rest = pltpu.roll(full - top, 4, 0)
        line = lax.broadcasted_iota(jnp.int32, full.shape, 0)
        outs[0][...] = jnp.where(line % 8 < 4, top, rest).astype(BF16)

    scratch = [pltpu.VMEM((rows * count, 128), F32) for rows in (8, 4, 2, 8)]
    return call(fn, [((8 * count, 128), BF16)], (blocks,), 1_000_000, scratch)[0]


def pack(*args):
    def fill(tok, cot, inw, bcw, outw, dtw, rates, biases, gains):
        blocks = []
        for x in (tok.astype(F32), cot.astype(F32)):
            for odd in (0, 8):
                blocks += [x[k + odd : k + odd + 8] for k in range(0, 64, 16)]
        lane = lax.broadcasted_iota(jnp.int32, (8, 128), 1)
        square = lax.broadcasted_iota(jnp.int32, (8, 8), 0) == lax.broadcasted_iota(
            jnp.int32, (8, 8), 1
        )
        last = jnp.zeros((8, 128), F32)
        for k in range(4):
            row = jnp.broadcast_to(dtw[k % 2 : k % 2 + 1].astype(F32), (8, 8))
            column = jnp.sum(jnp.where(square, row, 0.0), axis=1, keepdims=True)
            last = jnp.where(lane == k, column, last)
        rows = jnp.concatenate([inw, bcw, outw, last.astype(BF16)], 1)
        sub = lax.broadcasted_iota(jnp.int32, (8, 128), 0)
        table = jnp.zeros((8, 128), F32)
        for k in range(4):
            r, h = k // 2, k % 2
            values = (rates[r : r + 1, h : h + 1], biases[r : r + 1, h : h + 1], gains[:, h : h + 1])
            for at, value in enumerate(values):
                table = jnp.where((sub == k) & (lane == at), value, table)
        return (
            jnp.concatenate(blocks, 0).astype(BF16),
            jnp.broadcast_to(rows[None], (32, 8, 512)),
            table,
        )

    if PLAIN:
        return fill(*args)

    def fn(ins, outs):
        for ref, value in zip(outs, fill(*(r[...] for r in ins))):
            ref[...] = value

    outs = [((128, args[0].shape[1]), BF16), ((32, 8, 512), BF16), ((8, 128), F32)]
    return call(fn, outs, args, 1_000_000, grant=None)


def add_rows(grads, wide, decay_rate, scale):
    def add(pieces, rates):
        total = jnp.sum(pieces.astype(F32), axis=0)
        inside = jnp.concatenate(halves(total[:, 128:256]), 1)
        last = total[:, 384:512]
        numbers = scale * (last + rolled(last, 96))[:1]
        lane = lax.broadcasted_iota(jnp.int32, (1, 128), 1)

        def pick(k):
            return jnp.sum(jnp.where(lane == k, numbers, 0.0), axis=1, keepdims=True)

        def table(shape, at):
            i = lax.broadcasted_iota(jnp.int32, shape, 0)
            j = lax.broadcasted_iota(jnp.int32, shape, 1)
            out = jnp.zeros(shape, F32)
            for k in range(shape[0] * shape[1]):
                out = jnp.where(i * shape[1] + j == k, pick(at + k), out)
            return out

        square = lax.broadcasted_iota(jnp.int32, (8, 8), 0) == lax.broadcasted_iota(
            jnp.int32, (8, 8), 1
        )
        steps = [
            jnp.sum(
                jnp.where(square, last[:, k : k + 1] + last[:, k + 2 : k + 3], 0.0),
                axis=0,
                keepdims=True,
            )
            for k in (0, 1)
        ]
        return (
            jnp.broadcast_to(inside[None], (8, *inside.shape)),
            scale * total[:, :128],
            scale * total[:, 256:384],
            scale * jnp.concatenate(steps, 0),
            table((2, 2), 8) * rates,
            table((2, 2), 12),
            table((1, 2), 16),
        )

    if PLAIN:
        inside, *rest = add(grads, decay_rate)
    else:

        def fn(ins, outs):
            for ref, value in zip(outs, add(ins[0][...], ins[1][...])):
                ref[...] = value

        shapes = [(8, 128), (8, 128), (2, 8), (2, 2), (2, 2), (1, 2)]
        outs = [((8, 8, 256), BF16)] + [(shape, F32) for shape in shapes]
        inside, *rest = call(fn, outs, (grads, decay_rate), 1_000_000)
    return wide.at[:, 64:].set(inside), *rest


def add_parts(parts, scale):
    def add(pieces):
        total = jnp.sum(pieces.astype(F32), axis=0)
        blocks = [total[8 * (k // 2) + 32 * (k % 2) :][:8] for k in range(8)]
        return jnp.concatenate(blocks, 0).astype(BF16), scale * (total[64:, :128] + total[64:, 128:])

    if PLAIN:
        return add(parts)

    def fn(ins, outs):
        outs[0][...], outs[1][...] = add(ins[0][...])

    n = parts.shape[2]
    return call(fn, [((64, n), BF16), ((8, 128), F32)], (parts,), 1_000_000)


def exchange(array, axis):
    return lax.all_to_all(array, axis, 0, 0, tiled=True)


def body(
    tokens, out_grad, in_weight, dt_weight, bc_weight, out_weight, decay_rate, dt_bias, skip_gain
):
    seq_count = lax.axis_size(SEQ)
    tok_rows = tokens.shape[0]
    scale = (tok_rows * seq_count) ** (-0.5)
    own, rows, params = pack(
        tokens.T,
        out_grad.T,
        in_weight,
        bc_weight,
        out_weight.T,
        dt_weight.T,
        decay_rate,
        dt_bias,
        skip_gain.reshape(1, -1),
    )
    around = lax.axis_index("chan_1")
    order = jnp.stack(
        [2 * k + (around ^ e) for k in range(4) for e in range(2)] + [lax.axis_index(CORE)]
    ).astype(jnp.int32)
    other = lax.ppermute(own, "chan_1", SWAP)
    pair = jnp.concatenate([own, other], 0)
    parts = lax.all_gather(pair, "chan_0", axis=0, tiled=True)
    here = exchange(rows, ZY).reshape(-1, 512)
    there = lax.ppermute(here, CORE, SWAP)
    sums, pre, bc, cot, vec = project(order, parts, here, there, params)
    sums = exchange(sums.reshape(64, 8, 128), SEQ).reshape(512, 128)
    mixed, dgated, dbc, extra = within(pre, bc, cot, vec, params)
    back = exchange(carry(sums).reshape(64, 8, 128), SEQ).reshape(512, 128)
    wide, keep, give = finish(
        order, parts, here, there, params, pre, bc, cot, vec, mixed, dgated, dbc, extra, back
    )
    grads = join(keep, lax.ppermute(give, CORE, SWAP))
    grads = exchange(grads.reshape(32, 8, 512), ZY)
    wide, in_weight_grad, out_rows, dt_rows, rate_grad, bias_grad, skip_grad = add_rows(
        grads, wide, decay_rate, scale
    )
    tokens_grad, bc_weight_grad = add_parts(exchange(wide, CHAN), scale)
    tokens_grad = tokens_grad.T
    out_weight_grad = out_rows.T
    dt_weight_grad = dt_rows.T
    skip_grad = skip_grad.reshape(-1)
    return (
        tokens_grad,
        in_weight_grad,
        dt_weight_grad,
        bc_weight_grad,
        out_weight_grad,
        rate_grad,
        bias_grad,
        skip_grad,
    )


def solution(mesh):
    split = Mesh(
        mesh.devices.reshape(8, 4, 2, 4, 2), (*SEQ, *CHAN)
    )
    return jax.shard_map(
        body,
        mesh=split,
        in_specs=(
            P(SEQ, CHAN),
            P(SEQ, CHAN),
            P(SEQ, CHAN),
            P(SEQ, CHAN),
            P(SEQ, None),
            P(CHAN, SEQ),
            P(None, CHAN),
            P(None, CHAN),
            P(CHAN),
        ),
        out_specs=(
            P(SEQ, CHAN),
            P(SEQ, CHAN),
            P(SEQ, CHAN),
            P(SEQ, None),
            P(CHAN, SEQ),
            P(None, CHAN),
            P(None, CHAN),
            P(CHAN),
        ),
        check_vma=False,
    )
```

```python
import jax
import jax.numpy as jnp
from jax import lax
from jax.experimental import pallas as pl
from jax.experimental.pallas import tpu as pltpu
from jax.sharding import Mesh
from jax.sharding import PartitionSpec as P


STATE = 64
HEAD = 64
SEQ = ("seq_0", "seq_1", "seq_2")
ZY = ("seq_0", "seq_1")
CORE = "seq_2"
CHAN = ("chan_0", "chan_1")
NN = (((1,), (0,)), ((), ()))
NT = (((1,), (1,)), ((), ()))
TN = (((0,), (0,)), ((), ()))
F32 = jnp.float32
BF16 = jnp.bfloat16
INTERPRET = False


def low(x, y, dims):
    return lax.dot_general(x.astype(BF16), y.astype(BF16), dims, preferred_element_type=F32)


def halves(x):
    top = x.astype(BF16)
    return top, (x - top.astype(F32)).astype(BF16)


def mid(x, y, dims):
    xt, xl = halves(x)
    yt, yl = halves(y)
    return low(xt, yt, dims) + (low(xt, yl, dims) + low(xl, yt, dims))


def running(x):
    n = x.shape[1]
    top, rest = halves(x)
    low_ = (x - top.astype(F32) - rest.astype(F32)).astype(BF16)
    parts = jnp.concatenate([top.astype(F32), rest.astype(F32), low_.astype(F32)], 0)
    both = jnp.concatenate([before(n), before(n, True)], 1)
    sums = low(parts, both, NN)
    sums = sums[:8] + (sums[8:16] + sums[16:24])
    return sums[:, :n], sums[:, n:]


def before(n, flip=False):
    i = lax.broadcasted_iota(jnp.int32, (n, n), 0)
    j = lax.broadcasted_iota(jnp.int32, (n, n), 1)
    return (i >= j if flip else i <= j).astype(F32)


def by_head(x, r, width):
    n = x.shape[1]
    return jnp.concatenate(
        [
            jnp.broadcast_to(x[2 * r : 2 * r + 1], (width // 2, n)),
            jnp.broadcast_to(x[2 * r + 1 : 2 * r + 2], (width // 2, n)),
        ],
        0,
    )


def forward_rows(n):
    return lax.broadcasted_iota(jnp.int32, (8, n), 0) < 2


def sigmoid(x):
    return 1.0 / (1.0 + jnp.exp(-x))


def stage_project(u, q, weights, params):
    width = 128
    n = u.shape[1]
    pre = lax.dot_general(weights[:, :width], u, TN, preferred_element_type=F32)
    bc = lax.dot_general(weights[:, 128:256], u, TN, preferred_element_type=F32)
    cot = lax.dot_general(weights[:, 256:384], q, TN, preferred_element_type=F32)
    z = lax.dot_general(weights[:, 384:512], u, TN, preferred_element_type=F32)[:8]
    rate, bias = params[:, 0:1], params[:, 1:2]
    v = z + bias
    step = jnp.maximum(v, 0.0) + jnp.log1p(jnp.exp(-jnp.abs(v)))
    slope = sigmoid(v)
    decay = -rate * step
    from_start, from_end = running(decay)
    run = jnp.where(forward_rows(n), from_start, from_end)
    total = jnp.sum(decay, axis=1, keepdims=True)
    grown = jnp.exp(run)
    tail = jnp.exp(total - run)
    gated = pre * sigmoid(pre)
    b, c = bc[:STATE], bc[STATE:]
    push = step * tail
    pushed = jnp.concatenate([gated * by_head(push, r, width) for r in (0, 1)], 0)
    pulled = jnp.concatenate([cot * by_head(grown, r, width) for r in (0, 1)], 0)
    ps = mid(b, pushed, NT)
    pl_ = mid(c, pulled, NT)
    kept = jnp.broadcast_to(jnp.exp(total), (8, width))
    lane = lax.broadcasted_iota(jnp.int32, (1, width), 1)
    sends = [ps[:, :width], pl_[:, width:], pl_[:, :width], ps[:, width:]]
    tops = [part.astype(BF16).astype(F32) for part in sends]
    rests = [part - top for part, top in zip(sends, tops)]
    for k in range(4):
        top = kept[k : k + 1].astype(BF16).astype(F32)
        rests[3] = jnp.where(lane == 120 + 2 * k, top, rests[3])
        rests[3] = jnp.where(lane == 121 + 2 * k, kept[k : k + 1] - top, rests[3])
    sends = tops + rests
    vec = jnp.concatenate(
        [step, run, grown, tail, slope, jnp.broadcast_to(jnp.exp(total), (8, n))], 0
    )
    return sends, pre, bc, cot, vec


def stage_within(pre, bc, cot, vec, params):
    n = pre.shape[1]
    gated = pre * sigmoid(pre)
    b, c = bc[:STATE], bc[STATE:]
    step, run = vec[0:8], vec[8:16]
    columns = jnp.concatenate([run, jnp.zeros((120, n), F32)], 0).T
    t = lax.broadcasted_iota(jnp.int32, (n, n), 0)
    s = lax.broadcasted_iota(jnp.int32, (n, n), 1)
    later, same = t >= s, t == s
    earlier = t <= s
    scores = mid(c.T, b, NN)
    dscores = jnp.zeros((n, n), F32)
    mixed, dgated = ([], []), ([], [])
    lanes = lax.broadcasted_iota(jnp.int32, (n, 128), 1)
    rows = jnp.zeros((n, 128), F32)
    direct = [None] * 4
    for h in (0, 1):
        x = gated[HEAD * h : HEAD * (h + 1)]
        dy = cot[HEAD * h : HEAD * (h + 1)]
        step0, step1 = step[h : h + 1], step[2 + h : 3 + h]
        up = columns[:, h : h + 1] - run[h : h + 1]
        down = columns[:, 2 + h : 3 + h] - run[2 + h : 3 + h]
        fade = jnp.exp(jnp.where(later, up, down))
        pair = mid(dy.T, x, NN)
        faded = scores * fade
        moved = faded * pair
        scaled = fade * jnp.where(later, step0, step1) + jnp.where(same, step1, 0.0)
        dscores = dscores + scaled * pair
        for r, (mask, st) in enumerate(((later, step0), (earlier, step1))):
            part = jnp.where(mask, moved, 0.0)
            mix = jnp.where(mask, faded, 0.0) * st
            mixed[r].append(mid(x, mix, NT))
            dgated[r].append(mid(dy, mix, NN))
            direct[2 * r + h] = jnp.sum(part, axis=0, keepdims=True)
            rows = jnp.where(
                lanes == 2 * r + h, jnp.sum(part * st, axis=1, keepdims=True), rows
            )
    direct = jnp.concatenate(direct + [jnp.zeros((4, n), F32)], 0)
    drun = rows.T[:8] - step * direct
    gains = jnp.concatenate(
        [jnp.broadcast_to(params[h : h + 1, 2:3], (HEAD, n)) for h in (0, 1)], 0
    )
    mixed = jnp.concatenate([jnp.concatenate(m, 0) + gains * gated for m in mixed], 0)
    dgated = jnp.concatenate([jnp.concatenate(d, 0) + gains * cot for d in dgated], 0)
    both = gated * cot
    dskip = [
        2.0 * jnp.sum(both[HEAD * h : HEAD * (h + 1)], axis=0, keepdims=True) for h in (0, 1)
    ]
    dbc = jnp.concatenate([mid(c, dscores, NN), mid(b, dscores, NT)], 0)
    extra = jnp.concatenate([direct, drun] + dskip + [jnp.zeros((6, n), F32)], 0)
    return mixed, dgated, dbc, extra


def stage_finish(u, q, weights, params, pre, bc, cot, vec, mixed, dgated, dbc, extra, carried):
    width = 128
    n = pre.shape[1]
    sig = sigmoid(pre)
    gated = pre * sig
    b, c = bc[:STATE], bc[STATE:]
    step, grown, tail, slope = vec[0:8], vec[16:24], vec[24:32], vec[32:40]
    kept = vec[40:48, 0:1]
    rate = params[:, 0:1]
    h0, g1, g0, h1 = carried
    start = jnp.concatenate([h0, h1], 1)
    end = jnp.concatenate([g0, g1], 1)
    reach = mid(start.T, c, NN)
    pull = mid(end.T, b, NN)
    gains, falls, pushed, pulled = [], [], [], []
    dpre, lower = [], []
    bend = sig * (1.0 + pre * (1.0 - sig))
    for r in (0, 1):
        grow, tails, steps = (by_head(v, r, width) for v in (grown, tail, step))
        here = slice(width * r, width * (r + 1))
        got = reach[here] * grow
        lower.append((mixed[here] + got).astype(BF16))
        back = pull[here] * tails
        dpre.append(((dgated[here] + steps * back) * bend).astype(BF16))
        gain, fall = cot * got, gated * back
        for h in (0, 1):
            gains.append(jnp.sum(gain[HEAD * h : HEAD * (h + 1)], axis=0, keepdims=True))
            falls.append(jnp.sum(fall[HEAD * h : HEAD * (h + 1)], axis=0, keepdims=True))
        pulled.append(cot * grow)
        pushed.append(gated * steps * tails)
    none = [jnp.zeros((4, n), F32)]
    gains = jnp.concatenate(gains + none, 0)
    falls = jnp.concatenate(falls + none, 0)
    pulled = jnp.concatenate(pulled, 0)
    pushed = jnp.concatenate(pushed, 0)
    dbc = dbc + jnp.concatenate([mid(end, pushed, NN), mid(start, pulled, NN)], 0)
    lost = step * falls
    drun = extra[8:16] + gains - lost
    overlap = jnp.sum(start * end, axis=0, keepdims=True)
    lane = lax.broadcasted_iota(jnp.int32, (1, 2 * width), 1)
    ends = [
        jnp.sum(jnp.where(lane // HEAD == k, overlap, 0.0), axis=1, keepdims=True)
        for k in range(4)
    ]
    ends = jnp.concatenate(ends + [jnp.zeros((4, 1), F32)], 0)
    ends = kept * ends + jnp.sum(lost, axis=1, keepdims=True)
    from_start, from_end = running(drun)
    ddecay = ends + jnp.where(forward_rows(n), from_end, from_start)
    dstep = extra[0:8] + falls - rate * ddecay
    valid = lax.broadcasted_iota(jnp.int32, (8, n), 0) < 4
    dz = jnp.where(valid, dstep * slope, 0.0)
    drate = -jnp.sum(ddecay * step, axis=1, keepdims=True)
    dbias = jnp.sum(dz, axis=1, keepdims=True)
    dskip = jnp.sum(extra[16:24], axis=1, keepdims=True)
    dzs = jnp.concatenate([dz, jnp.zeros((120, n), F32)], 0).astype(BF16)
    dbcs = halves(dbc)
    front, inside = weights[:, :width], weights[:, 128:256]
    dinput = low(jnp.concatenate([front, front], 1), jnp.concatenate(dpre, 0), NN)
    dinput = dinput + low(
        jnp.concatenate([weights[:, 384:512]] + [inside] * len(dbcs), 1),
        jnp.concatenate([dzs, *dbcs], 0),
        NN,
    )
    dfront = low(u, jnp.concatenate(dpre, 0), NT)
    dfront = dfront[:, :width] + dfront[:, width:]
    rest = low(u, jnp.concatenate([dbcs[0], dzs], 0), NT)
    dinside = rest[:, :width] + low(u, dbcs[1], NT)
    dout = low(q, jnp.concatenate(lower, 0), NT)
    dout = dout[:, :width] + dout[:, width:]
    lane = lax.broadcasted_iota(jnp.int32, (1, width), 1)
    numbers = jnp.zeros((1, width), F32)
    for k in range(4):
        numbers = jnp.where(lane == 8 + k, drate[k : k + 1], numbers)
        numbers = jnp.where(lane == 12 + k, dbias[k : k + 1], numbers)
    for k in range(2):
        numbers = jnp.where(lane == 16 + k, dskip[k : k + 1], numbers)
    rough = numbers.astype(BF16).astype(F32)
    fine = rolled(jnp.broadcast_to(numbers - rough, (8, width)), 32)[:1]
    last = rest[:, width:] + jnp.broadcast_to(rough + fine, (u.shape[0], width))
    grads = jnp.concatenate([dfront, dinside, dout, last], 1)
    return dinput, grads


def rolled(x, by):
    return jnp.roll(x, by, 1) if PLAIN else pltpu.roll(x, by, 1)


PLAIN = False
SWAP = [(0, 1), (1, 0)]


def call(fn, outs, args, flops, scratch=(), scalars=0, grant=24 << 20):
    def kernel(*refs):
        k = len(args)
        fn(refs[:k], refs[k : k + len(outs)], *refs[k + len(outs) :])

    size = sum(a.size * a.dtype.itemsize for a in args)
    spaces = [pltpu.SMEM] * scalars + [pltpu.VMEM] * (len(args) - scalars)
    return pl.pallas_call(
        kernel,
        out_shape=[jax.ShapeDtypeStruct(s, d) for s, d in outs],
        in_specs=[pl.BlockSpec(memory_space=m) for m in spaces],
        scratch_shapes=list(scratch),
        cost_estimate=pl.CostEstimate(flops=flops, bytes_accessed=size, transcendentals=0),
        compiler_params=pltpu.CompilerParams(vmem_limit_bytes=grant),
        interpret=INTERPRET,
    )(*args)


def gathered(order, parts, own, other):
    if PLAIN:
        n = parts[0].shape[1]
        blocks = jnp.concatenate(parts, 0).reshape(8, 2, 2, 32, n)
        mine = order[8]
        u, q = (
            jnp.concatenate([blocks[:, k, mine], blocks[:, k, 1 - mine]], 0).reshape(512, n)
            for k in (0, 1)
        )
        halves_ = [w.reshape(8, 32, -1)[order[:8]] for w in (own, other)]
        return u, q, jnp.concatenate(halves_, 0).reshape(512, -1)
    mine = order[8] * 32
    up, down, rows = [], [], []
    for at, weights in ((mine, own), (32 - mine, other)):
        for k in range(8):
            part, base = parts[k // 2], 128 * (k % 2)
            up.append(part[pl.ds(pl.multiple_of(base + at, 32), 32), :])
            down.append(part[pl.ds(pl.multiple_of(base + 64 + at, 32), 32), :])
            rows.append(weights[pl.ds(pl.multiple_of(order[k] * 32, 32), 32), :])
    return jnp.concatenate(up, 0), jnp.concatenate(down, 0), jnp.concatenate(rows, 0)


def project(order, parts, own, other, params):
    if PLAIN:
        sends, *rest = stage_project(*gathered(order, parts, own, other), params)
        return (jnp.stack(sends, 1).reshape(512, 128).astype(BF16), *rest)

    def fn(ins, outs, lines):
        sends, *rest = stage_project(*gathered(ins[0], ins[1:5], *ins[5:7]), ins[7][...])
        for j, part in enumerate(sends):
            lines[pl.ds(j, STATE, stride=8), :] = part
        outs[0][...] = lines[...].astype(BF16)
        for ref, value in zip(outs[1:], rest):
            ref[...] = value

    n = parts[0].shape[1]
    outs = [((512, 128), BF16), ((128, n), F32), ((128, n), F32), ((128, n), F32), ((48, n), F32)]
    lines = pltpu.VMEM((512, 128), F32)
    return call(fn, outs, (order, *parts, own, other, params), 300_000_000, (lines,), 1)


def within(pre, bc, cot, vec, params):
    if PLAIN:
        return stage_within(pre, bc, cot, vec, params)

    def fn(ins, outs):
        for ref, value in zip(outs, stage_within(*(r[...] for r in ins))):
            ref[...] = value

    n = pre.shape[1]
    outs = [((256, n), F32), ((256, n), F32), ((128, n), F32), ((24, n), F32)]
    return call(fn, outs, (pre, bc, cot, vec, params), 300_000_000)


def finish(order, parts, own, other, params, pre, bc, cot, vec, mixed, dgated, dbc, extra, back):
    more = (params, pre, bc, cot, vec, mixed, dgated, dbc, extra)
    n = pre.shape[1]
    if PLAIN:
        rows = back.astype(F32).reshape(64, 8, 128)
        carried = [rows[:, j] + rows[:, 4 + j] for j in range(4)]
        dinput, grads = stage_finish(*gathered(order, parts, own, other), *more, carried)
        at, mine = order[:8], order[8]
        dinput = dinput.astype(BF16).reshape(2, 8, 32, n)
        dinput = jnp.where(mine == 0, dinput, dinput[::-1]).transpose(1, 0, 2, 3)
        wide = jnp.zeros((8, 72, n), BF16).at[at, :64].set(dinput.reshape(8, 64, n))
        grads = grads.reshape(2, 8, 32, 512)
        keep = jnp.zeros((8, 32, 512), F32).at[at].set(grads[0]).reshape(256, 512)
        give = jnp.zeros((8, 32, 512), F32).at[at].set(grads[1]).reshape(256, 512)
        return wide, keep, give.astype(BF16)

    def fn(ins, outs, lines):
        order = ins[0]
        lines[...] = ins[-1][...].astype(F32)
        carried = [
            lines[pl.ds(j, STATE, stride=8), :] + lines[pl.ds(4 + j, STATE, stride=8), :]
            for j in range(4)
        ]
        dinput, grads = stage_finish(
            *gathered(order, ins[1:5], *ins[5:7]), *(r[...] for r in ins[7:-1]), carried
        )
        dinput = dinput.astype(BF16)
        give = grads[256:].astype(BF16)
        mine = order[8] * 32
        for k in range(8):
            at = order[k]
            block = slice(32 * k, 32 * k + 32)
            rows = pl.ds(pl.multiple_of(at * 32, 32), 32)
            outs[0][at, pl.ds(pl.multiple_of(mine, 32), 32), :] = dinput[block]
            outs[0][at, pl.ds(pl.multiple_of(32 - mine, 32), 32), :] = dinput[256:][block]
            outs[0][at, 64:, :] = jnp.zeros((8, n), BF16)
            outs[1][rows, :] = grads[block]
            outs[2][rows, :] = give[block]

    outs = [((8, 72, n), BF16), ((256, 512), F32), ((256, 512), BF16)]
    lines = pltpu.VMEM((512, 128), F32)
    args = (order, *parts, own, other, *more, back)
    return call(fn, outs, args, 600_000_000, (lines,), 1)


def join(keep, got):
    def add(mine, theirs):
        total = mine + theirs.astype(F32)
        last = total[:, 384:]
        lane = lax.broadcasted_iota(jnp.int32, last.shape, 1)
        numbers = last + rolled(last, 96)
        rough = numbers.astype(BF16).astype(F32)
        fine = rolled(numbers - rough, 32)
        last = jnp.where(lane < 8, last, jnp.where(lane < 32, rough, fine))
        return jnp.concatenate([total[:, :384], last], 1).astype(BF16)

    if PLAIN:
        return add(keep, got)

    def fn(ins, outs):
        outs[0][...] = add(ins[0][...], ins[1][...])

    return call(fn, [(keep.shape, BF16)], (keep, got), 1_000_000)[0]


def carry(blocks):
    count = blocks.shape[0] // 8

    def unpack(take):
        lane = lax.broadcasted_iota(jnp.int32, (1, 128), 1)
        last = take(7)
        rests = [take(4), take(5), take(6), jnp.where(lane < 120, last, 0.0)]
        sums = [take(j) + rests[j] for j in range(4)]
        kept = [last[:, k : k + 1] + last[:, k + 1 : k + 2] for k in range(120, 128, 2)]
        return sums, [jnp.where(lane < HEAD, kept[2 * r], kept[2 * r + 1]) for r in (0, 1)]

    def scan(added, kept, keep):
        up = jnp.zeros((2, 128), F32)
        down = jnp.zeros((2, 128), F32)
        for k in range(count):
            m = count - 1 - k
            keep(k, up, m, down)
            up = kept[2 * k : 2 * k + 2, :] * up + added[4 * k : 4 * k + 2, :]
            down = kept[2 * m : 2 * m + 2, :] * down + added[4 * m + 2 : 4 * m + 4, :]

    if PLAIN:
        lines = blocks.astype(F32).reshape(count, 8, 128)
        sums, kept = unpack(lambda j: lines[:, j])
        ups, downs = [None] * count, [None] * count

        def keep(k, up, m, down):
            ups[k], downs[m] = up, down

        scan(jnp.stack(sums, 1).reshape(-1, 128), jnp.stack(kept, 1).reshape(-1, 128), keep)
        full = jnp.concatenate([jnp.stack(ups), jnp.stack(downs)], 1)
        top = full.astype(BF16)
        rest = (full - top.astype(F32)).astype(BF16)
        return jnp.concatenate([top, rest], 1).reshape(-1, 128)

    def fn(ins, outs, lines, added, factors, done):
        lines[...] = ins[0][...].astype(F32)
        sums, kept = unpack(lambda j: lines[pl.ds(j, count, stride=8), :])
        for j in range(4):
            added[pl.ds(j, count, stride=4), :] = sums[j]
        for r in (0, 1):
            factors[pl.ds(r, count, stride=2), :] = kept[r]

        def keep(k, up, m, down):
            done[8 * k : 8 * k + 2, :] = up
            done[8 * m + 2 : 8 * m + 4, :] = down

        scan(added, factors, keep)
        full = done[...]
        top = full.astype(BF16).astype(F32)
        rest = pltpu.roll(full - top, 4, 0)
        line = lax.broadcasted_iota(jnp.int32, full.shape, 0)
        outs[0][...] = jnp.where(line % 8 < 4, top, rest).astype(BF16)

    scratch = [pltpu.VMEM((rows * count, 128), F32) for rows in (8, 4, 2, 8)]
    return call(fn, [((8 * count, 128), BF16)], (blocks,), 1_000_000, scratch)[0]


def pack(*args):
    def fill(tok, cot, inw, bcw, outw, dtw, rates, biases, gains):
        blocks = []
        for x in (tok.astype(F32), cot.astype(F32)):
            for odd in (0, 8):
                blocks += [x[k + odd : k + odd + 8] for k in range(0, 64, 16)]
        lane = lax.broadcasted_iota(jnp.int32, (8, 128), 1)
        square = lax.broadcasted_iota(jnp.int32, (8, 8), 0) == lax.broadcasted_iota(
            jnp.int32, (8, 8), 1
        )
        last = jnp.zeros((8, 128), F32)
        for k in range(4):
            row = jnp.broadcast_to(dtw[k % 2 : k % 2 + 1].astype(F32), (8, 8))
            column = jnp.sum(jnp.where(square, row, 0.0), axis=1, keepdims=True)
            last = jnp.where(lane == k, column, last)
        rows = jnp.concatenate([inw, bcw, outw, last.astype(BF16)], 1)
        sub = lax.broadcasted_iota(jnp.int32, (8, 128), 0)
        table = jnp.zeros((8, 128), F32)
        for k in range(4):
            r, h = k // 2, k % 2
            values = (rates[r : r + 1, h : h + 1], biases[r : r + 1, h : h + 1], gains[:, h : h + 1])
            for at, value in enumerate(values):
                table = jnp.where((sub == k) & (lane == at), value, table)
        return (
            jnp.concatenate(blocks, 0).astype(BF16),
            jnp.broadcast_to(rows[None], (32, 8, 512)),
            table,
        )

    if PLAIN:
        return fill(*args)

    def fn(ins, outs):
        for ref, value in zip(outs, fill(*(r[...] for r in ins))):
            ref[...] = value

    outs = [((128, args[0].shape[1]), BF16), ((32, 8, 512), BF16), ((8, 128), F32)]
    return call(fn, outs, args, 1_000_000, grant=None)


def add_rows(grads, wide, decay_rate, scale):
    def add(pieces, rates):
        total = jnp.sum(pieces.astype(F32), axis=0)
        inside = jnp.concatenate(halves(total[:, 128:256]), 1)
        last = total[:, 384:512]
        numbers = scale * (last + rolled(last, 96))[:1]
        lane = lax.broadcasted_iota(jnp.int32, (1, 128), 1)

        def pick(k):
            return jnp.sum(jnp.where(lane == k, numbers, 0.0), axis=1, keepdims=True)

        def table(shape, at):
            i = lax.broadcasted_iota(jnp.int32, shape, 0)
            j = lax.broadcasted_iota(jnp.int32, shape, 1)
            out = jnp.zeros(shape, F32)
            for k in range(shape[0] * shape[1]):
                out = jnp.where(i * shape[1] + j == k, pick(at + k), out)
            return out

        square = lax.broadcasted_iota(jnp.int32, (8, 8), 0) == lax.broadcasted_iota(
            jnp.int32, (8, 8), 1
        )
        steps = [
            jnp.sum(
                jnp.where(square, last[:, k : k + 1] + last[:, k + 2 : k + 3], 0.0),
                axis=0,
                keepdims=True,
            )
            for k in (0, 1)
        ]
        return (
            jnp.broadcast_to(inside[None], (8, *inside.shape)),
            scale * total[:, :128],
            scale * total[:, 256:384],
            scale * jnp.concatenate(steps, 0),
            table((2, 2), 8) * rates,
            table((2, 2), 12),
            table((1, 2), 16),
        )

    if PLAIN:
        inside, *rest = add(grads, decay_rate)
    else:

        def fn(ins, outs):
            for ref, value in zip(outs, add(ins[0][...], ins[1][...])):
                ref[...] = value

        shapes = [(8, 128), (8, 128), (2, 8), (2, 2), (2, 2), (1, 2)]
        outs = [((8, 8, 256), BF16)] + [(shape, F32) for shape in shapes]
        inside, *rest = call(fn, outs, (grads, decay_rate), 1_000_000)
    return wide.at[:, 64:].set(inside), *rest


def add_parts(parts, scale):
    def add(pieces):
        total = jnp.sum(pieces.astype(F32), axis=0)
        blocks = [total[8 * (k // 2) + 32 * (k % 2) :][:8] for k in range(8)]
        return jnp.concatenate(blocks, 0).astype(BF16), scale * (total[64:, :128] + total[64:, 128:])

    if PLAIN:
        return add(parts)

    def fn(ins, outs):
        outs[0][...], outs[1][...] = add(ins[0][...])

    n = parts.shape[2]
    return call(fn, [((64, n), BF16), ((8, 128), F32)], (parts,), 1_000_000)


def exchange(array, axis):
    return lax.all_to_all(array, axis, 0, 0, tiled=True)


def body(
    tokens, out_grad, in_weight, dt_weight, bc_weight, out_weight, decay_rate, dt_bias, skip_gain
):
    seq_count = lax.axis_size(SEQ)
    tok_rows = tokens.shape[0]
    scale = (tok_rows * seq_count) ** (-0.5)
    own, rows, params = pack(
        tokens.T,
        out_grad.T,
        in_weight,
        bc_weight,
        out_weight.T,
        dt_weight.T,
        decay_rate,
        dt_bias,
        skip_gain.reshape(1, -1),
    )
    other = lax.ppermute(own, "chan_1", SWAP)
    pair = jnp.concatenate([own, other], 0)
    parts = [pair] + [
        lax.ppermute(pair, "chan_0", [(k, (k + d) % 4) for k in range(4)])
        for d in (1, 2, 3)
    ]
    here = exchange(rows, ZY).reshape(-1, 512)
    there = lax.ppermute(here, CORE, SWAP)
    across, around = lax.axis_index("chan_0"), lax.axis_index("chan_1")
    order = jnp.stack(
        [(across - d) % 4 * 2 + (around ^ e) for d in range(4) for e in range(2)]
        + [lax.axis_index(CORE)]
    ).astype(jnp.int32)
    sums, pre, bc, cot, vec = project(order, parts, here, there, params)
    sums = exchange(sums.reshape(64, 8, 128), SEQ).reshape(512, 128)
    mixed, dgated, dbc, extra = within(pre, bc, cot, vec, params)
    back = exchange(carry(sums).reshape(64, 8, 128), SEQ).reshape(512, 128)
    wide, keep, give = finish(
        order, parts, here, there, params, pre, bc, cot, vec, mixed, dgated, dbc, extra, back
    )
    grads = join(keep, lax.ppermute(give, CORE, SWAP))
    grads = exchange(grads.reshape(32, 8, 512), ZY)
    wide, in_weight_grad, out_rows, dt_rows, rate_grad, bias_grad, skip_grad = add_rows(
        grads, wide, decay_rate, scale
    )
    tokens_grad, bc_weight_grad = add_parts(exchange(wide, CHAN), scale)
    tokens_grad = tokens_grad.T
    out_weight_grad = out_rows.T
    dt_weight_grad = dt_rows.T
    skip_grad = skip_grad.reshape(-1)
    return (
        tokens_grad,
        in_weight_grad,
        dt_weight_grad,
        bc_weight_grad,
        out_weight_grad,
        rate_grad,
        bias_grad,
        skip_grad,
    )


def solution(mesh):
    split = Mesh(
        mesh.devices.reshape(8, 4, 2, 4, 2), (*SEQ, *CHAN)
    )
    return jax.shard_map(
        body,
        mesh=split,
        in_specs=(
            P(SEQ, CHAN),
            P(SEQ, CHAN),
            P(SEQ, CHAN),
            P(SEQ, CHAN),
            P(SEQ, None),
            P(CHAN, SEQ),
            P(None, CHAN),
            P(None, CHAN),
            P(CHAN),
        ),
        out_specs=(
            P(SEQ, CHAN),
            P(SEQ, CHAN),
            P(SEQ, CHAN),
            P(SEQ, None),
            P(CHAN, SEQ),
            P(None, CHAN),
            P(None, CHAN),
            P(CHAN),
        ),
        check_vma=False,
    )
```

```python
import jax
import jax.numpy as jnp
from jax import lax
from jax.experimental import pallas as pl
from jax.experimental.pallas import tpu as pltpu
from jax.sharding import Mesh
from jax.sharding import PartitionSpec as P


STATE = 64
HEAD = 64
SEQ = ("seq_0", "seq_1", "seq_2")
ZY = ("seq_0", "seq_1")
CORE = "seq_2"
CHAN = ("chan_0", "chan_1")
NN = (((1,), (0,)), ((), ()))
NT = (((1,), (1,)), ((), ()))
TN = (((0,), (0,)), ((), ()))
F32 = jnp.float32
BF16 = jnp.bfloat16
INTERPRET = False


def low(x, y, dims):
    return lax.dot_general(x.astype(BF16), y.astype(BF16), dims, preferred_element_type=F32)


def halves(x):
    top = x.astype(BF16)
    return top, (x - top.astype(F32)).astype(BF16)


def mid(x, y, dims):
    xt, xl = halves(x)
    yt, yl = halves(y)
    return low(xt, yt, dims) + (low(xt, yl, dims) + low(xl, yt, dims))


def running(x):
    n = x.shape[1]
    top, rest = halves(x)
    low_ = (x - top.astype(F32) - rest.astype(F32)).astype(BF16)
    parts = jnp.concatenate([top.astype(F32), rest.astype(F32), low_.astype(F32)], 0)
    both = jnp.concatenate([before(n), before(n, True)], 1)
    sums = low(parts, both, NN)
    sums = sums[:8] + (sums[8:16] + sums[16:24])
    return sums[:, :n], sums[:, n:]


def before(n, flip=False):
    i = lax.broadcasted_iota(jnp.int32, (n, n), 0)
    j = lax.broadcasted_iota(jnp.int32, (n, n), 1)
    return (i >= j if flip else i <= j).astype(F32)


def by_head(x, r, width):
    n = x.shape[1]
    return jnp.concatenate(
        [
            jnp.broadcast_to(x[2 * r : 2 * r + 1], (width // 2, n)),
            jnp.broadcast_to(x[2 * r + 1 : 2 * r + 2], (width // 2, n)),
        ],
        0,
    )


def forward_rows(n):
    return lax.broadcasted_iota(jnp.int32, (8, n), 0) < 2


def sigmoid(x):
    return 1.0 / (1.0 + jnp.exp(-x))


def stage_project(u, q, weights, params):
    width = 128
    n = u.shape[1]
    pre = lax.dot_general(weights[:, :width], u, TN, preferred_element_type=F32)
    bc = lax.dot_general(weights[:, 128:256], u, TN, preferred_element_type=F32)
    cot = lax.dot_general(weights[:, 256:384], q, TN, preferred_element_type=F32)
    z = lax.dot_general(weights[:, 384:512], u, TN, preferred_element_type=F32)[:8]
    rate, bias = params[:, 0:1], params[:, 1:2]
    v = z + bias
    step = jnp.maximum(v, 0.0) + jnp.log1p(jnp.exp(-jnp.abs(v)))
    slope = sigmoid(v)
    decay = -rate * step
    from_start, from_end = running(decay)
    run = jnp.where(forward_rows(n), from_start, from_end)
    total = jnp.sum(decay, axis=1, keepdims=True)
    grown = jnp.exp(run)
    tail = jnp.exp(total - run)
    gated = pre * sigmoid(pre)
    b, c = bc[:STATE], bc[STATE:]
    push = step * tail
    pushed = jnp.concatenate([gated * by_head(push, r, width) for r in (0, 1)], 0)
    pulled = jnp.concatenate([cot * by_head(grown, r, width) for r in (0, 1)], 0)
    ps = mid(b, pushed, NT)
    pl_ = mid(c, pulled, NT)
    kept = jnp.broadcast_to(jnp.exp(total), (8, width))
    lane = lax.broadcasted_iota(jnp.int32, (1, width), 1)
    sends = [ps[:, :width], pl_[:, width:], pl_[:, :width], ps[:, width:]]
    tops = [part.astype(BF16).astype(F32) for part in sends]
    rests = [part - top for part, top in zip(sends, tops)]
    for k in range(4):
        top = kept[k : k + 1].astype(BF16).astype(F32)
        rests[3] = jnp.where(lane == 120 + 2 * k, top, rests[3])
        rests[3] = jnp.where(lane == 121 + 2 * k, kept[k : k + 1] - top, rests[3])
    sends = tops + rests
    vec = jnp.concatenate(
        [step, run, grown, tail, slope, jnp.broadcast_to(jnp.exp(total), (8, n))], 0
    )
    return sends, pre, bc, cot, vec


def stage_within(pre, bc, cot, vec, params):
    n = pre.shape[1]
    gated = pre * sigmoid(pre)
    b, c = bc[:STATE], bc[STATE:]
    step, run = vec[0:8], vec[8:16]
    columns = jnp.concatenate([run, jnp.zeros((120, n), F32)], 0).T
    t = lax.broadcasted_iota(jnp.int32, (n, n), 0)
    s = lax.broadcasted_iota(jnp.int32, (n, n), 1)
    later, same = t >= s, t == s
    earlier = t <= s
    scores = mid(c.T, b, NN)
    dscores = jnp.zeros((n, n), F32)
    mixed, dgated = ([], []), ([], [])
    lanes = lax.broadcasted_iota(jnp.int32, (n, 128), 1)
    rows = jnp.zeros((n, 128), F32)
    direct = [None] * 4
    for h in (0, 1):
        x = gated[HEAD * h : HEAD * (h + 1)]
        dy = cot[HEAD * h : HEAD * (h + 1)]
        step0, step1 = step[h : h + 1], step[2 + h : 3 + h]
        up = columns[:, h : h + 1] - run[h : h + 1]
        down = columns[:, 2 + h : 3 + h] - run[2 + h : 3 + h]
        fade = jnp.exp(jnp.where(later, up, down))
        pair = mid(dy.T, x, NN)
        faded = scores * fade
        moved = faded * pair
        scaled = fade * jnp.where(later, step0, step1) + jnp.where(same, step1, 0.0)
        dscores = dscores + scaled * pair
        for r, (mask, st) in enumerate(((later, step0), (earlier, step1))):
            part = jnp.where(mask, moved, 0.0)
            mix = jnp.where(mask, faded, 0.0) * st
            mixed[r].append(mid(x, mix, NT))
            dgated[r].append(mid(dy, mix, NN))
            direct[2 * r + h] = jnp.sum(part, axis=0, keepdims=True)
            rows = jnp.where(
                lanes == 2 * r + h, jnp.sum(part * st, axis=1, keepdims=True), rows
            )
    direct = jnp.concatenate(direct + [jnp.zeros((4, n), F32)], 0)
    drun = rows.T[:8] - step * direct
    gains = jnp.concatenate(
        [jnp.broadcast_to(params[h : h + 1, 2:3], (HEAD, n)) for h in (0, 1)], 0
    )
    mixed = jnp.concatenate([jnp.concatenate(m, 0) + gains * gated for m in mixed], 0)
    dgated = jnp.concatenate([jnp.concatenate(d, 0) + gains * cot for d in dgated], 0)
    both = gated * cot
    dskip = [
        2.0 * jnp.sum(both[HEAD * h : HEAD * (h + 1)], axis=0, keepdims=True) for h in (0, 1)
    ]
    dbc = jnp.concatenate([mid(c, dscores, NN), mid(b, dscores, NT)], 0)
    extra = jnp.concatenate([direct, drun] + dskip + [jnp.zeros((6, n), F32)], 0)
    return mixed, dgated, dbc, extra


def stage_finish(params, pre, bc, cot, vec, mixed, dgated, dbc, extra, carried):
    width = 128
    n = pre.shape[1]
    sig = sigmoid(pre)
    gated = pre * sig
    b, c = bc[:STATE], bc[STATE:]
    step, grown, tail, slope = vec[0:8], vec[16:24], vec[24:32], vec[32:40]
    kept = vec[40:48, 0:1]
    rate = params[:, 0:1]
    h0, g1, g0, h1 = carried
    start = jnp.concatenate([h0, h1], 1)
    end = jnp.concatenate([g0, g1], 1)
    reach = mid(start.T, c, NN)
    pull = mid(end.T, b, NN)
    gains, falls, pushed, pulled = [], [], [], []
    dpre, lower = [], []
    bend = sig * (1.0 + pre * (1.0 - sig))
    for r in (0, 1):
        grow, tails, steps = (by_head(v, r, width) for v in (grown, tail, step))
        here = slice(width * r, width * (r + 1))
        got = reach[here] * grow
        lower.append((mixed[here] + got).astype(BF16))
        back = pull[here] * tails
        dpre.append(((dgated[here] + steps * back) * bend).astype(BF16))
        gain, fall = cot * got, gated * back
        for h in (0, 1):
            gains.append(jnp.sum(gain[HEAD * h : HEAD * (h + 1)], axis=0, keepdims=True))
            falls.append(jnp.sum(fall[HEAD * h : HEAD * (h + 1)], axis=0, keepdims=True))
        pulled.append(cot * grow)
        pushed.append(gated * steps * tails)
    none = [jnp.zeros((4, n), F32)]
    gains = jnp.concatenate(gains + none, 0)
    falls = jnp.concatenate(falls + none, 0)
    pulled = jnp.concatenate(pulled, 0)
    pushed = jnp.concatenate(pushed, 0)
    dbc = dbc + jnp.concatenate([mid(end, pushed, NN), mid(start, pulled, NN)], 0)
    lost = step * falls
    drun = extra[8:16] + gains - lost
    overlap = jnp.sum(start * end, axis=0, keepdims=True)
    lane = lax.broadcasted_iota(jnp.int32, (1, 2 * width), 1)
    ends = [
        jnp.sum(jnp.where(lane // HEAD == k, overlap, 0.0), axis=1, keepdims=True)
        for k in range(4)
    ]
    ends = jnp.concatenate(ends + [jnp.zeros((4, 1), F32)], 0)
    ends = kept * ends + jnp.sum(lost, axis=1, keepdims=True)
    from_start, from_end = running(drun)
    ddecay = ends + jnp.where(forward_rows(n), from_end, from_start)
    dstep = extra[0:8] + falls - rate * ddecay
    valid = lax.broadcasted_iota(jnp.int32, (8, n), 0) < 4
    dz = jnp.where(valid, dstep * slope, 0.0)
    drate = -jnp.sum(ddecay * step, axis=1, keepdims=True)
    dbias = jnp.sum(dz, axis=1, keepdims=True)
    dskip = jnp.sum(extra[16:24], axis=1, keepdims=True)
    dzs = jnp.concatenate([dz, jnp.zeros((120, n), F32)], 0).astype(BF16)
    lane = lax.broadcasted_iota(jnp.int32, (1, width), 1)
    numbers = jnp.zeros((1, width), F32)
    for k in range(4):
        numbers = jnp.where(lane == 8 + k, drate[k : k + 1], numbers)
        numbers = jnp.where(lane == 12 + k, dbias[k : k + 1], numbers)
    for k in range(2):
        numbers = jnp.where(lane == 16 + k, dskip[k : k + 1], numbers)
    rough = numbers.astype(BF16).astype(F32)
    fine = rolled(jnp.broadcast_to(numbers - rough, (8, width)), 32)[:1]
    numbers = jnp.broadcast_to(rough + fine, (8, width))
    front = jnp.concatenate([*dpre, *halves(dbc), dzs], 0)
    return front, jnp.concatenate(lower, 0), numbers


def stage_outer(u, q, front, lower, numbers):
    width = 128
    dfront = low(u, front[: 2 * width], NT)
    dinside = low(u, front[2 * width : 4 * width], NT)
    dstep = low(u, front[4 * width :], NT)
    dout = low(q, lower, NT)
    return jnp.concatenate(
        [
            dfront[:, :width] + dfront[:, width:],
            dinside[:, :width] + dinside[:, width:],
            dout[:, :width] + dout[:, width:],
            dstep + jnp.broadcast_to(numbers[:1], (u.shape[0], width)),
        ],
        1,
    )


def stage_input(weights, front):
    outer, inside = weights[:, :128], weights[:, 128:256]
    return low(jnp.concatenate([outer, outer], 1), front[:256], NN) + low(
        jnp.concatenate([inside, inside, weights[:, 384:]], 1), front[256:], NN
    )


def rolled(x, by):
    return jnp.roll(x, by, 1) if PLAIN else pltpu.roll(x, by, 1)


PLAIN = False
SWAP = [(0, 1), (1, 0)]


def call(fn, outs, args, flops, scratch=(), scalars=0, grant=24 << 20):
    def kernel(*refs):
        k = len(args)
        fn(refs[:k], refs[k : k + len(outs)], *refs[k + len(outs) :])

    size = sum(a.size * a.dtype.itemsize for a in args)
    spaces = [pltpu.SMEM] * scalars + [pltpu.VMEM] * (len(args) - scalars)
    return pl.pallas_call(
        kernel,
        out_shape=[jax.ShapeDtypeStruct(s, d) for s, d in outs],
        in_specs=[pl.BlockSpec(memory_space=m) for m in spaces],
        scratch_shapes=list(scratch),
        cost_estimate=pl.CostEstimate(flops=flops, bytes_accessed=size, transcendentals=0),
        compiler_params=pltpu.CompilerParams(vmem_limit_bytes=grant),
        interpret=INTERPRET,
    )(*args)


def features(order, parts, partner):
    if PLAIN:
        n = parts[0].shape[1]
        blocks = jnp.concatenate(parts, 0).reshape(8, 2, 2, 32, n)
        side = 1 - order[8] if partner else order[8]
        return tuple(blocks[:, k, side].reshape(256, n) for k in (0, 1))
    at = (1 - order[8]) * 32 if partner else order[8] * 32
    up, down = [], []
    for k in range(8):
        part, base = parts[k // 2], 128 * (k % 2)
        up.append(part[pl.ds(pl.multiple_of(base + at, 32), 32), :])
        down.append(part[pl.ds(pl.multiple_of(base + 64 + at, 32), 32), :])
    return jnp.concatenate(up, 0), jnp.concatenate(down, 0)


def matching(order, weights):
    if PLAIN:
        return weights.reshape(8, 32, -1)[order[:8]].reshape(256, -1)
    rows = [weights[pl.ds(pl.multiple_of(order[k] * 32, 32), 32), :] for k in range(8)]
    return jnp.concatenate(rows, 0)


def gathered(order, parts, own, other):
    first, second = features(order, parts, False), features(order, parts, True)
    u, q = (jnp.concatenate(pair, 0) for pair in zip(first, second))
    return u, q, jnp.concatenate([matching(order, own), matching(order, other)], 0)


def project(order, parts, own, other, params):
    if PLAIN:
        sends, *rest = stage_project(*gathered(order, parts, own, other), params)
        return (jnp.stack(sends, 1).reshape(512, 128).astype(BF16), *rest)

    def fn(ins, outs, lines):
        sends, *rest = stage_project(*gathered(ins[0], ins[1:5], *ins[5:7]), ins[7][...])
        for j, part in enumerate(sends):
            lines[pl.ds(j, STATE, stride=8), :] = part
        outs[0][...] = lines[...].astype(BF16)
        for ref, value in zip(outs[1:], rest):
            ref[...] = value

    n = parts[0].shape[1]
    outs = [((512, 128), BF16), ((128, n), F32), ((128, n), F32), ((128, n), F32), ((48, n), F32)]
    lines = pltpu.VMEM((512, 128), F32)
    return call(fn, outs, (order, *parts, own, other, params), 300_000_000, (lines,), 1)


def within(pre, bc, cot, vec, params):
    if PLAIN:
        return stage_within(pre, bc, cot, vec, params)

    def fn(ins, outs):
        for ref, value in zip(outs, stage_within(*(r[...] for r in ins))):
            ref[...] = value

    n = pre.shape[1]
    outs = [((256, n), F32), ((256, n), F32), ((128, n), F32), ((24, n), F32)]
    return call(fn, outs, (pre, bc, cot, vec, params), 300_000_000)


def finish(order, parts, params, pre, bc, cot, vec, mixed, dgated, dbc, extra, back):
    more = (params, pre, bc, cot, vec, mixed, dgated, dbc, extra)
    n = pre.shape[1]
    if PLAIN:
        rows = back.astype(F32).reshape(64, 8, 128)
        carried = [rows[:, j] + rows[:, 4 + j] for j in range(4)]
        results = stage_finish(*more, carried)
        grads = stage_outer(*features(order, parts, True), *results).reshape(8, 32, 512)
        give = jnp.zeros((8, 32, 512), F32).at[order[:8]].set(grads).reshape(256, 512)
        return give.astype(BF16), *results

    def fn(ins, outs, lines):
        order = ins[0]
        lines[...] = ins[-1][...].astype(F32)
        carried = [
            lines[pl.ds(j, STATE, stride=8), :] + lines[pl.ds(4 + j, STATE, stride=8), :]
            for j in range(4)
        ]
        results = stage_finish(*(r[...] for r in ins[5:-1]), carried)
        grads = stage_outer(*features(order, ins[1:5], True), *results).astype(BF16)
        for k in range(8):
            rows = pl.ds(pl.multiple_of(order[k] * 32, 32), 32)
            outs[0][rows, :] = grads[32 * k : 32 * k + 32]
        for ref, value in zip(outs[1:], results):
            ref[...] = value

    outs = [((256, 512), BF16), ((640, n), BF16), ((256, n), BF16), ((8, 128), F32)]
    lines = pltpu.VMEM((512, 128), F32)
    return call(fn, outs, (order, *parts, *more, back), 400_000_000, (lines,), 1)


def finish_own(order, parts, own, other, front, lower, numbers):
    n = front.shape[1]
    if PLAIN:
        at, mine = order[:8], order[8]
        weights = jnp.concatenate([matching(order, own), matching(order, other)], 0)
        dinput = stage_input(weights, front).astype(BF16).reshape(2, 8, 32, n)
        dinput = jnp.where(mine == 0, dinput, dinput[::-1]).transpose(1, 0, 2, 3)
        wide = jnp.zeros((8, 72, n), BF16).at[at, :64].set(dinput.reshape(8, 64, n))
        grads = stage_outer(*features(order, parts, False), front, lower, numbers)
        keep = jnp.zeros((8, 32, 512), F32).at[at].set(grads.reshape(8, 32, 512))
        return wide, keep.reshape(256, 512)

    def fn(ins, outs):
        order = ins[0]
        front, lower, numbers = (r[...] for r in ins[7:])
        weights = jnp.concatenate([matching(order, ins[5]), matching(order, ins[6])], 0)
        dinput = stage_input(weights, front).astype(BF16)
        grads = stage_outer(*features(order, ins[1:5], False), front, lower, numbers)
        mine = order[8] * 32
        for k in range(8):
            at = order[k]
            block = slice(32 * k, 32 * k + 32)
            outs[0][at, pl.ds(pl.multiple_of(mine, 32), 32), :] = dinput[block]
            outs[0][at, pl.ds(pl.multiple_of(32 - mine, 32), 32), :] = dinput[256:][block]
            outs[0][at, 64:, :] = jnp.zeros((8, n), BF16)
            outs[1][pl.ds(pl.multiple_of(at * 32, 32), 32), :] = grads[block]

    outs = [((8, 72, n), BF16), ((256, 512), F32)]
    args = (order, *parts, own, other, front, lower, numbers)
    return call(fn, outs, args, 400_000_000, (), 1)


def join(keep, got):
    def add(mine, theirs):
        total = mine + theirs.astype(F32)
        last = total[:, 384:]
        lane = lax.broadcasted_iota(jnp.int32, last.shape, 1)
        numbers = last + rolled(last, 96)
        rough = numbers.astype(BF16).astype(F32)
        fine = rolled(numbers - rough, 32)
        last = jnp.where(lane < 8, last, jnp.where(lane < 32, rough, fine))
        return jnp.concatenate([total[:, :384], last], 1).astype(BF16)

    if PLAIN:
        return add(keep, got)

    def fn(ins, outs):
        outs[0][...] = add(ins[0][...], ins[1][...])

    return call(fn, [(keep.shape, BF16)], (keep, got), 1_000_000)[0]


def carry(blocks):
    count = blocks.shape[0] // 8

    def unpack(take):
        lane = lax.broadcasted_iota(jnp.int32, (1, 128), 1)
        last = take(7)
        rests = [take(4), take(5), take(6), jnp.where(lane < 120, last, 0.0)]
        sums = [take(j) + rests[j] for j in range(4)]
        kept = [last[:, k : k + 1] + last[:, k + 1 : k + 2] for k in range(120, 128, 2)]
        return sums, [jnp.where(lane < HEAD, kept[2 * r], kept[2 * r + 1]) for r in (0, 1)]

    def scan(added, kept, keep):
        up = jnp.zeros((2, 128), F32)
        down = jnp.zeros((2, 128), F32)
        for k in range(count):
            m = count - 1 - k
            keep(k, up, m, down)
            up = kept[2 * k : 2 * k + 2, :] * up + added[4 * k : 4 * k + 2, :]
            down = kept[2 * m : 2 * m + 2, :] * down + added[4 * m + 2 : 4 * m + 4, :]

    if PLAIN:
        lines = blocks.astype(F32).reshape(count, 8, 128)
        sums, kept = unpack(lambda j: lines[:, j])
        ups, downs = [None] * count, [None] * count

        def keep(k, up, m, down):
            ups[k], downs[m] = up, down

        scan(jnp.stack(sums, 1).reshape(-1, 128), jnp.stack(kept, 1).reshape(-1, 128), keep)
        full = jnp.concatenate([jnp.stack(ups), jnp.stack(downs)], 1)
        top = full.astype(BF16)
        rest = (full - top.astype(F32)).astype(BF16)
        return jnp.concatenate([top, rest], 1).reshape(-1, 128)

    def fn(ins, outs, lines, added, factors, done):
        lines[...] = ins[0][...].astype(F32)
        sums, kept = unpack(lambda j: lines[pl.ds(j, count, stride=8), :])
        for j in range(4):
            added[pl.ds(j, count, stride=4), :] = sums[j]
        for r in (0, 1):
            factors[pl.ds(r, count, stride=2), :] = kept[r]

        def keep(k, up, m, down):
            done[8 * k : 8 * k + 2, :] = up
            done[8 * m + 2 : 8 * m + 4, :] = down

        scan(added, factors, keep)
        full = done[...]
        top = full.astype(BF16).astype(F32)
        rest = pltpu.roll(full - top, 4, 0)
        line = lax.broadcasted_iota(jnp.int32, full.shape, 0)
        outs[0][...] = jnp.where(line % 8 < 4, top, rest).astype(BF16)

    scratch = [pltpu.VMEM((rows * count, 128), F32) for rows in (8, 4, 2, 8)]
    return call(fn, [((8 * count, 128), BF16)], (blocks,), 1_000_000, scratch)[0]


def pack(*args):
    def fill(tok, cot, inw, bcw, outw, dtw, rates, biases, gains):
        blocks = []
        for x in (tok.astype(F32), cot.astype(F32)):
            for odd in (0, 8):
                blocks += [x[k + odd : k + odd + 8] for k in range(0, 64, 16)]
        lane = lax.broadcasted_iota(jnp.int32, (8, 128), 1)
        square = lax.broadcasted_iota(jnp.int32, (8, 8), 0) == lax.broadcasted_iota(
            jnp.int32, (8, 8), 1
        )
        last = jnp.zeros((8, 128), F32)
        for k in range(4):
            row = jnp.broadcast_to(dtw[k % 2 : k % 2 + 1].astype(F32), (8, 8))
            column = jnp.sum(jnp.where(square, row, 0.0), axis=1, keepdims=True)
            last = jnp.where(lane == k, column, last)
        rows = jnp.concatenate([inw, bcw, outw, last.astype(BF16)], 1)
        sub = lax.broadcasted_iota(jnp.int32, (8, 128), 0)
        table = jnp.zeros((8, 128), F32)
        for k in range(4):
            r, h = k // 2, k % 2
            values = (rates[r : r + 1, h : h + 1], biases[r : r + 1, h : h + 1], gains[:, h : h + 1])
            for at, value in enumerate(values):
                table = jnp.where((sub == k) & (lane == at), value, table)
        return (
            jnp.concatenate(blocks, 0).astype(BF16),
            jnp.broadcast_to(rows[None], (32, 8, 512)),
            table,
        )

    if PLAIN:
        return fill(*args)

    def fn(ins, outs):
        for ref, value in zip(outs, fill(*(r[...] for r in ins))):
            ref[...] = value

    outs = [((128, args[0].shape[1]), BF16), ((32, 8, 512), BF16), ((8, 128), F32)]
    return call(fn, outs, args, 1_000_000, grant=None)


def add_rows(grads, wide, decay_rate, scale):
    def add(pieces, rates):
        total = jnp.sum(pieces.astype(F32), axis=0)
        inside = jnp.concatenate(halves(total[:, 128:256]), 1)
        last = total[:, 384:512]
        numbers = scale * (last + rolled(last, 96))[:1]
        lane = lax.broadcasted_iota(jnp.int32, (1, 128), 1)

        def pick(k):
            return jnp.sum(jnp.where(lane == k, numbers, 0.0), axis=1, keepdims=True)

        def table(shape, at):
            i = lax.broadcasted_iota(jnp.int32, shape, 0)
            j = lax.broadcasted_iota(jnp.int32, shape, 1)
            out = jnp.zeros(shape, F32)
            for k in range(shape[0] * shape[1]):
                out = jnp.where(i * shape[1] + j == k, pick(at + k), out)
            return out

        square = lax.broadcasted_iota(jnp.int32, (8, 8), 0) == lax.broadcasted_iota(
            jnp.int32, (8, 8), 1
        )
        steps = [
            jnp.sum(
                jnp.where(square, last[:, k : k + 1] + last[:, k + 2 : k + 3], 0.0),
                axis=0,
                keepdims=True,
            )
            for k in (0, 1)
        ]
        return (
            jnp.broadcast_to(inside[None], (8, *inside.shape)),
            scale * total[:, :128],
            scale * total[:, 256:384],
            scale * jnp.concatenate(steps, 0),
            table((2, 2), 8) * rates,
            table((2, 2), 12),
            table((1, 2), 16),
        )

    if PLAIN:
        inside, *rest = add(grads, decay_rate)
    else:

        def fn(ins, outs):
            for ref, value in zip(outs, add(ins[0][...], ins[1][...])):
                ref[...] = value

        shapes = [(8, 128), (8, 128), (2, 8), (2, 2), (2, 2), (1, 2)]
        outs = [((8, 8, 256), BF16)] + [(shape, F32) for shape in shapes]
        inside, *rest = call(fn, outs, (grads, decay_rate), 1_000_000)
    return wide.at[:, 64:].set(inside), *rest


def add_parts(parts, scale):
    def add(pieces):
        total = jnp.sum(pieces.astype(F32), axis=0)
        blocks = [total[8 * (k // 2) + 32 * (k % 2) :][:8] for k in range(8)]
        return jnp.concatenate(blocks, 0).astype(BF16), scale * (total[64:, :128] + total[64:, 128:])

    if PLAIN:
        return add(parts)

    def fn(ins, outs):
        outs[0][...], outs[1][...] = add(ins[0][...])

    n = parts.shape[2]
    return call(fn, [((64, n), BF16), ((8, 128), F32)], (parts,), 1_000_000)


def exchange(array, axis):
    return lax.all_to_all(array, axis, 0, 0, tiled=True)


def body(
    tokens, out_grad, in_weight, dt_weight, bc_weight, out_weight, decay_rate, dt_bias, skip_gain
):
    seq_count = lax.axis_size(SEQ)
    tok_rows = tokens.shape[0]
    scale = (tok_rows * seq_count) ** (-0.5)
    own, rows, params = pack(
        tokens.T,
        out_grad.T,
        in_weight,
        bc_weight,
        out_weight.T,
        dt_weight.T,
        decay_rate,
        dt_bias,
        skip_gain.reshape(1, -1),
    )
    other = lax.ppermute(own, "chan_1", SWAP)
    pair = jnp.concatenate([own, other], 0)
    parts = [pair] + [
        lax.ppermute(pair, "chan_0", [(k, (k + d) % 4) for k in range(4)])
        for d in (1, 2, 3)
    ]
    here = exchange(rows, ZY).reshape(-1, 512)
    there = lax.ppermute(here, CORE, SWAP)
    across, around = lax.axis_index("chan_0"), lax.axis_index("chan_1")
    order = jnp.stack(
        [(across - d) % 4 * 2 + (around ^ e) for d in range(4) for e in range(2)]
        + [lax.axis_index(CORE)]
    ).astype(jnp.int32)
    sums, pre, bc, cot, vec = project(order, parts, here, there, params)
    sums = exchange(sums.reshape(64, 8, 128), SEQ).reshape(512, 128)
    mixed, dgated, dbc, extra = within(pre, bc, cot, vec, params)
    back = exchange(carry(sums).reshape(64, 8, 128), SEQ).reshape(512, 128)
    give, *results = finish(
        order, parts, params, pre, bc, cot, vec, mixed, dgated, dbc, extra, back
    )
    got = lax.ppermute(give, CORE, SWAP)
    wide, keep = finish_own(order, parts, here, there, *results)
    grads = join(keep, got)
    grads = exchange(grads.reshape(32, 8, 512), ZY)
    wide, in_weight_grad, out_rows, dt_rows, rate_grad, bias_grad, skip_grad = add_rows(
        grads, wide, decay_rate, scale
    )
    tokens_grad, bc_weight_grad = add_parts(exchange(wide, CHAN), scale)
    tokens_grad = tokens_grad.T
    out_weight_grad = out_rows.T
    dt_weight_grad = dt_rows.T
    skip_grad = skip_grad.reshape(-1)
    return (
        tokens_grad,
        in_weight_grad,
        dt_weight_grad,
        bc_weight_grad,
        out_weight_grad,
        rate_grad,
        bias_grad,
        skip_grad,
    )


def solution(mesh):
    split = Mesh(
        mesh.devices.reshape(8, 4, 2, 4, 2), (*SEQ, *CHAN)
    )
    return jax.shard_map(
        body,
        mesh=split,
        in_specs=(
            P(SEQ, CHAN),
            P(SEQ, CHAN),
            P(SEQ, CHAN),
            P(SEQ, CHAN),
            P(SEQ, None),
            P(CHAN, SEQ),
            P(None, CHAN),
            P(None, CHAN),
            P(CHAN),
        ),
        out_specs=(
            P(SEQ, CHAN),
            P(SEQ, CHAN),
            P(SEQ, CHAN),
            P(SEQ, None),
            P(CHAN, SEQ),
            P(None, CHAN),
            P(None, CHAN),
            P(CHAN),
        ),
        check_vma=False,
    )
```

```python
import jax
import jax.numpy as jnp
from jax import lax
from jax.experimental import pallas as pl
from jax.experimental.pallas import tpu as pltpu
from jax.sharding import Mesh
from jax.sharding import PartitionSpec as P


STATE = 64
HEAD = 64
SEQ = ("seq_0", "seq_1", "seq_2")
ZY = ("seq_0", "seq_1")
CORE = "seq_2"
CHAN = ("chan_0", "chan_1")
NN = (((1,), (0,)), ((), ()))
NT = (((1,), (1,)), ((), ()))
TN = (((0,), (0,)), ((), ()))
F32 = jnp.float32
BF16 = jnp.bfloat16
INTERPRET = False


def low(x, y, dims):
    return lax.dot_general(x.astype(BF16), y.astype(BF16), dims, preferred_element_type=F32)


def halves(x):
    top = x.astype(BF16)
    return top, (x - top.astype(F32)).astype(BF16)


def mid(x, y, dims):
    xt, xl = halves(x)
    yt, yl = halves(y)
    return low(xt, yt, dims) + (low(xt, yl, dims) + low(xl, yt, dims))


def running(x):
    n = x.shape[1]
    top, rest = halves(x)
    low_ = (x - top.astype(F32) - rest.astype(F32)).astype(BF16)
    parts = jnp.concatenate([top.astype(F32), rest.astype(F32), low_.astype(F32)], 0)
    both = jnp.concatenate([before(n), before(n, True)], 1)
    sums = low(parts, both, NN)
    sums = sums[:8] + (sums[8:16] + sums[16:24])
    return sums[:, :n], sums[:, n:]


def before(n, flip=False):
    i = lax.broadcasted_iota(jnp.int32, (n, n), 0)
    j = lax.broadcasted_iota(jnp.int32, (n, n), 1)
    return (i >= j if flip else i <= j).astype(F32)


def by_head(x, r, width):
    n = x.shape[1]
    return jnp.concatenate(
        [
            jnp.broadcast_to(x[2 * r : 2 * r + 1], (width // 2, n)),
            jnp.broadcast_to(x[2 * r + 1 : 2 * r + 2], (width // 2, n)),
        ],
        0,
    )


def forward_rows(n):
    return lax.broadcasted_iota(jnp.int32, (8, n), 0) < 2


def sigmoid(x):
    return 1.0 / (1.0 + jnp.exp(-x))


def stage_project(u, q, weights, params):
    width = 128
    n = u.shape[1]
    pre = lax.dot_general(weights[:, :width], u, TN, preferred_element_type=F32)
    bc = lax.dot_general(weights[:, 128:256], u, TN, preferred_element_type=F32)
    cot = lax.dot_general(weights[:, 256:384], q, TN, preferred_element_type=F32)
    z = lax.dot_general(weights[:, 384:512], u, TN, preferred_element_type=F32)[:8]
    rate, bias = params[:, 0:1], params[:, 1:2]
    v = z + bias
    step = jnp.maximum(v, 0.0) + jnp.log1p(jnp.exp(-jnp.abs(v)))
    slope = sigmoid(v)
    decay = -rate * step
    from_start, from_end = running(decay)
    run = jnp.where(forward_rows(n), from_start, from_end)
    total = jnp.sum(decay, axis=1, keepdims=True)
    grown = jnp.exp(run)
    tail = jnp.exp(total - run)
    gated = pre * sigmoid(pre)
    b, c = bc[:STATE], bc[STATE:]
    push = step * tail
    pushed = jnp.concatenate([gated * by_head(push, r, width) for r in (0, 1)], 0)
    pulled = jnp.concatenate([cot * by_head(grown, r, width) for r in (0, 1)], 0)
    ps = mid(b, pushed, NT)
    pl_ = mid(c, pulled, NT)
    kept = jnp.broadcast_to(jnp.exp(total), (8, width))
    lane = lax.broadcasted_iota(jnp.int32, (1, width), 1)
    sends = [ps[:, :width], pl_[:, width:], pl_[:, :width], ps[:, width:]]
    tops = [part.astype(BF16).astype(F32) for part in sends]
    rests = [part - top for part, top in zip(sends, tops)]
    for k in range(4):
        top = kept[k : k + 1].astype(BF16).astype(F32)
        rests[3] = jnp.where(lane == 120 + 2 * k, top, rests[3])
        rests[3] = jnp.where(lane == 121 + 2 * k, kept[k : k + 1] - top, rests[3])
    sends = tops + rests
    vec = jnp.concatenate(
        [step, run, grown, tail, slope, jnp.broadcast_to(jnp.exp(total), (8, n))], 0
    )
    return sends, pre, bc, cot, vec


def stage_within(pre, bc, cot, vec, params):
    n = pre.shape[1]
    gated = pre * sigmoid(pre)
    b, c = bc[:STATE], bc[STATE:]
    step, run = vec[0:8], vec[8:16]
    columns = jnp.concatenate([run, jnp.zeros((120, n), F32)], 0).T
    t = lax.broadcasted_iota(jnp.int32, (n, n), 0)
    s = lax.broadcasted_iota(jnp.int32, (n, n), 1)
    later, same = t >= s, t == s
    earlier = t <= s
    scores = mid(c.T, b, NN)
    dscores = jnp.zeros((n, n), F32)
    mixed, dgated = ([], []), ([], [])
    lanes = lax.broadcasted_iota(jnp.int32, (n, 128), 1)
    rows = jnp.zeros((n, 128), F32)
    direct = [None] * 4
    for h in (0, 1):
        x = gated[HEAD * h : HEAD * (h + 1)]
        dy = cot[HEAD * h : HEAD * (h + 1)]
        step0, step1 = step[h : h + 1], step[2 + h : 3 + h]
        up = columns[:, h : h + 1] - run[h : h + 1]
        down = columns[:, 2 + h : 3 + h] - run[2 + h : 3 + h]
        fade = jnp.exp(jnp.where(later, up, down))
        pair = mid(dy.T, x, NN)
        faded = scores * fade
        moved = faded * pair
        scaled = fade * jnp.where(later, step0, step1) + jnp.where(same, step1, 0.0)
        dscores = dscores + scaled * pair
        for r, (mask, st) in enumerate(((later, step0), (earlier, step1))):
            part = jnp.where(mask, moved, 0.0)
            mix = jnp.where(mask, faded, 0.0) * st
            mixed[r].append(mid(x, mix, NT))
            dgated[r].append(mid(dy, mix, NN))
            direct[2 * r + h] = jnp.sum(part, axis=0, keepdims=True)
            rows = jnp.where(
                lanes == 2 * r + h, jnp.sum(part * st, axis=1, keepdims=True), rows
            )
    direct = jnp.concatenate(direct + [jnp.zeros((4, n), F32)], 0)
    drun = rows.T[:8] - step * direct
    gains = jnp.concatenate(
        [jnp.broadcast_to(params[h : h + 1, 2:3], (HEAD, n)) for h in (0, 1)], 0
    )
    mixed = jnp.concatenate([jnp.concatenate(m, 0) + gains * gated for m in mixed], 0)
    dgated = jnp.concatenate([jnp.concatenate(d, 0) + gains * cot for d in dgated], 0)
    both = gated * cot
    dskip = [
        2.0 * jnp.sum(both[HEAD * h : HEAD * (h + 1)], axis=0, keepdims=True) for h in (0, 1)
    ]
    dbc = jnp.concatenate([mid(c, dscores, NN), mid(b, dscores, NT)], 0)
    extra = jnp.concatenate([direct, drun] + dskip + [jnp.zeros((6, n), F32)], 0)
    return mixed, dgated, dbc, extra


def stage_finish(params, pre, bc, cot, vec, mixed, dgated, dbc, extra, carried):
    width = 128
    n = pre.shape[1]
    sig = sigmoid(pre)
    gated = pre * sig
    b, c = bc[:STATE], bc[STATE:]
    step, grown, tail, slope = vec[0:8], vec[16:24], vec[24:32], vec[32:40]
    kept = vec[40:48, 0:1]
    rate = params[:, 0:1]
    h0, g1, g0, h1 = carried
    start = jnp.concatenate([h0, h1], 1)
    end = jnp.concatenate([g0, g1], 1)
    reach = mid(start.T, c, NN)
    pull = mid(end.T, b, NN)
    gains, falls, pushed, pulled = [], [], [], []
    dpre, lower = [], []
    bend = sig * (1.0 + pre * (1.0 - sig))
    for r in (0, 1):
        grow, tails, steps = (by_head(v, r, width) for v in (grown, tail, step))
        here = slice(width * r, width * (r + 1))
        got = reach[here] * grow
        lower.append((mixed[here] + got).astype(BF16))
        back = pull[here] * tails
        dpre.append(((dgated[here] + steps * back) * bend).astype(BF16))
        gain, fall = cot * got, gated * back
        for h in (0, 1):
            gains.append(jnp.sum(gain[HEAD * h : HEAD * (h + 1)], axis=0, keepdims=True))
            falls.append(jnp.sum(fall[HEAD * h : HEAD * (h + 1)], axis=0, keepdims=True))
        pulled.append(cot * grow)
        pushed.append(gated * steps * tails)
    none = [jnp.zeros((4, n), F32)]
    gains = jnp.concatenate(gains + none, 0)
    falls = jnp.concatenate(falls + none, 0)
    pulled = jnp.concatenate(pulled, 0)
    pushed = jnp.concatenate(pushed, 0)
    dbc = dbc + jnp.concatenate([mid(end, pushed, NN), mid(start, pulled, NN)], 0)
    lost = step * falls
    drun = extra[8:16] + gains - lost
    overlap = jnp.sum(start * end, axis=0, keepdims=True)
    lane = lax.broadcasted_iota(jnp.int32, (1, 2 * width), 1)
    ends = [
        jnp.sum(jnp.where(lane // HEAD == k, overlap, 0.0), axis=1, keepdims=True)
        for k in range(4)
    ]
    ends = jnp.concatenate(ends + [jnp.zeros((4, 1), F32)], 0)
    ends = kept * ends + jnp.sum(lost, axis=1, keepdims=True)
    from_start, from_end = running(drun)
    ddecay = ends + jnp.where(forward_rows(n), from_end, from_start)
    dstep = extra[0:8] + falls - rate * ddecay
    valid = lax.broadcasted_iota(jnp.int32, (8, n), 0) < 4
    dz = jnp.where(valid, dstep * slope, 0.0)
    drate = -jnp.sum(ddecay * step, axis=1, keepdims=True)
    dbias = jnp.sum(dz, axis=1, keepdims=True)
    dskip = jnp.sum(extra[16:24], axis=1, keepdims=True)
    dzs = jnp.concatenate([dz, jnp.zeros((120, n), F32)], 0).astype(BF16)
    lane = lax.broadcasted_iota(jnp.int32, (1, width), 1)
    numbers = jnp.zeros((1, width), F32)
    for k in range(4):
        numbers = jnp.where(lane == 8 + k, drate[k : k + 1], numbers)
        numbers = jnp.where(lane == 12 + k, dbias[k : k + 1], numbers)
    for k in range(2):
        numbers = jnp.where(lane == 16 + k, dskip[k : k + 1], numbers)
    rough = numbers.astype(BF16).astype(F32)
    fine = rolled(jnp.broadcast_to(numbers - rough, (8, width)), 32)[:1]
    numbers = jnp.broadcast_to(rough + fine, (8, width))
    front = jnp.concatenate([*dpre, *halves(dbc), dzs], 0)
    return front, jnp.concatenate(lower, 0), numbers


def stage_outer(u, q, front, lower, numbers):
    width = 128
    dfront = low(u, front[: 2 * width], NT)
    dinside = low(u, front[2 * width : 4 * width], NT)
    dstep = low(u, front[4 * width :], NT)
    dout = low(q, lower, NT)
    return jnp.concatenate(
        [
            dfront[:, :width] + dfront[:, width:],
            dinside[:, :width] + dinside[:, width:],
            dout[:, :width] + dout[:, width:],
            dstep + jnp.broadcast_to(numbers[:1], (u.shape[0], width)),
        ],
        1,
    )


def stage_input(weights, front):
    outer, inside = weights[:, :128], weights[:, 128:256]
    return low(jnp.concatenate([outer, outer], 1), front[:256], NN) + low(
        jnp.concatenate([inside, inside, weights[:, 384:]], 1), front[256:], NN
    )


def rolled(x, by):
    return jnp.roll(x, by, 1) if PLAIN else pltpu.roll(x, by, 1)


PLAIN = False
SWAP = [(0, 1), (1, 0)]


def call(fn, outs, args, flops, scratch=(), scalars=0, grant=24 << 20):
    def kernel(*refs):
        k = len(args)
        fn(refs[:k], refs[k : k + len(outs)], *refs[k + len(outs) :])

    size = sum(a.size * a.dtype.itemsize for a in args)
    spaces = [pltpu.SMEM] * scalars + [pltpu.VMEM] * (len(args) - scalars)
    return pl.pallas_call(
        kernel,
        out_shape=[jax.ShapeDtypeStruct(s, d) for s, d in outs],
        in_specs=[pl.BlockSpec(memory_space=m) for m in spaces],
        scratch_shapes=list(scratch),
        cost_estimate=pl.CostEstimate(flops=flops, bytes_accessed=size, transcendentals=0),
        compiler_params=pltpu.CompilerParams(vmem_limit_bytes=grant),
        interpret=INTERPRET,
    )(*args)


def features(order, parts, partner):
    if PLAIN:
        n = parts[0].shape[1]
        blocks = jnp.concatenate(parts, 0).reshape(8, 2, 2, 32, n)
        side = 1 - order[8] if partner else order[8]
        return tuple(blocks[:, k, side].reshape(256, n) for k in (0, 1))
    at = (1 - order[8]) * 32 if partner else order[8] * 32
    up, down = [], []
    for k in range(8):
        part, base = parts[k // 2], 128 * (k % 2)
        up.append(part[pl.ds(pl.multiple_of(base + at, 32), 32), :])
        down.append(part[pl.ds(pl.multiple_of(base + 64 + at, 32), 32), :])
    return jnp.concatenate(up, 0), jnp.concatenate(down, 0)


def matching(order, weights):
    if PLAIN:
        return weights.reshape(8, 32, -1)[order[:8]].reshape(256, -1)
    rows = [weights[pl.ds(pl.multiple_of(order[k] * 32, 32), 32), :] for k in range(8)]
    return jnp.concatenate(rows, 0)


def gathered(order, parts, own, other):
    first, second = features(order, parts, False), features(order, parts, True)
    u, q = (jnp.concatenate(pair, 0) for pair in zip(first, second))
    return u, q, jnp.concatenate([matching(order, own), matching(order, other)], 0)


def project(order, parts, own, other, params):
    if PLAIN:
        sends, *rest = stage_project(*gathered(order, parts, own, other), params)
        return (jnp.stack(sends, 1).reshape(512, 128).astype(BF16), *rest)

    def fn(ins, outs, lines):
        sends, *rest = stage_project(*gathered(ins[0], ins[1:5], *ins[5:7]), ins[7][...])
        for j, part in enumerate(sends):
            lines[pl.ds(j, STATE, stride=8), :] = part
        outs[0][...] = lines[...].astype(BF16)
        for ref, value in zip(outs[1:], rest):
            ref[...] = value

    n = parts[0].shape[1]
    outs = [((512, 128), BF16), ((128, n), F32), ((128, n), F32), ((128, n), F32), ((48, n), F32)]
    lines = pltpu.VMEM((512, 128), F32)
    return call(fn, outs, (order, *parts, own, other, params), 300_000_000, (lines,), 1)


def within(pre, bc, cot, vec, params):
    if PLAIN:
        return stage_within(pre, bc, cot, vec, params)

    def fn(ins, outs):
        for ref, value in zip(outs, stage_within(*(r[...] for r in ins))):
            ref[...] = value

    n = pre.shape[1]
    outs = [((256, n), F32), ((256, n), F32), ((128, n), F32), ((24, n), F32)]
    return call(fn, outs, (pre, bc, cot, vec, params), 300_000_000)


def finish(order, parts, params, pre, bc, cot, vec, mixed, dgated, dbc, extra, back):
    more = (params, pre, bc, cot, vec, mixed, dgated, dbc, extra)
    n = pre.shape[1]
    if PLAIN:
        rows = back.astype(F32).reshape(64, 8, 128)
        carried = [rows[:, j] + rows[:, 4 + j] for j in range(4)]
        results = stage_finish(*more, carried)
        grads = stage_outer(*features(order, parts, True), *results).reshape(8, 32, 512)
        give = jnp.zeros((8, 32, 512), F32).at[order[:8]].set(grads).reshape(256, 512)
        return give.astype(BF16), *results

    def fn(ins, outs, lines):
        order = ins[0]
        lines[...] = ins[-1][...].astype(F32)
        carried = [
            lines[pl.ds(j, STATE, stride=8), :] + lines[pl.ds(4 + j, STATE, stride=8), :]
            for j in range(4)
        ]
        results = stage_finish(*(r[...] for r in ins[5:-1]), carried)
        grads = stage_outer(*features(order, ins[1:5], True), *results).astype(BF16)
        for k in range(8):
            rows = pl.ds(pl.multiple_of(order[k] * 32, 32), 32)
            outs[0][rows, :] = grads[32 * k : 32 * k + 32]
        for ref, value in zip(outs[1:], results):
            ref[...] = value

    outs = [((256, 512), BF16), ((640, n), BF16), ((256, n), BF16), ((8, 128), F32)]
    lines = pltpu.VMEM((512, 128), F32)
    return call(fn, outs, (order, *parts, *more, back), 400_000_000, (lines,), 1)


def finish_own(order, parts, own, other, front, lower, numbers):
    n = front.shape[1]
    if PLAIN:
        at, mine = order[:8], order[8]
        weights = jnp.concatenate([matching(order, own), matching(order, other)], 0)
        dinput = stage_input(weights, front).astype(BF16).reshape(2, 8, 32, n)
        dinput = jnp.where(mine == 0, dinput, dinput[::-1]).transpose(1, 0, 2, 3)
        wide = jnp.zeros((8, 72, n), BF16).at[at, :64].set(dinput.reshape(8, 64, n))
        grads = stage_outer(*features(order, parts, False), front, lower, numbers)
        keep = jnp.zeros((8, 32, 512), F32).at[at].set(grads.reshape(8, 32, 512))
        return wide, keep.reshape(256, 512)

    def fn(ins, outs):
        order = ins[0]
        front, lower, numbers = (r[...] for r in ins[7:])
        weights = jnp.concatenate([matching(order, ins[5]), matching(order, ins[6])], 0)
        dinput = stage_input(weights, front).astype(BF16)
        grads = stage_outer(*features(order, ins[1:5], False), front, lower, numbers)
        mine = order[8] * 32
        for k in range(8):
            at = order[k]
            block = slice(32 * k, 32 * k + 32)
            outs[0][at, pl.ds(pl.multiple_of(mine, 32), 32), :] = dinput[block]
            outs[0][at, pl.ds(pl.multiple_of(32 - mine, 32), 32), :] = dinput[256:][block]
            outs[0][at, 64:, :] = jnp.zeros((8, n), BF16)
            outs[1][pl.ds(pl.multiple_of(at * 32, 32), 32), :] = grads[block]

    outs = [((8, 72, n), BF16), ((256, 512), F32)]
    args = (order, *parts, own, other, front, lower, numbers)
    return call(fn, outs, args, 400_000_000, (), 1)


def join(keep, got):
    def add(mine, theirs):
        total = mine + theirs.astype(F32)
        last = total[:, 384:]
        lane = lax.broadcasted_iota(jnp.int32, last.shape, 1)
        numbers = last + rolled(last, 96)
        rough = numbers.astype(BF16).astype(F32)
        fine = rolled(numbers - rough, 32)
        last = jnp.where(lane < 8, last, jnp.where(lane < 32, rough, fine))
        return jnp.concatenate([total[:, :384], last], 1).astype(BF16)

    if PLAIN:
        return add(keep, got)

    def fn(ins, outs):
        outs[0][...] = add(ins[0][...], ins[1][...])

    return call(fn, [(keep.shape, BF16)], (keep, got), 1_000_000)[0]


def carry(blocks):
    count = blocks.shape[0] // 8

    def unpack(take):
        lane = lax.broadcasted_iota(jnp.int32, (1, 128), 1)
        last = take(7)
        rests = [take(4), take(5), take(6), jnp.where(lane < 120, last, 0.0)]
        sums = [take(j) + rests[j] for j in range(4)]
        kept = [last[:, k : k + 1] + last[:, k + 1 : k + 2] for k in range(120, 128, 2)]
        return sums, [jnp.where(lane < HEAD, kept[2 * r], kept[2 * r + 1]) for r in (0, 1)]

    def scan(added, kept, keep):
        up = jnp.zeros((2, 128), F32)
        down = jnp.zeros((2, 128), F32)
        for k in range(count):
            m = count - 1 - k
            keep(k, up, m, down)
            up = kept[2 * k : 2 * k + 2, :] * up + added[4 * k : 4 * k + 2, :]
            down = kept[2 * m : 2 * m + 2, :] * down + added[4 * m + 2 : 4 * m + 4, :]

    if PLAIN:
        lines = blocks.astype(F32).reshape(count, 8, 128)
        sums, kept = unpack(lambda j: lines[:, j])
        ups, downs = [None] * count, [None] * count

        def keep(k, up, m, down):
            ups[k], downs[m] = up, down

        scan(jnp.stack(sums, 1).reshape(-1, 128), jnp.stack(kept, 1).reshape(-1, 128), keep)
        full = jnp.concatenate([jnp.stack(ups), jnp.stack(downs)], 1)
        top = full.astype(BF16)
        rest = (full - top.astype(F32)).astype(BF16)
        return jnp.concatenate([top, rest], 1).reshape(-1, 128)

    def fn(ins, outs, lines, added, factors, done):
        lines[...] = ins[0][...].astype(F32)
        sums, kept = unpack(lambda j: lines[pl.ds(j, count, stride=8), :])
        for j in range(4):
            added[pl.ds(j, count, stride=4), :] = sums[j]
        for r in (0, 1):
            factors[pl.ds(r, count, stride=2), :] = kept[r]

        def keep(k, up, m, down):
            done[8 * k : 8 * k + 2, :] = up
            done[8 * m + 2 : 8 * m + 4, :] = down

        scan(added, factors, keep)
        full = done[...]
        top = full.astype(BF16).astype(F32)
        rest = pltpu.roll(full - top, 4, 0)
        line = lax.broadcasted_iota(jnp.int32, full.shape, 0)
        outs[0][...] = jnp.where(line % 8 < 4, top, rest).astype(BF16)

    scratch = [pltpu.VMEM((rows * count, 128), F32) for rows in (8, 4, 2, 8)]
    return call(fn, [((8 * count, 128), BF16)], (blocks,), 1_000_000, scratch)[0]


def pack(*args):
    def fill(tok, cot, inw, bcw, outw, dtw, rates, biases, gains):
        blocks = []
        for x in (tok.astype(F32), cot.astype(F32)):
            for odd in (0, 8):
                blocks += [x[k + odd : k + odd + 8] for k in range(0, 64, 16)]
        lane = lax.broadcasted_iota(jnp.int32, (8, 128), 1)
        square = lax.broadcasted_iota(jnp.int32, (8, 8), 0) == lax.broadcasted_iota(
            jnp.int32, (8, 8), 1
        )
        last = jnp.zeros((8, 128), F32)
        for k in range(4):
            row = jnp.broadcast_to(dtw[k % 2 : k % 2 + 1].astype(F32), (8, 8))
            column = jnp.sum(jnp.where(square, row, 0.0), axis=1, keepdims=True)
            last = jnp.where(lane == k, column, last)
        rows = jnp.concatenate([inw, bcw, outw, last.astype(BF16)], 1)
        sub = lax.broadcasted_iota(jnp.int32, (8, 128), 0)
        table = jnp.zeros((8, 128), F32)
        for k in range(4):
            r, h = k // 2, k % 2
            values = (rates[r : r + 1, h : h + 1], biases[r : r + 1, h : h + 1], gains[:, h : h + 1])
            for at, value in enumerate(values):
                table = jnp.where((sub == k) & (lane == at), value, table)
        return (
            jnp.concatenate(blocks, 0).astype(BF16),
            jnp.broadcast_to(rows[None], (32, 8, 512)),
            table,
        )

    if PLAIN:
        return fill(*args)

    def fn(ins, outs):
        for ref, value in zip(outs, fill(*(r[...] for r in ins))):
            ref[...] = value

    outs = [((128, args[0].shape[1]), BF16), ((32, 8, 512), BF16), ((8, 128), F32)]
    return call(fn, outs, args, 1_000_000, grant=None)


def add_rows(grads, wide, decay_rate, scale):
    def add(pieces, rates):
        total = jnp.sum(pieces.astype(F32), axis=0)
        inside = jnp.concatenate(halves(total[:, 128:256]), 1)
        last = total[:, 384:512]
        numbers = scale * (last + rolled(last, 96))[:1]
        lane = lax.broadcasted_iota(jnp.int32, (1, 128), 1)

        def pick(k):
            return jnp.sum(jnp.where(lane == k, numbers, 0.0), axis=1, keepdims=True)

        def table(shape, at):
            i = lax.broadcasted_iota(jnp.int32, shape, 0)
            j = lax.broadcasted_iota(jnp.int32, shape, 1)
            out = jnp.zeros(shape, F32)
            for k in range(shape[0] * shape[1]):
                out = jnp.where(i * shape[1] + j == k, pick(at + k), out)
            return out

        square = lax.broadcasted_iota(jnp.int32, (8, 8), 0) == lax.broadcasted_iota(
            jnp.int32, (8, 8), 1
        )
        steps = [
            jnp.sum(
                jnp.where(square, last[:, k : k + 1] + last[:, k + 2 : k + 3], 0.0),
                axis=0,
                keepdims=True,
            )
            for k in (0, 1)
        ]
        return (
            jnp.broadcast_to(inside[None], (8, *inside.shape)),
            scale * total[:, :128],
            scale * total[:, 256:384],
            scale * jnp.concatenate(steps, 0),
            table((2, 2), 8) * rates,
            table((2, 2), 12),
            table((1, 2), 16),
        )

    if PLAIN:
        inside, *rest = add(grads, decay_rate)
    else:

        def fn(ins, outs):
            for ref, value in zip(outs, add(ins[0][...], ins[1][...])):
                ref[...] = value

        shapes = [(8, 128), (8, 128), (2, 8), (2, 2), (2, 2), (1, 2)]
        outs = [((8, 8, 256), BF16)] + [(shape, F32) for shape in shapes]
        inside, *rest = call(fn, outs, (grads, decay_rate), 1_000_000)
    return wide.at[:, 64:].set(inside), *rest


def add_parts(parts, scale):
    def add(pieces):
        total = jnp.sum(pieces.astype(F32), axis=0)
        blocks = [total[8 * (k // 2) + 32 * (k % 2) :][:8] for k in range(8)]
        return jnp.concatenate(blocks, 0).astype(BF16), scale * (total[64:, :128] + total[64:, 128:])

    if PLAIN:
        return add(parts)

    def fn(ins, outs):
        outs[0][...], outs[1][...] = add(ins[0][...])

    n = parts.shape[2]
    return call(fn, [((64, n), BF16), ((8, 128), F32)], (parts,), 1_000_000)


def exchange(array, axis):
    return lax.all_to_all(array, axis, 0, 0, tiled=True)


def body(
    tokens, out_grad, in_weight, dt_weight, bc_weight, out_weight, decay_rate, dt_bias, skip_gain
):
    seq_count = lax.axis_size(SEQ)
    tok_rows = tokens.shape[0]
    scale = (tok_rows * seq_count) ** (-0.5)
    own, rows, params = pack(
        tokens.T,
        out_grad.T,
        in_weight,
        bc_weight,
        out_weight.T,
        dt_weight.T,
        decay_rate,
        dt_bias,
        skip_gain.reshape(1, -1),
    )
    other = lax.ppermute(own, "chan_1", SWAP)
    parts = [jnp.concatenate([own, other], 0)]
    for d in (1, 2, 3):
        ring = [(k, (k + d) % 4) for k in range(4)]
        parts.append(lax.ppermute(parts[0], "chan_0", ring))
    here = exchange(rows, ZY).reshape(-1, 512)
    there = lax.ppermute(here, CORE, SWAP)
    across, around = lax.axis_index("chan_0"), lax.axis_index("chan_1")
    order = jnp.stack(
        [(across - d) % 4 * 2 + (around ^ e) for d in range(4) for e in range(2)]
        + [lax.axis_index(CORE)]
    ).astype(jnp.int32)
    sums, pre, bc, cot, vec = project(order, parts, here, there, params)
    sums = exchange(sums.reshape(64, 8, 128), SEQ).reshape(512, 128)
    mixed, dgated, dbc, extra = within(pre, bc, cot, vec, params)
    back = exchange(carry(sums).reshape(64, 8, 128), SEQ).reshape(512, 128)
    give, *results = finish(
        order, parts, params, pre, bc, cot, vec, mixed, dgated, dbc, extra, back
    )
    got = lax.ppermute(give, CORE, SWAP)
    wide, keep = finish_own(order, parts, here, there, *results)
    grads = join(keep, got)
    grads = exchange(grads.reshape(32, 8, 512), ZY)
    wide, in_weight_grad, out_rows, dt_rows, rate_grad, bias_grad, skip_grad = add_rows(
        grads, wide, decay_rate, scale
    )
    tokens_grad, bc_weight_grad = add_parts(exchange(wide, CHAN), scale)
    tokens_grad = tokens_grad.T
    out_weight_grad = out_rows.T
    dt_weight_grad = dt_rows.T
    skip_grad = skip_grad.reshape(-1)
    return (
        tokens_grad,
        in_weight_grad,
        dt_weight_grad,
        bc_weight_grad,
        out_weight_grad,
        rate_grad,
        bias_grad,
        skip_grad,
    )


def solution(mesh):
    split = Mesh(
        mesh.devices.reshape(8, 4, 2, 4, 2), (*SEQ, *CHAN)
    )
    return jax.shard_map(
        body,
        mesh=split,
        in_specs=(
            P(SEQ, CHAN),
            P(SEQ, CHAN),
            P(SEQ, CHAN),
            P(SEQ, CHAN),
            P(SEQ, None),
            P(CHAN, SEQ),
            P(None, CHAN),
            P(None, CHAN),
            P(CHAN),
        ),
        out_specs=(
            P(SEQ, CHAN),
            P(SEQ, CHAN),
            P(SEQ, CHAN),
            P(SEQ, None),
            P(CHAN, SEQ),
            P(None, CHAN),
            P(None, CHAN),
            P(CHAN),
        ),
        check_vma=False,
    )
```

```python
import jax
import jax.numpy as jnp
from jax import lax
from jax.experimental import pallas as pl
from jax.experimental.pallas import tpu as pltpu
from jax.sharding import Mesh
from jax.sharding import PartitionSpec as P


STATE = 64
HEAD = 64
SEQ = ("seq_0", "seq_1", "seq_2")
ZY = ("seq_0", "seq_1")
CORE = "seq_2"
CHAN = ("chan_0", "chan_1")
NN = (((1,), (0,)), ((), ()))
NT = (((1,), (1,)), ((), ()))
TN = (((0,), (0,)), ((), ()))
F32 = jnp.float32
BF16 = jnp.bfloat16
INTERPRET = False


def low(x, y, dims):
    return lax.dot_general(x.astype(BF16), y.astype(BF16), dims, preferred_element_type=F32)


def halves(x):
    top = x.astype(BF16)
    return top, (x - top.astype(F32)).astype(BF16)


def mid(x, y, dims):
    xt, xl = halves(x)
    yt, yl = halves(y)
    return low(xt, yt, dims) + (low(xt, yl, dims) + low(xl, yt, dims))


def running(x):
    n = x.shape[1]
    top, rest = halves(x)
    low_ = (x - top.astype(F32) - rest.astype(F32)).astype(BF16)
    parts = jnp.concatenate([top.astype(F32), rest.astype(F32), low_.astype(F32)], 0)
    both = jnp.concatenate([before(n), before(n, True)], 1)
    sums = low(parts, both, NN)
    sums = sums[:8] + (sums[8:16] + sums[16:24])
    return sums[:, :n], sums[:, n:]


def before(n, flip=False):
    i = lax.broadcasted_iota(jnp.int32, (n, n), 0)
    j = lax.broadcasted_iota(jnp.int32, (n, n), 1)
    return (i >= j if flip else i <= j).astype(F32)


def by_head(x, r, width):
    n = x.shape[1]
    return jnp.concatenate(
        [
            jnp.broadcast_to(x[2 * r : 2 * r + 1], (width // 2, n)),
            jnp.broadcast_to(x[2 * r + 1 : 2 * r + 2], (width // 2, n)),
        ],
        0,
    )


def forward_rows(n):
    return lax.broadcasted_iota(jnp.int32, (8, n), 0) < 2


def sigmoid(x):
    return 1.0 / (1.0 + jnp.exp(-x))


def stage_project(u, q, weights, params):
    width = 128
    n = u.shape[1]
    pre = lax.dot_general(weights[:, :width], u, TN, preferred_element_type=F32)
    bc = lax.dot_general(weights[:, 128:256], u, TN, preferred_element_type=F32)
    cot = lax.dot_general(weights[:, 256:384], q, TN, preferred_element_type=F32)
    z = lax.dot_general(weights[:, 384:512], u, TN, preferred_element_type=F32)[:8]
    rate, bias = params[:, 0:1], params[:, 1:2]
    v = z + bias
    step = jnp.maximum(v, 0.0) + jnp.log1p(jnp.exp(-jnp.abs(v)))
    slope = sigmoid(v)
    decay = -rate * step
    from_start, from_end = running(decay)
    run = jnp.where(forward_rows(n), from_start, from_end)
    total = jnp.where(forward_rows(1), run[:, n - 1 : n], run[:, :1])
    grown = jnp.exp(run)
    tail = jnp.exp(total - run)
    gated = pre * sigmoid(pre)
    b, c = bc[:STATE], bc[STATE:]
    push = step * tail
    pushed = jnp.concatenate([gated * by_head(push, r, width) for r in (0, 1)], 0)
    pulled = jnp.concatenate([cot * by_head(grown, r, width) for r in (0, 1)], 0)
    ps = mid(b, pushed, NT)
    pl_ = mid(c, pulled, NT)
    kept = jnp.broadcast_to(jnp.exp(total), (8, width))
    lane = lax.broadcasted_iota(jnp.int32, (1, width), 1)
    sends = [ps[:, :width], pl_[:, width:], pl_[:, :width], ps[:, width:]]
    tops = [part.astype(BF16).astype(F32) for part in sends]
    rests = [part - top for part, top in zip(sends, tops)]
    for k in range(4):
        top = kept[k : k + 1].astype(BF16).astype(F32)
        rests[3] = jnp.where(lane == 120 + 2 * k, top, rests[3])
        rests[3] = jnp.where(lane == 121 + 2 * k, kept[k : k + 1] - top, rests[3])
    sends = tops + rests
    vec = jnp.concatenate(
        [step, run, grown, tail, slope, jnp.broadcast_to(jnp.exp(total), (8, n))], 0
    )
    return sends, pre, bc, cot, vec


def stage_within(pre, bc, cot, vec, params):
    n = pre.shape[1]
    gated = pre * sigmoid(pre)
    b, c = bc[:STATE], bc[STATE:]
    step, run = vec[0:8], vec[8:16]
    columns = jnp.concatenate([run, jnp.zeros((120, n), F32)], 0).T
    t = lax.broadcasted_iota(jnp.int32, (n, n), 0)
    s = lax.broadcasted_iota(jnp.int32, (n, n), 1)
    later, same = t >= s, t == s
    earlier = t <= s
    scores = mid(c.T, b, NN)
    dscores = jnp.zeros((n, n), F32)
    mixed, dgated = ([], []), ([], [])
    lanes = lax.broadcasted_iota(jnp.int32, (n, 128), 1)
    rows = jnp.zeros((n, 128), F32)
    direct = [None] * 4
    for h in (0, 1):
        x = gated[HEAD * h : HEAD * (h + 1)]
        dy = cot[HEAD * h : HEAD * (h + 1)]
        step0, step1 = step[h : h + 1], step[2 + h : 3 + h]
        up = columns[:, h : h + 1] - run[h : h + 1]
        down = columns[:, 2 + h : 3 + h] - run[2 + h : 3 + h]
        fade = jnp.exp(jnp.where(later, up, down))
        pair = mid(dy.T, x, NN)
        faded = scores * fade
        moved = faded * pair
        scaled = fade * jnp.where(later, step0, step1) + jnp.where(same, step1, 0.0)
        dscores = dscores + scaled * pair
        for r, (mask, st) in enumerate(((later, step0), (earlier, step1))):
            part = jnp.where(mask, moved, 0.0)
            mix = jnp.where(mask, faded, 0.0) * st
            mixed[r].append(mid(x, mix, NT))
            dgated[r].append(mid(dy, mix, NN))
            direct[2 * r + h] = jnp.sum(part, axis=0, keepdims=True)
            rows = jnp.where(
                lanes == 2 * r + h, jnp.sum(part * st, axis=1, keepdims=True), rows
            )
    direct = jnp.concatenate(direct + [jnp.zeros((4, n), F32)], 0)
    drun = rows.T[:8] - step * direct
    gains = jnp.concatenate(
        [jnp.broadcast_to(params[h : h + 1, 2:3], (HEAD, n)) for h in (0, 1)], 0
    )
    mixed = jnp.concatenate([jnp.concatenate(m, 0) + gains * gated for m in mixed], 0)
    dgated = jnp.concatenate([jnp.concatenate(d, 0) + gains * cot for d in dgated], 0)
    both = gated * cot
    dskip = [
        2.0 * jnp.sum(both[HEAD * h : HEAD * (h + 1)], axis=0, keepdims=True) for h in (0, 1)
    ]
    dbc = jnp.concatenate([mid(c, dscores, NN), mid(b, dscores, NT)], 0)
    extra = jnp.concatenate([direct, drun] + dskip + [jnp.zeros((6, n), F32)], 0)
    return mixed, dgated, dbc, extra


def stage_finish(params, pre, bc, cot, vec, mixed, dgated, dbc, extra, carried):
    width = 128
    n = pre.shape[1]
    sig = sigmoid(pre)
    gated = pre * sig
    b, c = bc[:STATE], bc[STATE:]
    step, grown, tail, slope = vec[0:8], vec[16:24], vec[24:32], vec[32:40]
    kept = vec[40:48, 0:1]
    rate = params[:, 0:1]
    h0, g1, g0, h1 = carried
    start = jnp.concatenate([h0, h1], 1)
    end = jnp.concatenate([g0, g1], 1)
    reach = mid(start.T, c, NN)
    pull = mid(end.T, b, NN)
    gains, falls, pushed, pulled = [], [], [], []
    dpre, lower = [], []
    bend = sig * (1.0 + pre * (1.0 - sig))
    for r in (0, 1):
        grow, tails, steps = (by_head(v, r, width) for v in (grown, tail, step))
        here = slice(width * r, width * (r + 1))
        got = reach[here] * grow
        lower.append((mixed[here] + got).astype(BF16))
        back = pull[here] * tails
        dpre.append(((dgated[here] + steps * back) * bend).astype(BF16))
        gain, fall = cot * got, gated * back
        for h in (0, 1):
            gains.append(jnp.sum(gain[HEAD * h : HEAD * (h + 1)], axis=0, keepdims=True))
            falls.append(jnp.sum(fall[HEAD * h : HEAD * (h + 1)], axis=0, keepdims=True))
        pulled.append(cot * grow)
        pushed.append(gated * steps * tails)
    none = [jnp.zeros((4, n), F32)]
    gains = jnp.concatenate(gains + none, 0)
    falls = jnp.concatenate(falls + none, 0)
    pulled = jnp.concatenate(pulled, 0)
    pushed = jnp.concatenate(pushed, 0)
    dbc = dbc + jnp.concatenate([mid(end, pushed, NN), mid(start, pulled, NN)], 0)
    lost = step * falls
    drun = extra[8:16] + gains - lost
    overlap = jnp.sum(start * end, axis=0, keepdims=True)
    lane = lax.broadcasted_iota(jnp.int32, (1, 2 * width), 1)
    ends = [
        jnp.sum(jnp.where(lane // HEAD == k, overlap, 0.0), axis=1, keepdims=True)
        for k in range(4)
    ]
    ends = jnp.concatenate(ends + [jnp.zeros((4, 1), F32)], 0)
    ends = kept * ends + jnp.sum(lost, axis=1, keepdims=True)
    from_start, from_end = running(drun)
    ddecay = ends + jnp.where(forward_rows(n), from_end, from_start)
    dstep = extra[0:8] + falls - rate * ddecay
    valid = lax.broadcasted_iota(jnp.int32, (8, n), 0) < 4
    dz = jnp.where(valid, dstep * slope, 0.0)
    drate = -jnp.sum(ddecay * step, axis=1, keepdims=True)
    dbias = jnp.sum(dz, axis=1, keepdims=True)
    dskip = jnp.sum(extra[16:24], axis=1, keepdims=True)
    dzs = jnp.concatenate([dz, jnp.zeros((120, n), F32)], 0).astype(BF16)
    lane = lax.broadcasted_iota(jnp.int32, (1, width), 1)
    numbers = jnp.zeros((1, width), F32)
    for k in range(4):
        numbers = jnp.where(lane == 8 + k, drate[k : k + 1], numbers)
        numbers = jnp.where(lane == 12 + k, dbias[k : k + 1], numbers)
    for k in range(2):
        numbers = jnp.where(lane == 16 + k, dskip[k : k + 1], numbers)
    rough = numbers.astype(BF16).astype(F32)
    fine = rolled(jnp.broadcast_to(numbers - rough, (8, width)), 32)[:1]
    numbers = jnp.broadcast_to(rough + fine, (8, width))
    front = jnp.concatenate([*dpre, *halves(dbc), dzs], 0)
    return front, jnp.concatenate(lower, 0), numbers


def stage_outer(u, q, front, lower, numbers):
    width = 128
    dfront = low(u, front[: 2 * width], NT)
    dinside = low(u, front[2 * width : 4 * width], NT)
    dstep = low(u, front[4 * width :], NT)
    dout = low(q, lower, NT)
    return jnp.concatenate(
        [
            dfront[:, :width] + dfront[:, width:],
            dinside[:, :width] + dinside[:, width:],
            dout[:, :width] + dout[:, width:],
            dstep + jnp.broadcast_to(numbers[:1], (u.shape[0], width)),
        ],
        1,
    )


def stage_input(weights, front):
    outer, inside = weights[:, :128], weights[:, 128:256]
    return low(jnp.concatenate([outer, outer], 1), front[:256], NN) + low(
        jnp.concatenate([inside, inside, weights[:, 384:]], 1), front[256:], NN
    )


def rolled(x, by):
    return jnp.roll(x, by, 1) if PLAIN else pltpu.roll(x, by, 1)


PLAIN = False
SWAP = [(0, 1), (1, 0)]


def call(fn, outs, args, flops, scratch=(), scalars=0, grant=24 << 20):
    def kernel(*refs):
        k = len(args)
        fn(refs[:k], refs[k : k + len(outs)], *refs[k + len(outs) :])

    size = sum(a.size * a.dtype.itemsize for a in args)
    spaces = [pltpu.SMEM] * scalars + [pltpu.VMEM] * (len(args) - scalars)
    return pl.pallas_call(
        kernel,
        out_shape=[jax.ShapeDtypeStruct(s, d) for s, d in outs],
        in_specs=[pl.BlockSpec(memory_space=m) for m in spaces],
        scratch_shapes=list(scratch),
        cost_estimate=pl.CostEstimate(flops=flops, bytes_accessed=size, transcendentals=0),
        compiler_params=pltpu.CompilerParams(vmem_limit_bytes=grant),
        interpret=INTERPRET,
    )(*args)


def features(order, parts, partner):
    if PLAIN:
        n = parts[0].shape[1]
        blocks = jnp.concatenate(parts, 0).reshape(8, 2, 2, 32, n)
        side = 1 - order[8] if partner else order[8]
        return tuple(blocks[:, k, side].reshape(256, n) for k in (0, 1))
    at = (1 - order[8]) * 32 if partner else order[8] * 32
    up, down = [], []
    for k in range(8):
        part, base = parts[k // 2], 128 * (k % 2)
        up.append(part[pl.ds(pl.multiple_of(base + at, 32), 32), :])
        down.append(part[pl.ds(pl.multiple_of(base + 64 + at, 32), 32), :])
    return jnp.concatenate(up, 0), jnp.concatenate(down, 0)


def matching(order, weights):
    if PLAIN:
        return weights.reshape(8, 32, -1)[order[:8]].reshape(256, -1)
    rows = [weights[pl.ds(pl.multiple_of(order[k] * 32, 32), 32), :] for k in range(8)]
    return jnp.concatenate(rows, 0)


def gathered(order, parts, own, other):
    first, second = features(order, parts, False), features(order, parts, True)
    u, q = (jnp.concatenate(pair, 0) for pair in zip(first, second))
    return u, q, jnp.concatenate([matching(order, own), matching(order, other)], 0)


def project(order, parts, own, other, params):
    if PLAIN:
        sends, *rest = stage_project(*gathered(order, parts, own, other), params)
        return (jnp.stack(sends, 1).reshape(512, 128).astype(BF16), *rest)

    def fn(ins, outs, lines):
        sends, *rest = stage_project(*gathered(ins[0], ins[1:5], *ins[5:7]), ins[7][...])
        for j, part in enumerate(sends):
            lines[pl.ds(j, STATE, stride=8), :] = part
        outs[0][...] = lines[...].astype(BF16)
        for ref, value in zip(outs[1:], rest):
            ref[...] = value

    n = parts[0].shape[1]
    outs = [((512, 128), BF16), ((128, n), F32), ((128, n), F32), ((128, n), F32), ((48, n), F32)]
    lines = pltpu.VMEM((512, 128), F32)
    return call(fn, outs, (order, *parts, own, other, params), 300_000_000, (lines,), 1)


def within(pre, bc, cot, vec, params):
    if PLAIN:
        return stage_within(pre, bc, cot, vec, params)

    def fn(ins, outs):
        for ref, value in zip(outs, stage_within(*(r[...] for r in ins))):
            ref[...] = value

    n = pre.shape[1]
    outs = [((256, n), F32), ((256, n), F32), ((128, n), F32), ((24, n), F32)]
    return call(fn, outs, (pre, bc, cot, vec, params), 300_000_000)


def finish(order, parts, params, pre, bc, cot, vec, mixed, dgated, dbc, extra, back):
    more = (params, pre, bc, cot, vec, mixed, dgated, dbc, extra)
    n = pre.shape[1]
    if PLAIN:
        rows = back.astype(F32).reshape(64, 8, 128)
        carried = [rows[:, j] + rows[:, 4 + j] for j in range(4)]
        results = stage_finish(*more, carried)
        grads = stage_outer(*features(order, parts, True), *results).reshape(8, 32, 512)
        give = jnp.zeros((8, 32, 512), F32).at[order[:8]].set(grads).reshape(256, 512)
        return give.astype(BF16), *results

    def fn(ins, outs, lines):
        order = ins[0]
        lines[...] = ins[-1][...].astype(F32)
        carried = [
            lines[pl.ds(j, STATE, stride=8), :] + lines[pl.ds(4 + j, STATE, stride=8), :]
            for j in range(4)
        ]
        results = stage_finish(*(r[...] for r in ins[5:-1]), carried)
        grads = stage_outer(*features(order, ins[1:5], True), *results).astype(BF16)
        for k in range(8):
            rows = pl.ds(pl.multiple_of(order[k] * 32, 32), 32)
            outs[0][rows, :] = grads[32 * k : 32 * k + 32]
        for ref, value in zip(outs[1:], results):
            ref[...] = value

    outs = [((256, 512), BF16), ((640, n), BF16), ((256, n), BF16), ((8, 128), F32)]
    lines = pltpu.VMEM((512, 128), F32)
    return call(fn, outs, (order, *parts, *more, back), 400_000_000, (lines,), 1)


def finish_own(order, parts, own, other, front, lower, numbers):
    n = front.shape[1]
    if PLAIN:
        at, mine = order[:8], order[8]
        weights = jnp.concatenate([matching(order, own), matching(order, other)], 0)
        dinput = stage_input(weights, front).astype(BF16).reshape(2, 8, 32, n)
        dinput = jnp.where(mine == 0, dinput, dinput[::-1]).transpose(1, 0, 2, 3)
        wide = jnp.zeros((8, 72, n), BF16).at[at, :64].set(dinput.reshape(8, 64, n))
        grads = stage_outer(*features(order, parts, False), front, lower, numbers)
        keep = jnp.zeros((8, 32, 512), F32).at[at].set(grads.reshape(8, 32, 512))
        return wide, keep.reshape(256, 512)

    def fn(ins, outs):
        order = ins[0]
        front, lower, numbers = (r[...] for r in ins[7:])
        weights = jnp.concatenate([matching(order, ins[5]), matching(order, ins[6])], 0)
        dinput = stage_input(weights, front).astype(BF16)
        grads = stage_outer(*features(order, ins[1:5], False), front, lower, numbers)
        mine = order[8] * 32
        for k in range(8):
            at = order[k]
            block = slice(32 * k, 32 * k + 32)
            outs[0][at, pl.ds(pl.multiple_of(mine, 32), 32), :] = dinput[block]
            outs[0][at, pl.ds(pl.multiple_of(32 - mine, 32), 32), :] = dinput[256:][block]
            outs[1][pl.ds(pl.multiple_of(at * 32, 32), 32), :] = grads[block]

    outs = [((8, 72, n), BF16), ((256, 512), F32)]
    args = (order, *parts, own, other, front, lower, numbers)
    return call(fn, outs, args, 400_000_000, (), 1)


def join(keep, got):
    def add(mine, theirs):
        total = mine + theirs.astype(F32)
        last = total[:, 384:]
        lane = lax.broadcasted_iota(jnp.int32, last.shape, 1)
        numbers = last + rolled(last, 96)
        rough = numbers.astype(BF16).astype(F32)
        fine = rolled(numbers - rough, 32)
        last = jnp.where(lane < 8, last, jnp.where(lane < 32, rough, fine))
        return jnp.concatenate([total[:, :384], last], 1).astype(BF16)

    if PLAIN:
        return add(keep, got)

    def fn(ins, outs):
        outs[0][...] = add(ins[0][...], ins[1][...])

    return call(fn, [(keep.shape, BF16)], (keep, got), 1_000_000)[0]


def carry(blocks):
    count = blocks.shape[0] // 8

    def unpack(take):
        lane = lax.broadcasted_iota(jnp.int32, (1, 128), 1)
        last = take(7)
        rests = [take(4), take(5), take(6), jnp.where(lane < 120, last, 0.0)]
        sums = [take(j) + rests[j] for j in range(4)]
        kept = [last[:, k : k + 1] + last[:, k + 1 : k + 2] for k in range(120, 128, 2)]
        return sums, [jnp.where(lane < HEAD, kept[2 * r], kept[2 * r + 1]) for r in (0, 1)]

    def scan(added, kept, keep):
        up = jnp.zeros((2, 128), F32)
        down = jnp.zeros((2, 128), F32)
        for k in range(count):
            m = count - 1 - k
            keep(k, up, m, down)
            up = kept[2 * k : 2 * k + 2, :] * up + added[4 * k : 4 * k + 2, :]
            down = kept[2 * m : 2 * m + 2, :] * down + added[4 * m + 2 : 4 * m + 4, :]

    if PLAIN:
        lines = blocks.astype(F32).reshape(count, 8, 128)
        sums, kept = unpack(lambda j: lines[:, j])
        ups, downs = [None] * count, [None] * count

        def keep(k, up, m, down):
            ups[k], downs[m] = up, down

        scan(jnp.stack(sums, 1).reshape(-1, 128), jnp.stack(kept, 1).reshape(-1, 128), keep)
        full = jnp.concatenate([jnp.stack(ups), jnp.stack(downs)], 1)
        top = full.astype(BF16)
        rest = (full - top.astype(F32)).astype(BF16)
        return jnp.concatenate([top, rest], 1).reshape(-1, 128)

    def fn(ins, outs, lines, added, factors, done):
        lines[...] = ins[0][...].astype(F32)
        sums, kept = unpack(lambda j: lines[pl.ds(j, count, stride=8), :])
        for j in range(4):
            added[pl.ds(j, count, stride=4), :] = sums[j]
        for r in (0, 1):
            factors[pl.ds(r, count, stride=2), :] = kept[r]

        def keep(k, up, m, down):
            done[8 * k : 8 * k + 2, :] = up
            done[8 * m + 2 : 8 * m + 4, :] = down

        scan(added, factors, keep)
        full = done[...]
        top = full.astype(BF16).astype(F32)
        rest = pltpu.roll(full - top, 4, 0)
        line = lax.broadcasted_iota(jnp.int32, full.shape, 0)
        outs[0][...] = jnp.where(line % 8 < 4, top, rest).astype(BF16)

    scratch = [pltpu.VMEM((rows * count, 128), F32) for rows in (8, 4, 2, 8)]
    return call(fn, [((8 * count, 128), BF16)], (blocks,), 1_000_000, scratch)[0]


def pack(*args):
    def fill(tok, cot, inw, bcw, outw, dtw, rates, biases, gains):
        blocks = []
        for x in (tok.astype(F32), cot.astype(F32)):
            for odd in (0, 8):
                blocks += [x[k + odd : k + odd + 8] for k in range(0, 64, 16)]
        lane = lax.broadcasted_iota(jnp.int32, (8, 128), 1)
        square = lax.broadcasted_iota(jnp.int32, (8, 8), 0) == lax.broadcasted_iota(
            jnp.int32, (8, 8), 1
        )
        last = jnp.zeros((8, 128), F32)
        for k in range(4):
            row = jnp.broadcast_to(dtw[k % 2 : k % 2 + 1].astype(F32), (8, 8))
            column = jnp.sum(jnp.where(square, row, 0.0), axis=1, keepdims=True)
            last = jnp.where(lane == k, column, last)
        rows = jnp.concatenate([inw, bcw, outw, last.astype(BF16)], 1)
        sub = lax.broadcasted_iota(jnp.int32, (8, 128), 0)
        table = jnp.zeros((8, 128), F32)
        for k in range(4):
            r, h = k // 2, k % 2
            values = (rates[r : r + 1, h : h + 1], biases[r : r + 1, h : h + 1], gains[:, h : h + 1])
            for at, value in enumerate(values):
                table = jnp.where((sub == k) & (lane == at), value, table)
        return (
            jnp.concatenate(blocks, 0).astype(BF16),
            jnp.broadcast_to(rows[None], (32, 8, 512)),
            table,
        )

    if PLAIN:
        return fill(*args)

    def fn(ins, outs):
        for ref, value in zip(outs, fill(*(r[...] for r in ins))):
            ref[...] = value

    outs = [((128, args[0].shape[1]), BF16), ((32, 8, 512), BF16), ((8, 128), F32)]
    return call(fn, outs, args, 1_000_000, grant=None)


def add_rows(grads, wide, decay_rate, scale):
    def add(pieces, rates):
        total = jnp.sum(pieces.astype(F32), axis=0)
        inside = jnp.concatenate(halves(total[:, 128:256]), 1)
        last = total[:, 384:512]
        numbers = scale * (last + rolled(last, 96))[:1]
        lane = lax.broadcasted_iota(jnp.int32, (1, 128), 1)

        def pick(k):
            return jnp.sum(jnp.where(lane == k, numbers, 0.0), axis=1, keepdims=True)

        def table(shape, at):
            i = lax.broadcasted_iota(jnp.int32, shape, 0)
            j = lax.broadcasted_iota(jnp.int32, shape, 1)
            out = jnp.zeros(shape, F32)
            for k in range(shape[0] * shape[1]):
                out = jnp.where(i * shape[1] + j == k, pick(at + k), out)
            return out

        square = lax.broadcasted_iota(jnp.int32, (8, 8), 0) == lax.broadcasted_iota(
            jnp.int32, (8, 8), 1
        )
        steps = [
            jnp.sum(
                jnp.where(square, last[:, k : k + 1] + last[:, k + 2 : k + 3], 0.0),
                axis=0,
                keepdims=True,
            )
            for k in (0, 1)
        ]
        return (
            jnp.broadcast_to(inside[None], (8, *inside.shape)),
            scale * total[:, :128],
            scale * total[:, 256:384],
            scale * jnp.concatenate(steps, 0),
            table((2, 2), 8) * rates,
            table((2, 2), 12),
            table((1, 2), 16),
        )

    if PLAIN:
        inside, *rest = add(grads, decay_rate)
        return wide.at[:, 64:].set(inside), *rest

    def fn(ins, outs):
        inside, *rest = add(ins[0][...], ins[1][...])
        outs[0][:, :64, :] = ins[2][:, :64, :]
        outs[0][:, 64:, :] = inside
        for ref, value in zip(outs[1:], rest):
            ref[...] = value

    shapes = [(8, 128), (8, 128), (2, 8), (2, 2), (2, 2), (1, 2)]
    outs = [(wide.shape, BF16)] + [(shape, F32) for shape in shapes]
    return call(fn, outs, (grads, decay_rate, wide), 1_000_000)


def add_parts(parts, scale):
    def add(pieces):
        total = jnp.sum(pieces.astype(F32), axis=0)
        blocks = [total[8 * (k // 2) + 32 * (k % 2) :][:8] for k in range(8)]
        return jnp.concatenate(blocks, 0).astype(BF16), scale * (total[64:, :128] + total[64:, 128:])

    if PLAIN:
        return add(parts)

    def fn(ins, outs):
        outs[0][...], outs[1][...] = add(ins[0][...])

    n = parts.shape[2]
    return call(fn, [((64, n), BF16), ((8, 128), F32)], (parts,), 1_000_000)


def exchange(array, axis):
    return lax.all_to_all(array, axis, 0, 0, tiled=True)


def body(
    tokens, out_grad, in_weight, dt_weight, bc_weight, out_weight, decay_rate, dt_bias, skip_gain
):
    seq_count = lax.axis_size(SEQ)
    tok_rows = tokens.shape[0]
    scale = (tok_rows * seq_count) ** (-0.5)
    own, rows, params = pack(
        tokens.T,
        out_grad.T,
        in_weight,
        bc_weight,
        out_weight.T,
        dt_weight.T,
        decay_rate,
        dt_bias,
        skip_gain.reshape(1, -1),
    )
    other = lax.ppermute(own, "chan_1", SWAP)
    parts = [jnp.concatenate([own, other], 0)]
    for d in (1, 2, 3):
        ring = [(k, (k + d) % 4) for k in range(4)]
        parts.append(lax.ppermute(parts[0], "chan_0", ring))
    here = exchange(rows, ZY).reshape(-1, 512)
    there = lax.ppermute(here, CORE, SWAP)
    across, around = lax.axis_index("chan_0"), lax.axis_index("chan_1")
    order = jnp.stack(
        [(across - d) % 4 * 2 + (around ^ e) for d in range(4) for e in range(2)]
        + [lax.axis_index(CORE)]
    ).astype(jnp.int32)
    sums, pre, bc, cot, vec = project(order, parts, here, there, params)
    sums = exchange(sums.reshape(64, 8, 128), SEQ).reshape(512, 128)
    mixed, dgated, dbc, extra = within(pre, bc, cot, vec, params)
    back = exchange(carry(sums).reshape(64, 8, 128), SEQ).reshape(512, 128)
    give, *results = finish(
        order, parts, params, pre, bc, cot, vec, mixed, dgated, dbc, extra, back
    )
    got = lax.ppermute(give, CORE, SWAP)
    wide, keep = finish_own(order, parts, here, there, *results)
    grads = join(keep, got)
    grads = exchange(grads.reshape(32, 8, 512), ZY)
    wide, in_weight_grad, out_rows, dt_rows, rate_grad, bias_grad, skip_grad = add_rows(
        grads, wide, decay_rate, scale
    )
    tokens_grad, bc_weight_grad = add_parts(exchange(wide, CHAN), scale)
    tokens_grad = tokens_grad.T
    out_weight_grad = out_rows.T
    dt_weight_grad = dt_rows.T
    skip_grad = skip_grad.reshape(-1)
    return (
        tokens_grad,
        in_weight_grad,
        dt_weight_grad,
        bc_weight_grad,
        out_weight_grad,
        rate_grad,
        bias_grad,
        skip_grad,
    )


def solution(mesh):
    split = Mesh(
        mesh.devices.reshape(8, 4, 2, 4, 2), (*SEQ, *CHAN)
    )
    return jax.shard_map(
        body,
        mesh=split,
        in_specs=(
            P(SEQ, CHAN),
            P(SEQ, CHAN),
            P(SEQ, CHAN),
            P(SEQ, CHAN),
            P(SEQ, None),
            P(CHAN, SEQ),
            P(None, CHAN),
            P(None, CHAN),
            P(CHAN),
        ),
        out_specs=(
            P(SEQ, CHAN),
            P(SEQ, CHAN),
            P(SEQ, CHAN),
            P(SEQ, None),
            P(CHAN, SEQ),
            P(None, CHAN),
            P(None, CHAN),
            P(CHAN),
        ),
        check_vma=False,
    )
```
